32 devices in a mesh: dp: 8 (over y, x, core), tensor: 4 (over z).
Axes of the slice: x: 2, y: 2, z: 4, core: 2. Of those that a mesh axis runs over, the one named last changes fastest.
Arguments:
- tokens: bfloat16 [4096, 768], P('dp'), may hold values from -6 to 6
- lengths: int32 [8, 16], P('dp'), may hold values from 0 to 512, as said below
- w_query: bfloat16 [768, 768], P(None, 'tensor'), may hold values from -0.21875 to 0.21875
- w_key: bfloat16 [768, 768], P(None, 'tensor'), may hold values from -0.21875 to 0.21875
- w_value: bfloat16 [768, 768], P(None, 'tensor'), may hold values from -0.21875 to 0.21875
- b_query: float32 [768], P('tensor'), may hold values from -3 to 3
- b_value: float32 [768], P('tensor'), may hold values from -3 to 3
- w_out: bfloat16 [768, 768], P('tensor'), may hold values from -0.625 to 0.625
- b_out: float32 [768], replicated, may hold values from -3 to 3
- g_attn: float32 [768], replicated, may hold values from 0.5 to 1.5
- b_attn: float32 [768], replicated, may hold values from -3 to 3
- w_up: bfloat16 [768, 3072], P(None, 'tensor'), may hold values from -0.21875 to 0.21875
- b_up: float32 [3072], P('tensor'), may hold values from -3 to 3
- w_down: bfloat16 [3072, 768], P('tensor'), may hold values from -0.109375 to 0.109375
- b_down: float32 [768], replicated, may hold values from -3 to 3
- g_ffn: float32 [768], replicated, may hold values from 0.5 to 1.5
- b_ffn: float32 [768], replicated, may hold values from -3 to 3
- out_grad: bfloat16 [4096, 768], P('dp'), may hold values from -6 to 6
- pool_grad: float32 [128, 1728], P('dp'), may hold values from -6 to 6
Outputs:
- layer_out: bfloat16 [4096, 768], P('dp')
- pools: float32 [128, 1728], replicated
- d_tokens: float32 [4096, 768], P('dp')
- d_w_query: float32 [768, 768], P(None, 'tensor')
- d_w_key: float32 [768, 768], P(None, 'tensor')
- d_w_value: float32 [768, 768], P(None, 'tensor')
- d_b_query: float32 [768], P('tensor')
- d_b_value: float32 [768], P('tensor')
- d_w_out: float32 [768, 768], P('tensor')
- d_b_out: float32 [768], replicated
- d_g_attn: float32 [768], replicated
- d_b_attn: float32 [768], replicated
- d_w_up: float32 [768, 3072], P(None, 'tensor')
- d_b_up: float32 [3072], P('tensor')
- d_w_down: float32 [3072, 768], P('tensor')
- d_b_down: float32 [768], replicated
- d_g_ffn: float32 [768], replicated
- d_b_ffn: float32 [768], replicated
The draws below stay inside these ranges and needn't reach their ends.
Inputs may be any that keep to these rules, and one draw needn't show every extreme that they name: In each bucket the nonzero lengths come first and add up to at most 512; the first is nonzero; in every draw some bucket holds one sentence of exactly 512 tokens.
All inputs are finite; a program needn't handle non-finite values.
Results may differ from the reference program's by a relative error of at most 0.013.
Values sent between devices are 32-bit elements; how exact they have to be, the bound alone decides.
No kernel may reach another device: no remote copies, remote signals or barrier semaphores. Data moves between devices by JAX's collectives and lax.ppermute only.
A program may use at most 128 MiB of HBM per device.

```python
import jax
import jax.numpy as jnp
from jax import lax

D = 768
HEADS = 12
HDIM = 64
FF = 3072
BUCKET = 512
SENTS = 16
TOKENS = 4096
SLOTS = 128
PW = 1728
N_DP = 8


def draw_lengths(key, part):
    first_key, second_key, third_key, fourth_key = jax.random.split(key, 4)
    level = jnp.minimum(jax.random.randint(first_key, (N_DP, SENTS), 0, 7), jax.random.randint(second_key, (N_DP, SENTS), 0, 7))
    span = jnp.maximum(jnp.right_shift(jnp.full((N_DP, SENTS), BUCKET, jnp.int32), 6 - level), 1)
    extra = jax.random.randint(third_key, (N_DP, SENTS), 0, 1 << 20) % span
    sizes = jnp.minimum(span + extra, BUCKET)
    chosen = jax.random.randint(fourth_key, (), 0, N_DP)
    target = (jnp.arange(N_DP)[:, None] == chosen) & (jnp.arange(SENTS)[None, :] == 0)
    sizes = jnp.where(target, BUCKET, sizes)
    running = jnp.cumsum(sizes, axis=1)
    return jnp.where(running <= BUCKET, sizes, 0).astype(jnp.int32)


def block_scale(key, shape, cuts, smallest, top_value):
    factor_of = 1.0
    for axis_at, blocks in cuts:
        steps = jax.random.uniform(jax.random.fold_in(jax.random.fold_in(key, 6), axis_at), (blocks,), jnp.float32, smallest / len(cuts), top_value / len(cuts))
        factor_of = factor_of * jnp.repeat(jnp.exp(steps), shape[axis_at] // blocks).reshape((-1,) + (1,) * (len(shape) - 1 - axis_at))
    return factor_of


def gaussian(own_key, extent, spread, limit, cuts=(), kind=jnp.bfloat16):
    loudness = block_scale(own_key, extent, cuts, -0.22, 0.18) if cuts else 1.0
    result = jax.random.normal(own_key, extent, jnp.float32) * spread * loudness
    return jnp.minimum(jnp.maximum(result, -limit), limit).astype(kind)


def setup_inputs(seed: int = 0) -> dict:
    splits = jax.random.split(jax.random.key(seed), 20)
    tokens = gaussian(splits[0], (TOKENS, D), 1.0, 6.0, ((0, 8),))
    lengths = draw_lengths(jax.random.fold_in(splits[19], 71), 0)
    w_query = gaussian(splits[2], (D, D), D ** -0.5, 0.21875, ((1, 4),))
    w_key = gaussian(splits[3], (D, D), D ** -0.5, 0.21875, ((1, 4),))
    w_value = gaussian(splits[4], (D, D), D ** -0.5, 0.21875, ((1, 4),))
    b_query = gaussian(splits[5], (D,), 0.5, 3.0, ((0, 4),), jnp.float32)
    b_value = gaussian(splits[6], (D,), 0.5, 3.0, ((0, 4),), jnp.float32)
    w_out = gaussian(splits[7], (D, D), (D // 8) ** -0.5, 0.625, ((0, 4),))
    b_out = gaussian(splits[8], (D,), 0.5, 3.0, (), jnp.float32)
    g_attn = jnp.clip(1.0 + 0.1 * jax.random.normal(splits[9], (D,), jnp.float32), 0.5, 1.5)
    b_attn = gaussian(splits[10], (D,), 0.5, 3.0, (), jnp.float32)
    w_up = gaussian(splits[11], (D, FF), D ** -0.5, 0.21875, ((1, 4),))
    b_up = gaussian(splits[12], (FF,), 0.5, 3.0, ((0, 4),), jnp.float32)
    w_down = gaussian(splits[13], (FF, D), FF ** -0.5, 0.109375, ((0, 4),))
    b_down = gaussian(splits[14], (D,), 0.5, 3.0, (), jnp.float32)
    g_ffn = jnp.clip(1.0 + 0.1 * jax.random.normal(splits[15], (D,), jnp.float32), 0.5, 1.5)
    b_ffn = gaussian(splits[16], (D,), 0.5, 3.0, (), jnp.float32)
    out_grad = gaussian(splits[17], (TOKENS, D), 1.0, 6.0, ((0, 8),))
    pool_grad = gaussian(splits[18], (SLOTS, PW), 1.0, 6.0, ((0, 8),), jnp.float32)
    return dict(tokens=tokens, lengths=lengths, w_query=w_query, w_key=w_key, w_value=w_value, b_query=b_query, b_value=b_value, w_out=w_out, b_out=b_out, g_attn=g_attn, b_attn=b_attn, w_up=w_up, b_up=b_up, w_down=w_down, b_down=b_down, g_ffn=g_ffn, b_ffn=b_ffn, out_grad=out_grad, pool_grad=pool_grad)


@jax.custom_vjp
def low(v):
    return lax.optimization_barrier(v.astype(jnp.bfloat16)).astype(jnp.float32)

@jax.custom_vjp
def low_back(v):
    return v

def low_keep(v):
    return (low(v), None)

def low_pass(kept, grad):
    return (grad,)

def back_keep(v):
    return (v, None)

def back_low(kept, grad):
    return (low(grad),)
low.defvjp(low_keep, low_pass)
low_back.defvjp(back_keep, back_low)
highest = lax.Precision.HIGHEST
norm_eps = 1e-06
pool_eps = 1e-05

def matmul(left, right):
    return jnp.dot(left, right, precision=highest, preferred_element_type=jnp.float32)

def layer_norm(rows, gain, shift):
    centre = lax.optimization_barrier(jnp.mean(rows, axis=-1, keepdims=True))
    shifted = rows - centre
    inverse = lax.rsqrt(lax.optimization_barrier(jnp.mean(shifted * shifted, axis=-1, keepdims=True)) + norm_eps)
    return shifted * inverse * gain + shift

def segment_ids(sizes):
    ends = jnp.cumsum(sizes, dtype=jnp.int32)
    places = jnp.arange(BUCKET, dtype=jnp.int32)
    return lax.optimization_barrier(jnp.sum((places[:, None] >= ends[None, :]).astype(jnp.int32), axis=1))

def truncations(width):
    return [width, width * 2 // 3, width // 3, width // 6, width // 12]

def bucket_forward(params, block, segment):
    w_query, w_key, w_value, b_query, b_value, w_out, b_out, g_attn, b_attn, w_up, b_up, w_down, b_down, g_ffn, b_ffn = params
    inputs = low(block)
    query_rows = low(low_back(matmul(inputs, w_query)) + b_query)
    key_rows = low(low_back(matmul(inputs, w_key)))
    value_rows = low(low_back(matmul(inputs, w_value)) + b_value)
    query_heads = query_rows.reshape(BUCKET, HEADS, HDIM)
    key_heads = key_rows.reshape(BUCKET, HEADS, HDIM)
    value_heads = value_rows.reshape(BUCKET, HEADS, HDIM)
    scores = low_back(jnp.einsum('qhd,khd->hqk', query_heads, key_heads, precision=highest)) * HDIM ** (-0.5)
    allowed = segment[:, None] == segment[None, :]
    scores = jnp.where(allowed[None], scores, -1000000000.0)
    probs = jax.nn.softmax(scores, axis=-1)
    mixed = jnp.einsum('hqk,khd->qhd', low(probs), value_heads, precision=highest).reshape(BUCKET, D)
    mixed = low_back(low(mixed))
    hidden = block + low_back(matmul(mixed, w_out)) + b_out
    normed = layer_norm(hidden, g_attn, b_attn)
    upper = low_back(matmul(low(normed), w_up)) + b_up
    act_rows = low(jax.nn.gelu(upper, approximate=False))
    resid = normed + low_back(matmul(act_rows, w_down)) + b_down
    return layer_norm(resid, g_ffn, b_ffn)

def pool_rows(final, segment, sizes):
    sentence = jnp.arange(SENTS, dtype=jnp.int32)
    member = (segment[None, :] == sentence[:, None]).astype(jnp.float32)
    pooled = matmul(member, final) / jnp.maximum(sizes, 1).astype(jnp.float32)[:, None]
    pieces = []
    for keep_width in truncations(D):
        leading = pooled[:, :keep_width]
        pieces.append(leading * lax.rsqrt(lax.optimization_barrier(jnp.mean(leading * leading, axis=1, keepdims=True)) + pool_eps))
    return jnp.concatenate(pieces, axis=1)

def reference(tokens, lengths, w_query, w_key, w_value, b_query, b_value, w_out, b_out, g_attn, b_attn, w_up, b_up, w_down, b_down, g_ffn, b_ffn, out_grad, pool_grad):
    weights = tuple((item.astype(jnp.float32) for item in (w_query, w_key, w_value, b_query, b_value, w_out, b_out, g_attn, b_attn, w_up, b_up, w_down, b_down, g_ffn, b_ffn)))
    inputs = tokens.astype(jnp.float32).reshape(N_DP, BUCKET, D)
    segments = jax.vmap(segment_ids)(lengths)

    def forward(rows, params):

        def one_bucket(packed):
            block, segment, sizes = packed
            final = bucket_forward(params, block, segment)
            return (final, pool_rows(final, segment, sizes))
        return lax.map(jax.checkpoint(one_bucket), (rows, segments, lengths))
    (finals, pooled), pullback = jax.vjp(forward, inputs, weights)
    cotangent = (out_grad.astype(jnp.float32).reshape(N_DP, BUCKET, D), pool_grad.reshape(N_DP, SENTS, PW))
    grad_inputs, grad_weights = pullback(cotangent)
    grad_wquery, grad_wkey, grad_wvalue, grad_bquery, grad_bvalue, grad_wout, grad_bout, grad_gattn, grad_battn, grad_wup, grad_bup, grad_wdown, grad_bdown, grad_gffn, grad_bffn = grad_weights
    return (finals.reshape(TOKENS, D).astype(jnp.bfloat16), pooled.reshape(SLOTS, PW), grad_inputs.reshape(TOKENS, D), grad_wquery, grad_wkey, grad_wvalue, grad_bquery, grad_bvalue, grad_wout, grad_bout, grad_gattn, grad_battn, grad_wup, grad_bup, grad_wdown, grad_bdown, grad_gffn, grad_bffn)
```

```python
import functools

import jax
import jax.numpy as jnp
from jax import lax
from jax.experimental import pallas as pl
from jax.experimental.pallas import tpu as pltpu
from jax.sharding import PartitionSpec as P

HDIM = 64
SENTS = 16
norm_eps = 1e-06
pool_eps = 1e-05
highest = lax.Precision.HIGHEST
f32 = jnp.float32
bf16 = jnp.bfloat16
swaps = {k: [(i, i ^ k) for i in range(4)] for k in (1, 2, 3)}


def truncations(width):
    return [width, width * 2 // 3, width // 3, width // 6, width // 12]


def nn(left, right, precision=None):
    return lax.dot_general(
        left, right, (((1,), (0,)), ((), ())), precision=precision, preferred_element_type=f32
    )


def nt(left, right):
    return lax.dot_general(left, right, (((1,), (1,)), ((), ())), preferred_element_type=f32)


def tn(left, right):
    return lax.dot_general(left, right, (((0,), (0,)), ((), ())), preferred_element_type=f32)


def norm_stats(rows):
    centre = jnp.mean(rows, axis=-1, keepdims=True)
    shifted = rows - centre
    inverse = lax.rsqrt(jnp.mean(shifted * shifted, axis=-1, keepdims=True) + norm_eps)
    return shifted * inverse, inverse


def norm_back(grad_in, normal, inverse):
    centre = jnp.mean(grad_in, axis=-1, keepdims=True)
    along = jnp.mean(grad_in * normal, axis=-1, keepdims=True)
    return inverse * (grad_in - centre - normal * along)


def col_sum(rows):
    return jnp.sum(rows, axis=0, keepdims=True)


def shape(*extent, kind=f32):
    return jax.ShapeDtypeStruct(extent, kind)


def call(body, outs, ins, flops=0, moved=0, scratch=(), limit=32):
    specs = [
        pl.BlockSpec(memory_space=pltpu.SMEM if item.dtype == jnp.int32 else pltpu.VMEM)
        for item in ins
    ]
    return pl.pallas_call(
        body,
        out_shape=outs,
        in_specs=specs,
        out_specs=jax.tree.map(lambda _: pl.BlockSpec(memory_space=pltpu.VMEM), outs),
        scratch_shapes=list(scratch),
        cost_estimate=pl.CostEstimate(flops=flops, bytes_accessed=moved, transcendentals=0),
        compiler_params=pltpu.CompilerParams(vmem_limit_bytes=limit << 20),
    )(*ins)


def chunk(me, j, rows):
    return pl.ds(pl.multiple_of((me ^ j) * rows, rows), rows)


def segment_of(lengths, places):
    end = jnp.int32(0)
    found = jnp.zeros(places.shape, jnp.int32)
    for s in range(SENTS):
        end = end + lengths[0, s]
        found = found + jnp.where(places >= end, 1, 0)
    return found


def row_places(me, extent, dim, rows):
    at = lax.broadcasted_iota(jnp.int32, extent, dim)
    return ((at // rows) ^ me) * rows + at % rows


def attend(ids, lens, tok, wq, wk, wv, bq, bv, tok_x, q_out, k_out, v_out, probs_out, low_out, wide_out):
    me = ids[0]
    slots, cols = q_out.shape
    rows = slots // 4
    for j in range(4):
        tok_x[j * rows : (j + 1) * rows, :] = tok[chunk(me, j, rows), :]
    t = tok_x[...]
    q_out[...] = (nt(t, wq[...]) + bq[...]).astype(bf16)
    k_out[...] = nt(t, wk[...]).astype(bf16)
    v_out[...] = (nt(t, wv[...]) + bv[...]).astype(bf16)
    seg_row = segment_of(lens, row_places(me, (1, slots), 1, rows))
    seg_col = segment_of(lens, row_places(me, (slots, 1), 0, rows))
    scale = HDIM**-0.5
    for j in range(4):
        at = slice(j * rows, (j + 1) * rows)
        allowed = seg_col[at] == seg_row
        for h in range(cols // HDIM):
            lane = slice(h * HDIM, (h + 1) * HDIM)
            s = jnp.where(allowed, nt(q_out[at, lane], k_out[:, lane]) * scale, -1000000000.0)
            e = jnp.exp(s - jnp.max(s, axis=-1, keepdims=True))
            p = (e * (1.0 / jnp.sum(e, axis=-1, keepdims=True))).astype(bf16)
            probs_out[h, at, :] = p
            low_out[at, lane] = nn(p, v_out[:, lane]).astype(bf16)
        wide_out[at, :] = low_out[at, :].astype(f32)


def join_w_out(ids, *refs):
    pieces, out, held = refs[:-2], refs[-2], refs[-1]
    step = pieces[0].shape[1]
    for d in range(len(pieces)):
        at = pl.ds(pl.multiple_of((ids[1] ^ d) * step, 8), step)
        for k in range(4):
            held[k, at, :] = pieces[d][k]
    out[...] = held[...].astype(bf16)


def gelu_grad(upper, out):
    rows = 64
    for r in range(0, upper.shape[0], rows):
        u = upper[r : r + rows, :]
        cdf = 0.5 * (1.0 + lax.erf(u * 0.7071067811865476))
        out[r : r + rows, :] = cdf + u * (0.3989422804014327 * jnp.exp(-0.5 * u * u))


def feed(tok_x, m0, m1, m2, m3, w_all, b_out, g_attn, b_attn, w_up, b_up, w_down, b_down, *outs):
    p0, p1, p2, p3, low, upper, act, normal_own, inverse_own, resid_own = outs
    parts = (p0, p1, p2, p3)
    mixed = (m0, m1, m2, m3)
    rows = p0.shape[0]
    for j in (3, 2, 1, 0):
        at = slice(j * rows, (j + 1) * rows)
        total = tok_x[at, :].astype(f32) + b_out[...]
        for k in range(4):
            i = j ^ k
            total = total + nn(mixed[k][i * rows : (i + 1) * rows, :].astype(bf16), w_all[k])
        normal, inverse = norm_stats(total)
        normed = normal * g_attn[...] + b_attn[...]
        low[at, :] = normed.astype(bf16)
        up = nn(low[at, :], w_up[...]) + b_up[...]
        upper[at, :] = up
        half = rows // 2
        for r in (0, half):
            u = upper[j * rows + r : j * rows + r + half, :]
            cdf = 0.5 * (1.0 + lax.erf(u * 0.7071067811865476))
            act[j * rows + r : j * rows + r + half, :] = (u * cdf).astype(bf16)
        parts[j][...] = nn(act[at, :], w_down[...])
        if j == 0:
            normal_own[...] = normal
            inverse_own[...] = jnp.broadcast_to(inverse, inverse_own.shape)
            resid_own[...] = normed + b_down[...]


def finish(ids, lens, r0, r1, r2, r3, g_ffn, b_ffn, out_grad, pool_grad, grad_of, w_down, w_up, *refs):
    outs, (normal_ref, inverse_ref, pooled_grad) = refs[:-3], refs[-3:]
    p0, p1, p2, p3, layer_out, pools, d_own, low_out, up_out, side = outs
    me = ids[0]
    parts = (p0, p1, p2, p3)
    rows, width = r0.shape
    gain, shift = g_ffn[...], b_ffn[...]
    seg_row = segment_of(lens, row_places(me, (1, 4 * rows), 1, rows))
    seg_col = segment_of(lens, row_places(me, (4 * rows, 1), 0, rows))
    slot_col = lax.broadcasted_iota(jnp.int32, (SENTS, 1), 0)
    slot_row = lax.broadcasted_iota(jnp.int32, (1, SENTS), 1)
    pooled = jnp.zeros((SENTS, width), f32)
    for j, block in enumerate((r0, r1, r2, r3)):
        at = slice(j * rows, (j + 1) * rows)
        normal, inverse = norm_stats(block[...])
        normal_ref[at, :] = normal
        inverse_ref[at, :] = jnp.broadcast_to(inverse, (rows, 128))
        final = normal * gain + shift
        layer_out[chunk(me, j, rows), :] = final.astype(bf16)
        member = jnp.where(slot_col == seg_row[:, at], 1.0, 0.0)
        pooled = pooled + nn(member, final, highest)
    denom = jnp.zeros((SENTS, 1), f32)
    for s in range(SENTS):
        size = jnp.maximum(lens[0, s], 1).astype(f32)
        denom = denom + jnp.where(slot_col == s, size, 0.0)
    pooled = pooled / denom
    pooled_grad[...] = jnp.zeros((SENTS, width), f32)
    offset = 0
    for m in truncations(width):
        leading = pooled[:, :m]
        factor = lax.rsqrt(jnp.mean(leading * leading, axis=1, keepdims=True) + pool_eps)
        third, lane = offset // width, offset % width
        pools[third * SENTS : (third + 1) * SENTS, lane : lane + m] = leading * factor
        upstream = pool_grad[:, offset : offset + m]
        inner = jnp.mean(upstream * leading, axis=1, keepdims=True)
        pooled_grad[:, :m] += factor * upstream - leading * (factor * factor * factor * inner)
        offset += m
    rest = offset % width
    pools[2 * SENTS :, rest:] = jnp.zeros((SENTS, width - rest), f32)
    spread = pooled_grad[...] / denom
    sums = [jnp.zeros((1, width), f32) for _ in range(4)]
    for j in (3, 2, 1, 0):
        at = slice(j * rows, (j + 1) * rows)
        belongs = jnp.where(seg_col[at] == slot_row, 1.0, 0.0)
        d_final = out_grad[chunk(me, j, rows), :].astype(f32) + nn(belongs, spread, highest)
        normal = normal_ref[at, :]
        sums[0] = sums[0] + col_sum(d_final)
        sums[1] = sums[1] + col_sum(d_final * normal)
        d_resid = norm_back(d_final * gain, normal, inverse_ref[at, :1])
        sums[2] = sums[2] + col_sum(d_resid)
        low_out[at, :] = d_resid.astype(bf16)
        d_upper = nt(low_out[at, :], w_down[...]) * grad_of[at, :]
        sums[3] = sums[3] + col_sum(d_upper)
        up_out[at, :] = d_upper.astype(bf16)
        parts[j][...] = nt(up_out[at, :], w_up[...])
        if j == 0:
            d_own[...] = d_resid
    for n in range(4):
        side[n : n + 1, :] = sums[n]
    side[4:, :] = jnp.zeros((4, width), f32)


def ffn_grads(ids, low, up_low, act, resid_low, even, odd, held):
    width = low.shape[1]
    held[:width, :] = tn(low[...], up_low[...])
    held[width:, :] = tn(act[...], resid_low[...])
    step = even.shape[1]
    for d in range(8):
        at = pl.ds(pl.multiple_of((ids[1] ^ d) * step, 8), step)
        (odd if d & 1 else even)[d // 2] = held[at, :]


def back_hidden(own, near, across, d_resid, normal, inverse, g_attn, w_all, *outs):
    e0, e1, e2, e3, d_hidden_out, low_out = outs
    d_normed = d_resid[...] + (own[...] + near[...] + across[...])
    rows, width = d_normed.shape
    cols = e0.shape[1]
    side = [None, col_sum(d_normed * normal[...]), col_sum(d_normed)]
    d_hidden = norm_back(d_normed * g_attn[...], normal[...], inverse[:, :1])
    side[0] = col_sum(d_hidden)
    d_hidden_out[...] = d_hidden
    low_out[...] = d_hidden.astype(bf16)
    for k, out in enumerate((e0, e1, e2, e3)):
        out[:rows, :] = nt(low_out[...], w_all[k]).astype(bf16).astype(f32)
        for v in range(3):
            for s in range(width // cols):
                r = rows + 4 * v + s
                out[r : r + 1, :] = side[v][:, s * cols : (s + 1) * cols]
        out[rows + 12 :, :] = jnp.zeros((4, cols), f32)


def out_grads(ids, m0, m1, m2, m3, hidden_low, even, odd, held):
    rows = hidden_low.shape[0]
    for k, block in enumerate((m0, m1, m2, m3)):
        held[k] = tn(block[k * rows : (k + 1) * rows, :].astype(bf16), hidden_low[...])
    step = even.shape[2]
    for d in range(8):
        at = pl.ds(pl.multiple_of((ids[1] ^ d) * step, 8), step)
        for k in range(4):
            (odd if d & 1 else even)[d // 2, k] = held[k, at, :]


def attend_back(e0, e1, e2, e3, probs, q, k, v, wq, wk, wv, *refs):
    outs, (d_mixed, turned, d_scores) = refs[:-3], refs[-3:]
    p0, p1, p2, p3, grads, bias, shared = outs
    slots, cols = q.shape
    rows = slots // 4
    scale = HDIM**-0.5
    for j, block in enumerate((e0, e1, e2, e3)):
        d_mixed[j * rows : (j + 1) * rows, :] = block[:rows, :].astype(bf16)
    shared[...] = (e0[rows:, :] + e1[rows:, :]) + (e2[rows:, :] + e3[rows:, :])
    for h in range(cols // HDIM):
        lane = slice(h * HDIM, (h + 1) * HDIM)
        for j in range(4):
            at = slice(j * rows, (j + 1) * rows)
            p = probs[h, at, :].astype(f32)
            dp = nt(d_mixed[at, lane], v[:, lane])
            t = p * dp
            ds = (t - p * jnp.sum(t, axis=-1, keepdims=True)) * scale
            d_scores[at, :] = ds.astype(bf16)
        d_query = nn(d_scores[...], k[:, lane])
        bias[0:1, lane] = col_sum(d_query)
        grads[:, lane] = d_query.astype(bf16)
        d_key = tn(d_scores[...], q[:, lane])
        grads[:, cols + h * HDIM : cols + (h + 1) * HDIM] = d_key.astype(bf16)
        d_value = tn(probs[h], d_mixed[:, lane])
        bias[1:2, lane] = col_sum(d_value)
        grads[:, 2 * cols + h * HDIM : 2 * cols + (h + 1) * HDIM] = d_value.astype(bf16)
    bias[2:, :] = jnp.zeros((6, cols), f32)
    turned[:cols, :] = wq[...]
    turned[cols : 2 * cols, :] = wk[...]
    turned[2 * cols :, :] = wv[...]
    for j, out in ((3, p3), (2, p2), (1, p1), (0, p0)):
        out[...] = nn(grads[j * rows : (j + 1) * rows, :], turned[...])


def qkv_grads(ids, grads, tok_x, side, shared, bias, even, odd, held):
    width = tok_x.shape[1]
    cols = bias.shape[1]
    part = width // cols
    total = grads.shape[1]
    step = total // 8
    held[:total, :] = tn(grads[...], tok_x[...])
    held[total:, :] = jnp.zeros((64, width), f32)
    held[total : total + 4, :] = side[:4, :]

    @pl.when(ids[0] >= 0)
    def _():
        for n in range(2):
            held[total + 4 : total + 5, n * cols : (n + 1) * cols] = bias[n : n + 1, :]
        for n in range(3):
            for s in range(part):
                row = shared[4 * n + s : 4 * n + s + 1, :]
                held[total + 8 + n : total + 9 + n, s * cols : (s + 1) * cols] = row

    for d in range(8):
        c = ids[1] ^ d
        out = odd if d & 1 else even
        out[d // 2, :step, :] = held[pl.ds(pl.multiple_of(c * step, 8), step), :]
        out[d // 2, step:, :] = held[pl.ds(pl.multiple_of(total + c * 8, 8), 8), :]


def fold(mine, theirs, a0, a1, a2, a3):
    for n, out in enumerate((a0, a1, a2, a3)):
        out[...] = mine[n] + theirs[n]


def place(me, r0, r1, r2, r3, out):
    rows = r0.shape[0]
    for j, block in enumerate((r0, r1, r2, r3)):
        out[chunk(me[0], j, rows), :] = block[...]


def unpack_ffn(ids, *refs):
    blocks, (up_out, down_out, pools_out, held) = refs[:8], refs[8:]
    half = up_out.shape[0]
    step = 2 * half // 8
    wide = pools_out.shape[0]
    width = up_out.shape[1]
    for d, block in enumerate(blocks):
        c = ids[1] ^ d
        at = pl.ds(pl.multiple_of((c % 4) * step, 8), step)

        @pl.when(c < 4)
        def _(block=block, at=at):
            up_out[at, :] = block[:step, :]

        @pl.when(c >= 4)
        def _(block=block, at=at):
            down_out[at, :] = block[:step, :]

        to = pl.ds(pl.multiple_of(c * SENTS, 8), SENTS)
        for n in range(3):
            held[n, to, :] = block[step + n * SENTS : step + (n + 1) * SENTS, :]
    for n in range(3):
        m = min(width, wide - n * width)
        pools_out[n * width : n * width + m, :] = held[n].T[:m, :]


def unpack_attn(ids, *refs):
    blocks, (q_out, k_out, v_out, o_out, side, held) = refs[:8], refs[8:]
    cols = o_out.shape[0]
    step = 3 * cols // 8
    small = cols // 8
    for d, block in enumerate(blocks):
        c = ids[1] ^ d
        held[pl.ds(pl.multiple_of(c * step, 8), step), :] = block[:step, :]
        side[pl.ds(pl.multiple_of(c * 8, 8), 8), :] = block[step : step + 8, :]
        o_out[pl.ds(pl.multiple_of(c * small, 8), small), :] = block[step + 8 :, :]
    q_out[...] = held[:cols, :]
    k_out[...] = held[cols : 2 * cols, :]
    v_out[...] = held[2 * cols :, :]


def swap(block, k):
    return lax.ppermute(block, "tensor", swaps[k])


def swap_dp(block, k, n_dp):
    return lax.ppermute(block, "dp", [(i, i ^ k) for i in range(n_dp)])


def scatter_sum(parts):
    far = swap(parts[3], 1)
    across = swap(parts[2] + far, 2)
    near = swap(parts[1], 1)
    return parts[0], near, across


def gather(block):
    across = swap(block, 2)
    near = swap(block, 1)
    return block, near, across, swap(across, 1)


def rest_of_dp(block, n_dp):
    if n_dp == 8:
        return block
    groups = [[i + 8 * j for j in range(n_dp // 8)] for i in range(8)]
    return lax.psum(block, "dp", axis_index_groups=groups)


def dp_scatter(even, odd, n_dp):
    other = swap_dp(odd, 1, n_dp)
    flat = even.shape[-2] if even.ndim == 3 else even.shape[1] * even.shape[2]
    even = even.reshape(4, flat, even.shape[-1])
    other = other.reshape(even.shape)
    block = shape(*even.shape[1:])
    parts = call(fold, [block] * 4, [even, other], moved=3 * even.size * 4)
    total = parts[0]
    for n in (1, 2, 3):
        total = total + swap_dp(parts[n], 2 * n, n_dp)
    return rest_of_dp(total, n_dp)


def dp_gather(block, n_dp):
    blocks = [block] + [swap_dp(block, 2 * n, n_dp) for n in (1, 2, 3)]
    others = [swap_dp(item, 1, n_dp) for item in blocks]
    return [item for pair in zip(blocks, others) for item in pair]


def make_shards(n_dp):
    def shards(
        tokens,
        lengths,
        w_query,
        w_key,
        w_value,
        b_query,
        b_value,
        w_out,
        b_out,
        g_attn,
        b_attn,
        w_up,
        b_up,
        w_down,
        b_down,
        g_ffn,
        b_ffn,
        out_grad,
        pool_grad,
    ):
        me = lax.axis_index("tensor").astype(jnp.int32)
        group = (lax.axis_index("dp") % 8).astype(jnp.int32)
        ids = jnp.stack([me, group])
        slots, width = tokens.shape
        cols = w_query.shape[1]
        units = w_up.shape[1]
        heads = cols // HDIM
        rows = slots // 4
        row = lambda vector: vector.reshape(1, -1)
        wq, wk, wv = w_query.T, w_key.T, w_value.T

        piece = cols // 8
        slice_own = lax.dynamic_slice_in_dim(w_out, group * piece, piece, 0).astype(f32)
        slices = jnp.stack(gather(slice_own))
        w_all = call(
            join_w_out,
            shape(4, cols, width, kind=bf16),
            [ids] + dp_gather(slices, n_dp),
            moved=4 * cols * width * 6,
            scratch=[pltpu.VMEM((4, cols, width), f32)],
        )

        tok_x, q, k, v, probs, mixed_low, mixed = call(
            attend,
            [
                shape(slots, width, kind=bf16),
                shape(slots, cols, kind=bf16),
                shape(slots, cols, kind=bf16),
                shape(slots, cols, kind=bf16),
                shape(heads, slots, slots, kind=bf16),
                shape(slots, cols, kind=bf16),
                shape(slots, cols),
            ],
            [ids, lengths, tokens, wq, wk, wv, row(b_query), row(b_value)],
            flops=2 * slots * width * 3 * cols + 4 * slots * slots * cols,
            moved=slots * width * 4 + 3 * cols * width * 2 + heads * slots * slots * 2,
        )
        mixed_all = gather(mixed)
        *parts, normed_low, upper, act, normal_own, inverse_own, resid_own = call(
            feed,
            [shape(rows, width)] * 4
            + [
                shape(slots, width, kind=bf16),
                shape(slots, units),
                shape(slots, units, kind=bf16),
                shape(rows, width),
                shape(rows, 128),
                shape(rows, width),
            ],
            [tok_x, *mixed_all, w_all, row(b_out), row(g_attn), row(b_attn)]
            + [w_up, row(b_up), w_down, row(b_down)],
            flops=2 * slots * width * (width + 2 * units),
            moved=4 * slots * width * 4 + 3 * width * units * 2,
        )
        slope = call(
            gelu_grad, shape(slots, units), [upper], moved=8 * slots * units, flops=slots * units
        )
        own, near, across = scatter_sum(parts)
        resid = gather(resid_own + own + near + across)
        *parts, layer_out, own_pools, d_resid, resid_low, upper_low, side = call(
            finish,
            [shape(rows, width)] * 4
            + [
                shape(slots, width, kind=bf16),
                shape(3 * SENTS, width),
                shape(rows, width),
                shape(slots, width, kind=bf16),
                shape(slots, units, kind=bf16),
                shape(8, width),
            ],
            [ids, lengths, *resid, row(g_ffn), row(b_ffn), out_grad, pool_grad, slope]
            + [w_down, w_up],
            flops=4 * slots * width * units,
            moved=6 * slots * width * 4,
            scratch=[
                pltpu.VMEM((slots, width), f32),
                pltpu.VMEM((slots, 128), f32),
                pltpu.VMEM((SENTS, width), f32),
            ],
        )
        own, near, across = scatter_sum(parts)
        step = 2 * width // 8
        even, odd = call(
            ffn_grads,
            [shape(4, step, width)] * 2,
            [ids, normed_low, upper_low, act, resid_low],
            flops=4 * slots * width * units,
            moved=4 * slots * width * 2 + 8 * width * units,
            scratch=[pltpu.VMEM((2 * width, width), f32)],
        )
        ffn_sum = dp_scatter(even, odd, n_dp)
        *sent, d_hidden, hidden_low = call(
            back_hidden,
            [shape(rows + 16, cols)] * 4 + [shape(rows, width), shape(rows, width, kind=bf16)],
            [own, near, across, d_resid, normal_own, inverse_own, row(g_attn), w_all],
            flops=2 * rows * width * 4 * cols,
            moved=6 * rows * width * 4,
        )
        d_mixed = [sent[0]] + [swap(sent[n], n) for n in (1, 2, 3)]
        even, odd = call(
            out_grads,
            [shape(4, 4, piece, width)] * 2,
            [ids, *mixed_all, hidden_low],
            flops=2 * rows * width * 4 * cols,
            moved=8 * 4 * cols * width,
            scratch=[pltpu.VMEM((4, cols, width), f32)],
        )
        out_sum = dp_scatter(even, odd, n_dp)
        *parts, grads, bias, shared = call(
            attend_back,
            [shape(rows, width)] * 4
            + [shape(slots, 3 * cols, kind=bf16), shape(8, cols), shape(16, cols)],
            [*d_mixed, probs, q, k, v, wq, wk, wv],
            flops=8 * slots * slots * cols + 6 * slots * width * cols,
            moved=heads * slots * slots * 2 + 2 * slots * width * 4,
            scratch=[
                pltpu.VMEM((slots, cols), bf16),
                pltpu.VMEM((3 * cols, width), bf16),
                pltpu.VMEM((slots, slots), bf16),
            ],
        )
        even, odd = call(
            qkv_grads,
            [shape(4, 3 * piece + 8, width)] * 2,
            [ids, grads, tok_x, side, shared, bias],
            flops=6 * slots * width * cols,
            moved=8 * 3 * cols * width,
            scratch=[pltpu.VMEM((3 * cols + 64, width), f32)],
        )
        own, near, across = scatter_sum(parts)
        qkv_sum = dp_scatter(even, odd, n_dp)
        out_parts = out_sum.reshape(4, piece, width)
        out_terms = scatter_sum([out_parts[n] for n in range(4)])
        attn_own = jnp.concatenate([qkv_sum, sum(out_terms)])
        attn_blocks = dp_gather(attn_own, n_dp)
        own_rows = [own + near + across + d_hidden]
        d_tokens = call(
            place, shape(slots, width), [ids, *gather(own_rows[0])], moved=8 * slots * width
        )
        ffn_blocks = dp_gather(jnp.concatenate([ffn_sum, own_pools]), n_dp)
        wide = pool_grad.shape[1]
        d_w_up, d_w_down, pools = call(
            unpack_ffn,
            [shape(width, units), shape(units, width), shape(wide, 8 * SENTS)],
            [ids, *ffn_blocks],
            moved=16 * width * units,
            scratch=[pltpu.VMEM((3, 8 * SENTS, width), f32)],
        )
        pools = pools.T
        if n_dp > 8:
            third = [own_pools[n * SENTS : (n + 1) * SENTS] for n in range(3)]
            third = jnp.concatenate(third, axis=1)[:, :wide]
            pools = lax.all_gather(third, "dp", axis=0, tiled=True)
        d_w_query, d_w_key, d_w_value, d_w_out, vectors = call(
            unpack_attn,
            [shape(cols, width)] * 4 + [shape(64, width)],
            [ids, *attn_blocks],
            moved=8 * 4 * cols * width,
            scratch=[pltpu.VMEM((3 * cols, width), f32)],
        )
        return (
            layer_out,
            pools,
            d_tokens,
            d_w_query.T,
            d_w_key.T,
            d_w_value.T,
            vectors[4, :cols],
            vectors[4, cols : 2 * cols],
            d_w_out,
            vectors[8],
            vectors[9],
            vectors[10],
            d_w_up,
            vectors[3],
            d_w_down,
            vectors[2],
            vectors[1],
            vectors[0],
        )

    return shards


def solution(mesh):
    return jax.shard_map(
        make_shards(mesh.shape["dp"]),
        mesh=mesh,
        in_specs=(
            P("dp", None),
            P("dp", None),
            P(None, "tensor"),
            P(None, "tensor"),
            P(None, "tensor"),
            P("tensor"),
            P("tensor"),
            P("tensor", None),
            P(),
            P(),
            P(),
            P(None, "tensor"),
            P("tensor"),
            P("tensor", None),
            P(),
            P(),
            P(),
            P("dp", None),
            P("dp", None),
        ),
        out_specs=(
            P("dp", None),
            P(),
            P("dp", None),
            P(None, "tensor"),
            P(None, "tensor"),
            P(None, "tensor"),
            P("tensor"),
            P("tensor"),
            P("tensor", None),
            P(),
            P(),
            P(),
            P(None, "tensor"),
            P("tensor"),
            P("tensor", None),
            P(),
            P(),
            P(),
        ),
        check_vma=False,
    )
```

```python
import functools

import jax
import jax.numpy as jnp
from jax import lax
from jax.experimental import pallas as pl
from jax.experimental.pallas import tpu as pltpu
from jax.sharding import PartitionSpec as P

HDIM = 64
SENTS = 16
norm_eps = 1e-06
pool_eps = 1e-05
highest = lax.Precision.HIGHEST
f32 = jnp.float32
bf16 = jnp.bfloat16
swaps = {k: [(i, i ^ k) for i in range(4)] for k in (1, 2, 3)}


def truncations(width):
    return [width, width * 2 // 3, width // 3, width // 6, width // 12]


def nn(left, right, precision=None):
    return lax.dot_general(
        left, right, (((1,), (0,)), ((), ())), precision=precision, preferred_element_type=f32
    )


def nt(left, right):
    return lax.dot_general(left, right, (((1,), (1,)), ((), ())), preferred_element_type=f32)


def tn(left, right):
    return lax.dot_general(left, right, (((0,), (0,)), ((), ())), preferred_element_type=f32)


def norm_stats(rows):
    centre = jnp.mean(rows, axis=-1, keepdims=True)
    shifted = rows - centre
    inverse = lax.rsqrt(jnp.mean(shifted * shifted, axis=-1, keepdims=True) + norm_eps)
    return shifted * inverse, inverse


def norm_back(grad_in, normal, inverse):
    centre = jnp.mean(grad_in, axis=-1, keepdims=True)
    along = jnp.mean(grad_in * normal, axis=-1, keepdims=True)
    return inverse * (grad_in - centre - normal * along)


def col_sum(rows):
    return jnp.sum(rows, axis=0, keepdims=True)


def shape(*extent, kind=f32):
    return jax.ShapeDtypeStruct(extent, kind)


def call(body, outs, ins, flops=0, moved=0, scratch=(), limit=32):
    specs = [
        pl.BlockSpec(memory_space=pltpu.SMEM if item.dtype == jnp.int32 else pltpu.VMEM)
        for item in ins
    ]
    return pl.pallas_call(
        body,
        out_shape=outs,
        in_specs=specs,
        out_specs=jax.tree.map(lambda _: pl.BlockSpec(memory_space=pltpu.VMEM), outs),
        scratch_shapes=list(scratch),
        cost_estimate=pl.CostEstimate(flops=flops, bytes_accessed=moved, transcendentals=0),
        compiler_params=pltpu.CompilerParams(vmem_limit_bytes=limit << 20),
    )(*ins)


def chunk(me, j, rows):
    return pl.ds(pl.multiple_of((me ^ j) * rows, rows), rows)


def segment_of(lengths, places):
    end = jnp.int32(0)
    found = jnp.zeros(places.shape, jnp.int32)
    for s in range(SENTS):
        end = end + lengths[0, s]
        found = found + jnp.where(places >= end, 1, 0)
    return found


def row_places(me, extent, dim, rows):
    at = lax.broadcasted_iota(jnp.int32, extent, dim)
    return ((at // rows) ^ me) * rows + at % rows


def attend(ids, lens, tok, wq, wk, wv, bq, bv, tok_x, q_out, k_out, v_out, probs_out, low_out, wide_out):
    me = ids[0]
    slots, cols = q_out.shape
    rows = slots // 4
    for j in range(4):
        tok_x[j * rows : (j + 1) * rows, :] = tok[chunk(me, j, rows), :]
    t = tok_x[...]
    q_out[...] = (nt(t, wq[...]) + bq[...]).astype(bf16)
    k_out[...] = nt(t, wk[...]).astype(bf16)
    v_out[...] = (nt(t, wv[...]) + bv[...]).astype(bf16)
    seg_row = segment_of(lens, row_places(me, (1, slots), 1, rows))
    seg_col = segment_of(lens, row_places(me, (slots, 1), 0, rows))
    scale = HDIM**-0.5
    for j in range(4):
        at = slice(j * rows, (j + 1) * rows)
        allowed = seg_col[at] == seg_row
        for h in range(cols // HDIM):
            lane = slice(h * HDIM, (h + 1) * HDIM)
            s = jnp.where(allowed, nt(q_out[at, lane], k_out[:, lane]) * scale, -1000000000.0)
            e = jnp.exp(s - jnp.max(s, axis=-1, keepdims=True))
            p = (e * (1.0 / jnp.sum(e, axis=-1, keepdims=True))).astype(bf16)
            probs_out[h, at, :] = p
            low_out[at, lane] = nn(p, v_out[:, lane]).astype(bf16)
        wide_out[at, :] = low_out[at, :].astype(f32)


def join_w_out(ids, *refs):
    pieces, out, held = refs[:-2], refs[-2], refs[-1]
    step = pieces[0].shape[1]
    for d in range(len(pieces)):
        at = pl.ds(pl.multiple_of((ids[1] ^ d) * step, 8), step)
        for k in range(4):
            held[k, at, :] = pieces[d][k]
    out[...] = held[...].astype(bf16)


def gelu_grad(upper, out):
    rows = 64
    for r in range(0, upper.shape[0], rows):
        u = upper[r : r + rows, :]
        cdf = 0.5 * (1.0 + lax.erf(u * 0.7071067811865476))
        out[r : r + rows, :] = cdf + u * (0.3989422804014327 * jnp.exp(-0.5 * u * u))


def feed(tok_x, m0, m1, m2, m3, w_all, b_out, g_attn, b_attn, w_up, b_up, w_down, b_down, *outs):
    p0, p1, p2, p3, low, upper, act, normal_own, inverse_own, resid_own = outs
    parts = (p0, p1, p2, p3)
    mixed = (m0, m1, m2, m3)
    rows = p0.shape[0]
    for j in (3, 2, 1, 0):
        at = slice(j * rows, (j + 1) * rows)
        total = tok_x[at, :].astype(f32) + b_out[...]
        for k in range(4):
            i = j ^ k
            total = total + nn(mixed[k][i * rows : (i + 1) * rows, :].astype(bf16), w_all[k])
        normal, inverse = norm_stats(total)
        normed = normal * g_attn[...] + b_attn[...]
        low[at, :] = normed.astype(bf16)
        up = nn(low[at, :], w_up[...]) + b_up[...]
        upper[at, :] = up
        half = rows // 2
        for r in (0, half):
            u = upper[j * rows + r : j * rows + r + half, :]
            cdf = 0.5 * (1.0 + lax.erf(u * 0.7071067811865476))
            act[j * rows + r : j * rows + r + half, :] = (u * cdf).astype(bf16)
        parts[j][...] = nn(act[at, :], w_down[...])
        if j == 0:
            normal_own[...] = normal
            inverse_own[...] = jnp.broadcast_to(inverse, inverse_own.shape)
            resid_own[...] = normed + b_down[...]


def finish(ids, lens, r0, r1, r2, r3, g_ffn, b_ffn, out_grad, pool_grad, grad_of, w_down, w_up, *refs):
    outs, (normal_ref, inverse_ref, pooled_grad) = refs[:-3], refs[-3:]
    p0, p1, p2, p3, layer_out, pools, d_own, low_out, up_out, side = outs
    me = ids[0]
    parts = (p0, p1, p2, p3)
    rows, width = r0.shape
    gain, shift = g_ffn[...], b_ffn[...]
    seg_row = segment_of(lens, row_places(me, (1, 4 * rows), 1, rows))
    seg_col = segment_of(lens, row_places(me, (4 * rows, 1), 0, rows))
    slot_col = lax.broadcasted_iota(jnp.int32, (SENTS, 1), 0)
    slot_row = lax.broadcasted_iota(jnp.int32, (1, SENTS), 1)
    pooled = jnp.zeros((SENTS, width), f32)
    for j, block in enumerate((r0, r1, r2, r3)):
        at = slice(j * rows, (j + 1) * rows)
        normal, inverse = norm_stats(block[...])
        normal_ref[at, :] = normal
        inverse_ref[at, :] = jnp.broadcast_to(inverse, (rows, 128))
        final = normal * gain + shift
        layer_out[chunk(me, j, rows), :] = final.astype(bf16)
        member = jnp.where(slot_col == seg_row[:, at], 1.0, 0.0)
        pooled = pooled + nn(member, final, highest)
    denom = jnp.zeros((SENTS, 1), f32)
    for s in range(SENTS):
        size = jnp.maximum(lens[0, s], 1).astype(f32)
        denom = denom + jnp.where(slot_col == s, size, 0.0)
    pooled = pooled / denom
    pooled_grad[...] = jnp.zeros((SENTS, width), f32)
    offset = 0
    for m in truncations(width):
        leading = pooled[:, :m]
        factor = lax.rsqrt(jnp.mean(leading * leading, axis=1, keepdims=True) + pool_eps)
        third, lane = offset // width, offset % width
        pools[third * SENTS : (third + 1) * SENTS, lane : lane + m] = leading * factor
        upstream = pool_grad[:, offset : offset + m]
        inner = jnp.mean(upstream * leading, axis=1, keepdims=True)
        pooled_grad[:, :m] += factor * upstream - leading * (factor * factor * factor * inner)
        offset += m
    rest = offset % width
    pools[2 * SENTS :, rest:] = jnp.zeros((SENTS, width - rest), f32)
    spread = pooled_grad[...] / denom
    sums = [jnp.zeros((1, width), f32) for _ in range(4)]
    for j in (3, 2, 1, 0):
        at = slice(j * rows, (j + 1) * rows)
        belongs = jnp.where(seg_col[at] == slot_row, 1.0, 0.0)
        d_final = out_grad[chunk(me, j, rows), :].astype(f32) + nn(belongs, spread, highest)
        normal = normal_ref[at, :]
        sums[0] = sums[0] + col_sum(d_final)
        sums[1] = sums[1] + col_sum(d_final * normal)
        d_resid = norm_back(d_final * gain, normal, inverse_ref[at, :1])
        sums[2] = sums[2] + col_sum(d_resid)
        low_out[at, :] = d_resid.astype(bf16)
        d_upper = nt(low_out[at, :], w_down[...]) * grad_of[at, :]
        sums[3] = sums[3] + col_sum(d_upper)
        up_out[at, :] = d_upper.astype(bf16)
        parts[j][...] = nt(up_out[at, :], w_up[...])
        if j == 0:
            d_own[...] = d_resid
    for n in range(4):
        side[n : n + 1, :] = sums[n]
    side[4:, :] = jnp.zeros((4, width), f32)


def ffn_grads(ids, low, up_low, act, resid_low, even, odd, held):
    width = low.shape[1]
    held[:width, :] = tn(low[...], up_low[...])
    held[width:, :] = tn(act[...], resid_low[...])
    step = even.shape[1]
    for d in range(8):
        at = pl.ds(pl.multiple_of((ids[1] ^ d) * step, 8), step)
        (odd if d & 1 else even)[d // 2] = held[at, :]


def back_hidden(own, near, across, d_resid, normal, inverse, g_attn, w_all, *outs):
    e0, e1, e2, e3, d_hidden_out, low_out = outs
    d_normed = d_resid[...] + (own[...] + near[...] + across[...])
    rows, width = d_normed.shape
    cols = e0.shape[1]
    side = [None, col_sum(d_normed * normal[...]), col_sum(d_normed)]
    d_hidden = norm_back(d_normed * g_attn[...], normal[...], inverse[:, :1])
    side[0] = col_sum(d_hidden)
    d_hidden_out[...] = d_hidden
    low_out[...] = d_hidden.astype(bf16)
    for k, out in enumerate((e0, e1, e2, e3)):
        out[:rows, :] = nt(low_out[...], w_all[k]).astype(bf16).astype(f32)
        for v in range(3):
            for s in range(width // cols):
                r = rows + 4 * v + s
                out[r : r + 1, :] = side[v][:, s * cols : (s + 1) * cols]
        out[rows + 12 :, :] = jnp.zeros((4, cols), f32)


def out_grads(ids, m0, m1, m2, m3, hidden_low, even, odd, held):
    rows = hidden_low.shape[0]
    for k, block in enumerate((m0, m1, m2, m3)):
        held[k] = tn(block[k * rows : (k + 1) * rows, :].astype(bf16), hidden_low[...])
    step = even.shape[2]
    for d in range(8):
        at = pl.ds(pl.multiple_of((ids[1] ^ d) * step, 8), step)
        for k in range(4):
            (odd if d & 1 else even)[d // 2, k] = held[k, at, :]


def attend_back(e0, e1, e2, e3, probs, q, k, v, wq, wk, wv, *refs):
    outs, (d_mixed, turned, d_scores) = refs[:-3], refs[-3:]
    p0, p1, p2, p3, grads, bias, shared = outs
    slots, cols = q.shape
    rows = slots // 4
    scale = HDIM**-0.5
    for j, block in enumerate((e0, e1, e2, e3)):
        d_mixed[j * rows : (j + 1) * rows, :] = block[:rows, :].astype(bf16)
    shared[...] = (e0[rows:, :] + e1[rows:, :]) + (e2[rows:, :] + e3[rows:, :])
    for h in range(cols // HDIM):
        lane = slice(h * HDIM, (h + 1) * HDIM)
        for j in range(4):
            at = slice(j * rows, (j + 1) * rows)
            p = probs[h, at, :].astype(f32)
            dp = nt(d_mixed[at, lane], v[:, lane])
            t = p * dp
            ds = (t - p * jnp.sum(t, axis=-1, keepdims=True)) * scale
            d_scores[at, :] = ds.astype(bf16)
        d_query = nn(d_scores[...], k[:, lane])
        bias[0:1, lane] = col_sum(d_query)
        grads[:, lane] = d_query.astype(bf16)
        d_key = tn(d_scores[...], q[:, lane])
        grads[:, cols + h * HDIM : cols + (h + 1) * HDIM] = d_key.astype(bf16)
        d_value = tn(probs[h], d_mixed[:, lane])
        bias[1:2, lane] = col_sum(d_value)
        grads[:, 2 * cols + h * HDIM : 2 * cols + (h + 1) * HDIM] = d_value.astype(bf16)
    bias[2:, :] = jnp.zeros((6, cols), f32)
    turned[:cols, :] = wq[...]
    turned[cols : 2 * cols, :] = wk[...]
    turned[2 * cols :, :] = wv[...]
    for j, out in ((3, p3), (2, p2), (1, p1), (0, p0)):
        out[...] = nn(grads[j * rows : (j + 1) * rows, :], turned[...])


def qkv_grads(ids, grads, tok_x, side, shared, bias, even, odd, held):
    width = tok_x.shape[1]
    cols = bias.shape[1]
    part = width // cols
    total = grads.shape[1]
    step = total // 8
    held[:total, :] = tn(grads[...], tok_x[...])
    held[total:, :] = jnp.zeros((64, width), f32)
    held[total : total + 4, :] = side[:4, :]

    @pl.when(ids[0] >= 0)
    def _():
        for n in range(2):
            held[total + 4 : total + 5, n * cols : (n + 1) * cols] = bias[n : n + 1, :]
        for n in range(3):
            for s in range(part):
                row = shared[4 * n + s : 4 * n + s + 1, :]
                held[total + 8 + n : total + 9 + n, s * cols : (s + 1) * cols] = row

    for d in range(8):
        c = ids[1] ^ d
        out = odd if d & 1 else even
        out[d // 2, :step, :] = held[pl.ds(pl.multiple_of(c * step, 8), step), :]
        out[d // 2, step:, :] = held[pl.ds(pl.multiple_of(total + c * 8, 8), 8), :]


def fold(mine, theirs, a0, a1, a2, a3):
    for n, out in enumerate((a0, a1, a2, a3)):
        out[...] = mine[n] + theirs[n]


def place(me, r0, r1, r2, r3, out):
    rows = r0.shape[0]
    for j, block in enumerate((r0, r1, r2, r3)):
        out[chunk(me[0], j, rows), :] = block[...]


def unpack_ffn(ids, *refs):
    blocks, (up_out, down_out, pools_out, held) = refs[:8], refs[8:]
    half = up_out.shape[0]
    step = 2 * half // 8
    wide = pools_out.shape[0]
    width = up_out.shape[1]
    for d, block in enumerate(blocks):
        c = ids[1] ^ d
        at = pl.ds(pl.multiple_of((c % 4) * step, 8), step)

        @pl.when(c < 4)
        def _(block=block, at=at):
            up_out[at, :] = block[:step, :]

        @pl.when(c >= 4)
        def _(block=block, at=at):
            down_out[at, :] = block[:step, :]

        to = pl.ds(pl.multiple_of(c * SENTS, 8), SENTS)
        for n in range(3):
            held[n, to, :] = block[step + n * SENTS : step + (n + 1) * SENTS, :]
    for n in range(3):
        m = min(width, wide - n * width)
        pools_out[n * width : n * width + m, :] = held[n].T[:m, :]


def unpack_attn(ids, *refs):
    blocks, (q_out, k_out, v_out, o_out, side, held) = refs[:8], refs[8:]
    cols = o_out.shape[0]
    step = 3 * cols // 8
    small = cols // 8
    for d, block in enumerate(blocks):
        c = ids[1] ^ d
        held[pl.ds(pl.multiple_of(c * step, 8), step), :] = block[:step, :]
        side[pl.ds(pl.multiple_of(c * 8, 8), 8), :] = block[step : step + 8, :]
        o_out[pl.ds(pl.multiple_of(c * small, 8), small), :] = block[step + 8 :, :]
    q_out[...] = held[:cols, :]
    k_out[...] = held[cols : 2 * cols, :]
    v_out[...] = held[2 * cols :, :]


def swap(block, k):
    return lax.ppermute(block, "tensor", swaps[k])


def swap_dp(block, k, n_dp):
    return lax.ppermute(block, "dp", [(i, i ^ k) for i in range(n_dp)])


def together(*items):
    return lax.optimization_barrier(items)


def rest_of_dp(block, n_dp):
    if n_dp == 8:
        return block
    groups = [[i + 8 * j for j in range(n_dp // 8)] for i in range(8)]
    return lax.psum(block, "dp", axis_index_groups=groups)


def dp_fold(even, odd, n_dp):
    other = swap_dp(odd, 1, n_dp)
    flat = even.shape[-2] if even.ndim == 3 else even.shape[1] * even.shape[2]
    even = even.reshape(4, flat, even.shape[-1])
    other = other.reshape(even.shape)
    return call(fold, [shape(*even.shape[1:])] * 4, [even, other], moved=3 * even.size * 4)


def with_other_core(blocks, n_dp):
    others = [swap_dp(item, 1, n_dp) for item in blocks]
    return [item for pair in zip(blocks, others) for item in pair]


def make_shards(n_dp):
    def shards(
        tokens,
        lengths,
        w_query,
        w_key,
        w_value,
        b_query,
        b_value,
        w_out,
        b_out,
        g_attn,
        b_attn,
        w_up,
        b_up,
        w_down,
        b_down,
        g_ffn,
        b_ffn,
        out_grad,
        pool_grad,
    ):
        me = lax.axis_index("tensor").astype(jnp.int32)
        group = (lax.axis_index("dp") % 8).astype(jnp.int32)
        ids = jnp.stack([me, group])
        slots, width = tokens.shape
        cols = w_query.shape[1]
        units = w_up.shape[1]
        heads = cols // HDIM
        rows = slots // 4
        row = lambda vector: vector.reshape(1, -1)
        wq, wk, wv = w_query.T, w_key.T, w_value.T

        piece = cols // 8
        slice_own = lax.dynamic_slice_in_dim(w_out, group * piece, piece, 0).astype(f32)
        slices = [slice_own] + [swap(slice_own, n) for n in (1, 2, 3)]

        tok_x, q, k, v, probs, mixed_low, mixed = call(
            attend,
            [
                shape(slots, width, kind=bf16),
                shape(slots, cols, kind=bf16),
                shape(slots, cols, kind=bf16),
                shape(slots, cols, kind=bf16),
                shape(heads, slots, slots, kind=bf16),
                shape(slots, cols, kind=bf16),
                shape(slots, cols),
            ],
            [ids, lengths, tokens, wq, wk, wv, row(b_query), row(b_value)],
            flops=2 * slots * width * 3 * cols + 4 * slots * slots * cols,
            moved=slots * width * 4 + 3 * cols * width * 2 + heads * slots * slots * 2,
        )
        mixed, *slices = together(mixed, *slices)
        slices = jnp.stack(slices)
        across, near = swap(mixed, 2), swap(mixed, 1)
        w_blocks = [swap_dp(slices, 2 * n, n_dp) for n in (1, 2, 3)]
        across, near, slices, *w_blocks = together(across, near, slices, *w_blocks)
        mixed_all = [mixed, near, across, swap(across, 1)]
        w_all = call(
            join_w_out,
            shape(4, cols, width, kind=bf16),
            [ids] + with_other_core([slices] + w_blocks, n_dp),
            moved=4 * cols * width * 6,
            scratch=[pltpu.VMEM((4, cols, width), f32)],
        )
        *parts, normed_low, upper, act, normal_own, inverse_own, resid_own = call(
            feed,
            [shape(rows, width)] * 4
            + [
                shape(slots, width, kind=bf16),
                shape(slots, units),
                shape(slots, units, kind=bf16),
                shape(rows, width),
                shape(rows, 128),
                shape(rows, width),
            ],
            [tok_x, *mixed_all, w_all, row(b_out), row(g_attn), row(b_attn)]
            + [w_up, row(b_up), w_down, row(b_down)],
            flops=2 * slots * width * (width + 2 * units),
            moved=4 * slots * width * 4 + 3 * width * units * 2,
        )
        far = swap(parts[3], 1)
        slope = call(
            gelu_grad, shape(slots, units), [upper], moved=8 * slots * units, flops=slots * units
        )
        far, slope, part2, part1 = together(far, slope, parts[2], parts[1])
        across, near = swap(part2 + far, 2), swap(part1, 1)
        own = resid_own + parts[0] + near + across
        across, near = swap(own, 2), swap(own, 1)
        across, near = together(across, near)
        resid = [own, near, across, swap(across, 1)]
        *parts, layer_out, own_pools, d_resid, resid_low, upper_low, side = call(
            finish,
            [shape(rows, width)] * 4
            + [
                shape(slots, width, kind=bf16),
                shape(3 * SENTS, width),
                shape(rows, width),
                shape(slots, width, kind=bf16),
                shape(slots, units, kind=bf16),
                shape(8, width),
            ],
            [ids, lengths, *resid, row(g_ffn), row(b_ffn), out_grad, pool_grad, slope]
            + [w_down, w_up],
            flops=4 * slots * width * units,
            moved=6 * slots * width * 4,
            scratch=[
                pltpu.VMEM((slots, width), f32),
                pltpu.VMEM((slots, 128), f32),
                pltpu.VMEM((SENTS, width), f32),
            ],
        )
        far = swap(parts[3], 1)
        step = 2 * width // 8
        even, odd = call(
            ffn_grads,
            [shape(4, step, width)] * 2,
            [ids, normed_low, upper_low, act, resid_low],
            flops=4 * slots * width * units,
            moved=4 * slots * width * 2 + 8 * width * units,
            scratch=[pltpu.VMEM((2 * width, width), f32)],
        )
        ffn = dp_fold(even, odd, n_dp)
        far, part2, part1, *ffn = together(far, parts[2], parts[1], *ffn)
        across, near = swap(part2 + far, 2), swap(part1, 1)
        ffn[1], ffn[2] = swap_dp(ffn[1], 2, n_dp), swap_dp(ffn[2], 4, n_dp)
        across, near, *ffn = together(across, near, *ffn)
        *sent, d_hidden, hidden_low = call(
            back_hidden,
            [shape(rows + 16, cols)] * 4 + [shape(rows, width), shape(rows, width, kind=bf16)],
            [parts[0], near, across, d_resid, normal_own, inverse_own, row(g_attn), w_all],
            flops=2 * rows * width * 4 * cols,
            moved=6 * rows * width * 4,
        )
        d_mixed = [sent[0]] + [swap(sent[n], n) for n in (1, 2, 3)]
        ffn[3] = swap_dp(ffn[3], 6, n_dp)
        even, odd = call(
            out_grads,
            [shape(4, 4, piece, width)] * 2,
            [ids, *mixed_all, hidden_low],
            flops=2 * rows * width * 4 * cols,
            moved=8 * 4 * cols * width,
            scratch=[pltpu.VMEM((4, cols, width), f32)],
        )
        out = dp_fold(even, odd, n_dp)
        *joined, ffn_last = together(*d_mixed, *out, ffn[3])
        d_mixed, out = joined[:4], joined[4:]
        ffn_sum = rest_of_dp(ffn[0] + ffn[1] + ffn[2] + ffn_last, n_dp)
        *parts, grads, bias, shared = call(
            attend_back,
            [shape(rows, width)] * 4
            + [shape(slots, 3 * cols, kind=bf16), shape(8, cols), shape(16, cols)],
            [*d_mixed, probs, q, k, v, wq, wk, wv],
            flops=8 * slots * slots * cols + 6 * slots * width * cols,
            moved=heads * slots * slots * 2 + 2 * slots * width * 4,
            scratch=[
                pltpu.VMEM((slots, cols), bf16),
                pltpu.VMEM((3 * cols, width), bf16),
                pltpu.VMEM((slots, slots), bf16),
            ],
        )
        far = swap(parts[3], 1)
        out[1:] = [swap_dp(out[n], 2 * n, n_dp) for n in (1, 2, 3)]
        even, odd = call(
            qkv_grads,
            [shape(4, 3 * piece + 8, width)] * 2,
            [ids, grads, tok_x, side, shared, bias],
            flops=6 * slots * width * cols,
            moved=8 * 3 * cols * width,
            scratch=[pltpu.VMEM((3 * cols + 64, width), f32)],
        )
        qkv = dp_fold(even, odd, n_dp)
        ffn_own = jnp.concatenate([ffn_sum, own_pools])
        far, part2, part1, ffn_own, *joined = together(
            far, parts[2], parts[1], ffn_own, *qkv, *out
        )
        qkv, out = joined[:4], joined[4:]
        across, near = swap(part2 + far, 2), swap(part1, 1)
        ffn_x, ffn_y = swap_dp(ffn_own, 2, n_dp), swap_dp(ffn_own, 4, n_dp)
        qkv[1], qkv[2] = swap_dp(qkv[1], 2, n_dp), swap_dp(qkv[2], 4, n_dp)
        out_sum = rest_of_dp(sum(out), n_dp).reshape(4, piece, width)
        across, near, ffn_x, ffn_y, out_sum, *qkv = together(
            across, near, ffn_x, ffn_y, out_sum, *qkv
        )
        own = parts[0] + near + across + d_hidden
        across, near = swap(own, 2), swap(own, 1)
        ffn_d = swap_dp(ffn_own, 6, n_dp)
        qkv[3] = swap_dp(qkv[3], 6, n_dp)
        out_terms = [out_sum[0]] + [swap(out_sum[n], n) for n in (1, 2, 3)]
        across, near, ffn_d, *joined = together(across, near, ffn_d, *qkv, *out_terms)
        qkv, out_terms = joined[:4], joined[4:]
        far = swap(across, 1)
        attn_own = jnp.concatenate([rest_of_dp(sum(qkv), n_dp), sum(out_terms)])
        attn_blocks = [attn_own] + [swap_dp(attn_own, 2 * n, n_dp) for n in (1, 2, 3)]
        ffn_blocks = with_other_core([ffn_own, ffn_x, ffn_y, ffn_d], n_dp)
        d_tokens = call(
            place, shape(slots, width), [ids, own, near, across, far], moved=8 * slots * width
        )
        attn_blocks = with_other_core(attn_blocks, n_dp)
        wide = pool_grad.shape[1]
        d_w_up, d_w_down, pools = call(
            unpack_ffn,
            [shape(width, units), shape(units, width), shape(wide, 8 * SENTS)],
            [ids, *ffn_blocks],
            moved=16 * width * units,
            scratch=[pltpu.VMEM((3, 8 * SENTS, width), f32)],
        )
        pools = pools.T
        if n_dp > 8:
            third = [own_pools[n * SENTS : (n + 1) * SENTS] for n in range(3)]
            third = jnp.concatenate(third, axis=1)[:, :wide]
            pools = lax.all_gather(third, "dp", axis=0, tiled=True)
        d_w_query, d_w_key, d_w_value, d_w_out, vectors = call(
            unpack_attn,
            [shape(cols, width)] * 4 + [shape(64, width)],
            [ids, *attn_blocks],
            moved=8 * 4 * cols * width,
            scratch=[pltpu.VMEM((3 * cols, width), f32)],
        )
        return (
            layer_out,
            pools,
            d_tokens,
            d_w_query.T,
            d_w_key.T,
            d_w_value.T,
            vectors[4, :cols],
            vectors[4, cols : 2 * cols],
            d_w_out,
            vectors[8],
            vectors[9],
            vectors[10],
            d_w_up,
            vectors[3],
            d_w_down,
            vectors[2],
            vectors[1],
            vectors[0],
        )

    return shards


def solution(mesh):
    return jax.shard_map(
        make_shards(mesh.shape["dp"]),
        mesh=mesh,
        in_specs=(
            P("dp", None),
            P("dp", None),
            P(None, "tensor"),
            P(None, "tensor"),
            P(None, "tensor"),
            P("tensor"),
            P("tensor"),
            P("tensor", None),
            P(),
            P(),
            P(),
            P(None, "tensor"),
            P("tensor"),
            P("tensor", None),
            P(),
            P(),
            P(),
            P("dp", None),
            P("dp", None),
        ),
        out_specs=(
            P("dp", None),
            P(),
            P("dp", None),
            P(None, "tensor"),
            P(None, "tensor"),
            P(None, "tensor"),
            P("tensor"),
            P("tensor"),
            P("tensor", None),
            P(),
            P(),
            P(),
            P(None, "tensor"),
            P("tensor"),
            P("tensor", None),
            P(),
            P(),
            P(),
        ),
        check_vma=False,
    )
```

```python
import functools

import jax
import jax.numpy as jnp
from jax import lax
from jax.experimental import pallas as pl
from jax.experimental.pallas import tpu as pltpu
from jax.sharding import PartitionSpec as P

HDIM = 64
SENTS = 16
norm_eps = 1e-06
pool_eps = 1e-05
highest = lax.Precision.HIGHEST
f32 = jnp.float32
bf16 = jnp.bfloat16
order = 10**9
swaps = {k: [(i, i ^ k) for i in range(4)] for k in (1, 2, 3)}


def truncations(width):
    return [width, width * 2 // 3, width // 3, width // 6, width // 12]


def nn(left, right, precision=None):
    return lax.dot_general(
        left, right, (((1,), (0,)), ((), ())), precision=precision, preferred_element_type=f32
    )


def nt(left, right):
    return lax.dot_general(left, right, (((1,), (1,)), ((), ())), preferred_element_type=f32)


def tn(left, right):
    return lax.dot_general(left, right, (((0,), (0,)), ((), ())), preferred_element_type=f32)


def norm_stats(rows):
    centre = jnp.mean(rows, axis=-1, keepdims=True)
    shifted = rows - centre
    inverse = lax.rsqrt(jnp.mean(shifted * shifted, axis=-1, keepdims=True) + norm_eps)
    return shifted * inverse, inverse


def norm_back(grad_in, normal, inverse):
    centre = jnp.mean(grad_in, axis=-1, keepdims=True)
    along = jnp.mean(grad_in * normal, axis=-1, keepdims=True)
    return inverse * (grad_in - centre - normal * along)


def col_sum(rows):
    return jnp.sum(rows, axis=0, keepdims=True)


def shape(*extent, kind=f32):
    return jax.ShapeDtypeStruct(extent, kind)


def call(body, outs, ins, flops=0, moved=0, scratch=(), limit=32, raw=0):
    specs = [
        pl.BlockSpec(memory_space=pltpu.SMEM if item.dtype == jnp.int32 else pltpu.VMEM)
        for item in ins[: len(ins) - raw]
    ] + [pl.BlockSpec(memory_space=pltpu.HBM)] * raw
    return pl.pallas_call(
        body,
        out_shape=outs,
        in_specs=specs,
        out_specs=jax.tree.map(lambda _: pl.BlockSpec(memory_space=pltpu.VMEM), outs),
        scratch_shapes=list(scratch),
        cost_estimate=pl.CostEstimate(flops=flops, bytes_accessed=moved, transcendentals=0),
        compiler_params=pltpu.CompilerParams(vmem_limit_bytes=limit << 20),
    )(*ins)


def chunk(me, j, rows):
    return pl.ds(pl.multiple_of((me ^ j) * rows, rows), rows)


def segment_of(lengths, places):
    end = jnp.int32(0)
    found = jnp.zeros(places.shape, jnp.int32)
    for s in range(SENTS):
        end = end + lengths[0, s]
        found = found + jnp.where(places >= end, 1, 0)
    return found


def row_places(me, extent, dim, rows):
    at = lax.broadcasted_iota(jnp.int32, extent, dim)
    return ((at // rows) ^ me) * rows + at % rows


def packed_rows(rows, cols):
    return rows * (cols // 128) + (rows // 2 if cols % 128 else 0)


def pack_into(out, block):
    rows, cols = block.shape
    full = cols // 128
    for n in range(full):
        out[n * rows : (n + 1) * rows, :] = block[:, n * 128 : (n + 1) * 128]
    if cols % 128:
        half = rows // 2
        out[full * rows : full * rows + half, :HDIM] = block[:half, full * 128 :]
        out[full * rows : full * rows + half, HDIM:] = block[half:, full * 128 :]


def packed_parts(block, cols, slots, start, rows):
    full = cols // 128
    for n in range(full):
        yield n * 128, block[n * slots + start : n * slots + start + rows, :]
    if cols % 128:
        half = slots // 2
        side = start // half
        at = full * slots + start - side * half
        yield full * 128, block[at : at + rows, side * HDIM : (side + 1) * HDIM]


def attend(ids, lengths, tok, wq_in, wk_in, wv_in, bq_in, bv_in, *refs):
    tok_x, q_out, k_out, v_out, probs_out, packed, low, wq, wk, wv, bq, bv, lens, sems = refs
    me = ids[0]
    slots, cols = q_out.shape
    rows = slots // 4
    moves = [
        (lengths, lens),
        (wk_in, wk),
        *[(tok.at[chunk(me, j, rows), :], tok_x.at[j * rows : (j + 1) * rows, :]) for j in range(4)],
        (wv_in, wv),
        (bv_in, bv),
        (wq_in, wq),
        (bq_in, bq),
    ]
    moves = [pltpu.make_async_copy(a, b, sems.at[n]) for n, (a, b) in enumerate(moves)]
    for move in moves:
        move.start()
    for move in moves[:6]:
        move.wait()
    t = tok_x[...]
    k_out[...] = nt(t, wk[...]).astype(bf16)
    for move in moves[6:]:
        move.wait()
    v_out[...] = (nt(t, wv[...]) + bv[...]).astype(bf16)
    q_out[...] = (nt(t, wq[...]) + bq[...]).astype(bf16)
    seg_row = segment_of(lens, row_places(me, (1, slots), 1, rows))
    seg_col = segment_of(lens, row_places(me, (slots, 1), 0, rows))
    scale = HDIM**-0.5
    for j in range(4):
        at = slice(j * rows, (j + 1) * rows)
        allowed = seg_col[at] == seg_row
        for h in range(cols // HDIM):
            lane = slice(h * HDIM, (h + 1) * HDIM)
            s = jnp.where(allowed, nt(q_out[at, lane], k_out[:, lane]) * scale, -1000000000.0)
            e = jnp.exp(s - jnp.max(s, axis=-1, keepdims=True))
            p = (e * (1.0 / jnp.sum(e, axis=-1, keepdims=True))).astype(bf16)
            probs_out[h, at, :] = p
            low[at, lane] = nn(p, v_out[:, lane]).astype(bf16)
    pack_into(packed, low[...].astype(f32))


def join_w_out(ids, *refs):
    pieces, out, held = refs[:-2], refs[-2], refs[-1]
    step = pieces[0].shape[1]
    for d in range(len(pieces)):
        at = pl.ds(pl.multiple_of((ids[1] ^ d) * step, 8), step)
        for k in range(4):
            held[k, at, :] = pieces[d][k]
    out[...] = held[...].astype(bf16)


def gelu_grad(upper, out):
    rows = 64
    for r in range(0, upper.shape[0], rows):
        u = upper[r : r + rows, :]
        cdf = 0.5 * (1.0 + lax.erf(u * 0.7071067811865476))
        out[r : r + rows, :] = cdf + u * (0.3989422804014327 * jnp.exp(-0.5 * u * u))


def feed_chunk(j, tok_x, mixed, w_all, b_out, g_attn, b_attn, w_up, b_up, w_down, low, upper, act, part):
    rows = part.shape[0]
    at = slice(j * rows, (j + 1) * rows)
    total = tok_x[at, :].astype(f32) + b_out[...]
    for k in range(4):
        for col, block in packed_parts(mixed[k], w_all.shape[1], 4 * rows, (j ^ k) * rows, rows):
            total = total + nn(block.astype(bf16), w_all[k, col : col + block.shape[1], :])
    normal, inverse = norm_stats(total)
    normed = normal * g_attn[...] + b_attn[...]
    low[...] = normed.astype(bf16)
    upper[...] = nn(low[...], w_up[...]) + b_up[...]
    half = rows // 2
    for r in (0, half):
        u = upper[r : r + half, :]
        cdf = 0.5 * (1.0 + lax.erf(u * 0.7071067811865476))
        act[r : r + half, :] = (u * cdf).astype(bf16)
    part[...] = nn(act[...], w_down[...])
    return normed, normal, inverse


def feed_first(tok_x, m0, m1, m2, m3, w_all, b_out, g_attn, b_attn, w_up, b_up, w_down, *outs):
    part, low, upper, act = outs
    mixed = (m0, m1, m2, m3)
    ins = (tok_x, mixed, w_all, b_out, g_attn, b_attn, w_up, b_up, w_down)
    feed_chunk(3, *ins, low, upper, act, part)


def feed_rest(tok_x, m0, m1, m2, m3, w_all, b_out, g_attn, b_attn, w_up, b_up, w_down, b_down, *refs):
    (low3, upper3, act3), outs = refs[:3], refs[3:]
    p0, p1, p2, low, upper, act, normal_own, inverse_own, resid_own = outs
    parts = (p0, p1, p2)
    mixed = (m0, m1, m2, m3)
    ins = (tok_x, mixed, w_all, b_out, g_attn, b_attn, w_up, b_up, w_down)
    rows = p0.shape[0]
    for full, piece in ((low, low3), (upper, upper3), (act, act3)):
        full[3 * rows :, :] = piece[...]
    for j in (2, 1, 0):
        at = slice(j * rows, (j + 1) * rows)
        views = (low.at[at, :], upper.at[at, :], act.at[at, :], parts[j])
        normed, normal, inverse = feed_chunk(j, *ins, *views)
    normal_own[...] = normal
    inverse_own[...] = jnp.broadcast_to(inverse, inverse_own.shape)
    resid_own[...] = normed + b_down[...]


def finish_chunk(seg, normal, inverse, gain, spread, out_grad, grad_of, w_down, w_up, low, up, part):
    slot_row = lax.broadcasted_iota(jnp.int32, (1, SENTS), 1)
    belongs = jnp.where(seg == slot_row, 1.0, 0.0)
    d_final = out_grad.astype(f32) + nn(belongs, spread, highest)
    d_resid = norm_back(d_final * gain, normal, inverse)
    low[...] = d_resid.astype(bf16)
    d_upper = nt(low[...], w_down[...]) * grad_of
    up[...] = d_upper.astype(bf16)
    part[...] = nt(up[...], w_up[...])
    return d_resid, [col_sum(d_final), col_sum(d_final * normal), col_sum(d_resid), col_sum(d_upper)]


def finish_first(
    ids, lens, r0, r1, r2, r3, g_ffn, b_ffn, out_grad, pool_grad, grad_of, w_down, w_up, *refs
):
    outs, (pooled_grad,) = refs[:-1], refs[-1:]
    part, layer_out, pools, normal_ref, inverse_ref, spread_out, low, up, side = outs
    me = ids[0]
    rows, width = r0.shape
    gain, shift = g_ffn[...], b_ffn[...]
    seg_row = segment_of(lens, row_places(me, (1, 4 * rows), 1, rows))
    seg_col = segment_of(lens, row_places(me, (4 * rows, 1), 0, rows))
    slot_col = lax.broadcasted_iota(jnp.int32, (SENTS, 1), 0)
    pooled = jnp.zeros((SENTS, width), f32)
    for j, block in enumerate((r0, r1, r2, r3)):
        at = slice(j * rows, (j + 1) * rows)
        normal, inverse = norm_stats(block[...])
        normal_ref[at, :] = normal
        inverse_ref[at, :] = jnp.broadcast_to(inverse, (rows, 128))
        final = normal * gain + shift
        layer_out[chunk(me, j, rows), :] = final.astype(bf16)
        member = jnp.where(slot_col == seg_row[:, at], 1.0, 0.0)
        pooled = pooled + nn(member, final, highest)
    denom = jnp.zeros((SENTS, 1), f32)
    for s in range(SENTS):
        size = jnp.maximum(lens[0, s], 1).astype(f32)
        denom = denom + jnp.where(slot_col == s, size, 0.0)
    pooled = pooled / denom
    pooled_grad[...] = jnp.zeros((SENTS, width), f32)
    offset = 0
    for m in truncations(width):
        leading = pooled[:, :m]
        factor = lax.rsqrt(jnp.mean(leading * leading, axis=1, keepdims=True) + pool_eps)
        third, lane = offset // width, offset % width
        pools[third * SENTS : (third + 1) * SENTS, lane : lane + m] = leading * factor
        upstream = pool_grad[:, offset : offset + m]
        inner = jnp.mean(upstream * leading, axis=1, keepdims=True)
        pooled_grad[:, :m] += factor * upstream - leading * (factor * factor * factor * inner)
        offset += m
    rest = offset % width
    pools[2 * SENTS :, rest:] = jnp.zeros((SENTS, width - rest), f32)
    spread = pooled_grad[...] / denom
    spread_out[...] = spread
    _, sums = finish_chunk(
        seg_col[3 * rows :],
        normal_ref[3 * rows :, :],
        inverse_ref[3 * rows :, :1],
        gain,
        spread,
        out_grad[chunk(me, 3, rows), :],
        grad_of[3 * rows :, :],
        w_down,
        w_up,
        low,
        up,
        part,
    )
    for n in range(4):
        side[n : n + 1, :] = sums[n]
    side[4:, :] = jnp.zeros((4, width), f32)


def finish_rest(ids, lens, g_ffn, out_grad, grad_of, w_down, w_up, *refs):
    ins, outs, (resid_low, upper_low, held) = refs[:8], refs[8:-3], refs[-3:]
    normal_ref, inverse_ref, spread, low3, up3, side3, normed_low, act = ins
    p0, p1, p2, d_own, side, even, odd = outs
    parts = (p0, p1, p2)
    me = ids[0]
    rows, width = p0.shape
    seg_col = segment_of(lens, row_places(me, (4 * rows, 1), 0, rows))
    resid_low[3 * rows :, :] = low3[...]
    upper_low[3 * rows :, :] = up3[...]
    total = [side3[n : n + 1, :] for n in range(4)]
    for j in (2, 1, 0):
        at = slice(j * rows, (j + 1) * rows)
        d_resid, sums = finish_chunk(
            seg_col[at],
            normal_ref[at, :],
            inverse_ref[at, :1],
            g_ffn[...],
            spread[...],
            out_grad[chunk(me, j, rows), :],
            grad_of[at, :],
            w_down,
            w_up,
            resid_low.at[at, :],
            upper_low.at[at, :],
            parts[j],
        )
        total = [a + b for a, b in zip(total, sums)]
    d_own[...] = d_resid
    for n in range(4):
        side[n : n + 1, :] = total[n]
    side[4:, :] = jnp.zeros((4, width), f32)
    held[:width, :] = tn(normed_low[...], upper_low[...])
    held[width:, :] = tn(act[...], resid_low[...])
    step = even.shape[1]
    for d in range(8):
        at = pl.ds(pl.multiple_of((ids[1] ^ d) * step, 8), step)
        (odd if d & 1 else even)[d // 2] = held[at, :]


def back_hidden(own, near, across, d_resid, normal, inverse, g_attn, w_all, *outs):
    e0, e1, e2, e3, d_hidden_out, low_out = outs
    d_normed = d_resid[...] + (own[...] + near[...] + across[...])
    rows, width = d_normed.shape
    cols = w_all.shape[1]
    side = [None, col_sum(d_normed * normal[...]), col_sum(d_normed)]
    d_hidden = norm_back(d_normed * g_attn[...], normal[...], inverse[:, :1])
    side[0] = col_sum(d_hidden)
    d_hidden_out[...] = d_hidden
    low_out[...] = d_hidden.astype(bf16)
    base = packed_rows(rows, cols)
    for k, out in enumerate((e0, e1, e2, e3)):
        pack_into(out, nt(low_out[...], w_all[k]).astype(bf16).astype(f32))
        out[base:, :] = jnp.zeros((out.shape[0] - base, 128), f32)
        for v in range(3):
            for s in range(width // cols):
                for n in range(0, cols, 128):
                    r = base + (n // 128) * 16 + 4 * v + s
                    m = min(128, cols - n)
                    out[r : r + 1, :m] = side[v][:, s * cols + n : s * cols + n + m]


def out_grads(ids, m0, m1, m2, m3, hidden_low, even, odd, held):
    rows = hidden_low.shape[0]
    for k, block in enumerate((m0, m1, m2, m3)):
        for col, part in packed_parts(block, held.shape[1], 4 * rows, k * rows, rows):
            held[k, col : col + part.shape[1], :] = tn(part.astype(bf16), hidden_low[...])
    step = even.shape[2]
    for d in range(8):
        at = pl.ds(pl.multiple_of((ids[1] ^ d) * step, 8), step)
        for k in range(4):
            (odd if d & 1 else even)[d // 2, k] = held[k, at, :]


def attend_back(e0, e1, e2, e3, probs, q, k, v, wq, wk, wv, *refs):
    outs, (d_mixed, turned, d_scores) = refs[:-3], refs[-3:]
    p0, p1, p2, p3, grads, bias, shared = outs
    slots, cols = q.shape
    rows = slots // 4
    scale = HDIM**-0.5
    half = rows // 2
    for j, block in enumerate((e0, e1, e2, e3)):
        for r in (0, half):
            for col, part in packed_parts(block, cols, rows, r, half):
                at = slice(j * rows + r, j * rows + r + half)
                d_mixed[at, col : col + part.shape[1]] = part.astype(bf16)
    base = packed_rows(rows, cols)
    side = (e0[base:, :] + e1[base:, :]) + (e2[base:, :] + e3[base:, :])
    for n in range(0, cols, 128):
        m = min(128, cols - n)
        shared[:, n : n + m] = side[(n // 128) * 16 : (n // 128) * 16 + 16, :m]
    for h in range(cols // HDIM):
        lane = slice(h * HDIM, (h + 1) * HDIM)
        for j in range(4):
            at = slice(j * rows, (j + 1) * rows)
            p = probs[h, at, :].astype(f32)
            dp = nt(d_mixed[at, lane], v[:, lane])
            t = p * dp
            ds = (t - p * jnp.sum(t, axis=-1, keepdims=True)) * scale
            d_scores[at, :] = ds.astype(bf16)
        d_query = nn(d_scores[...], k[:, lane])
        bias[0:1, lane] = col_sum(d_query)
        grads[:, lane] = d_query.astype(bf16)
        d_key = tn(d_scores[...], q[:, lane])
        grads[:, cols + h * HDIM : cols + (h + 1) * HDIM] = d_key.astype(bf16)
        d_value = tn(probs[h], d_mixed[:, lane])
        bias[1:2, lane] = col_sum(d_value)
        grads[:, 2 * cols + h * HDIM : 2 * cols + (h + 1) * HDIM] = d_value.astype(bf16)
    bias[2:, :] = jnp.zeros((6, cols), f32)
    turned[:cols, :] = wq[...]
    turned[cols : 2 * cols, :] = wk[...]
    turned[2 * cols :, :] = wv[...]
    for j, out in ((3, p3), (2, p2), (1, p1), (0, p0)):
        out[...] = nn(grads[j * rows : (j + 1) * rows, :], turned[...])


def qkv_grads(ids, grads, tok_x, side, shared, bias, even, odd, held):
    width = tok_x.shape[1]
    cols = bias.shape[1]
    part = width // cols
    total = grads.shape[1]
    step = total // 8
    held[:total, :] = tn(grads[...], tok_x[...])
    held[total:, :] = jnp.zeros((64, width), f32)
    held[total : total + 4, :] = side[:4, :]

    @pl.when(ids[0] >= 0)
    def _():
        for n in range(2):
            held[total + 4 : total + 5, n * cols : (n + 1) * cols] = bias[n : n + 1, :]
        for n in range(3):
            for s in range(part):
                row = shared[4 * n + s : 4 * n + s + 1, :]
                held[total + 8 + n : total + 9 + n, s * cols : (s + 1) * cols] = row

    for d in range(8):
        c = ids[1] ^ d
        out = odd if d & 1 else even
        out[d // 2, :step, :] = held[pl.ds(pl.multiple_of(c * step, 8), step), :]
        out[d // 2, step:, :] = held[pl.ds(pl.multiple_of(total + c * 8, 8), 8), :]


def fold(mine, theirs, *refs):
    extra, outs = refs[: len(refs) - 4], refs[len(refs) - 4 :]
    rows = mine.shape[1]
    for n, out in enumerate(outs):
        out[:rows, :] = mine[n] + theirs[n]
        if n and extra:
            out[rows:, :] = extra[0][...]


def fold_halves(mine, theirs, extra, own, to_x, to_y, keep_y, keep_x):
    half = mine.shape[1] // 2
    more = extra.shape[0] // 2
    own[...] = mine[0] + theirs[0]
    for n, (out, at) in enumerate(((to_x, slice(0, half)), (to_y, slice(half, 2 * half)))):
        for m, block in enumerate((1 + n, 3)):
            out[m * half : (m + 1) * half, :] = mine[block, at, :] + theirs[block, at, :]
        out[2 * half :, :] = extra[n * more : (n + 1) * more, :]
    keep_y[...] = mine[2, :half, :] + theirs[2, :half, :]
    keep_x[...] = mine[1, half:, :] + theirs[1, half:, :]


def add(a, b, out):
    out[...] = a[...] + b[...]


def cut(block, out):
    out[...] = block[: out.shape[0], :]


def join_terms(part1, part2, far, *refs):
    blocks, (near_out, across_out, terms) = refs[:-3], refs[-3:]
    rows = part1.shape[0]
    near_out[:rows, :] = part1[...]
    across_out[...] = part2[...] + far[...]
    piece = terms.shape[1]
    for n in range(4):
        at = slice(n * piece, (n + 1) * piece)
        total = blocks[0][at, :]
        for block in blocks[1:]:
            total = total + block[at, :]
        terms[n] = total
    near_out[rows:, :] = terms[3]


def join_own(own, near, across, d_hidden, terms, near_out, across_out):
    rows = own.shape[0]
    piece = terms.shape[1]
    total = own[...] + near[:rows, :] + across[...] + d_hidden[...]
    near_out[:rows, :] = total
    across_out[:rows, :] = total
    near_out[rows:, :] = terms[1]
    across_out[rows:, :] = terms[2] + near[rows : rows + piece, :]


def place(me, r0, r1, r2, r3, out):
    rows = r3.shape[0]
    for j, block in enumerate((r0, r1, r2, r3)):
        out[chunk(me[0], j, rows), :] = block[:rows, :]


def unpack_ffn(ids, mine, theirs, up_out, down_out, pools_out, held):
    half = up_out.shape[0]
    step = 2 * half // 8
    wide = pools_out.shape[0]
    width = up_out.shape[1]
    for d in range(8):
        block = theirs if d & 1 else mine
        start = (d // 2) * step
        c = ids[1] ^ d
        at = pl.ds(pl.multiple_of((c % 4) * step, 8), step)

        @pl.when(c < 4)
        def _(block=block, at=at, start=start):
            up_out[at, :] = block[start : start + step, :]

        @pl.when(c >= 4)
        def _(block=block, at=at, start=start):
            down_out[at, :] = block[start : start + step, :]

        to = pl.ds(pl.multiple_of(c * SENTS, 8), SENTS)
        start = 4 * step + (d // 2) * 3 * SENTS
        for n in range(3):
            held[n, to, :] = block[start + n * SENTS : start + (n + 1) * SENTS, :]
    for n in range(3):
        m = min(width, wide - n * width)
        pools_out[n * width : n * width + m, :] = held[n].T[:m, :]


def unpack_attn(ids, *refs):
    blocks, (q_out, k_out, v_out, o_out, side, held) = refs[:8], refs[8:]
    cols = o_out.shape[0]
    step = 3 * cols // 8
    small = cols // 8
    for d, block in enumerate(blocks):
        c = ids[1] ^ d
        held[pl.ds(pl.multiple_of(c * step, 8), step), :] = block[:step, :]
        side[pl.ds(pl.multiple_of(c * 8, 8), 8), :] = block[step : step + 8, :]
        o_out[pl.ds(pl.multiple_of(c * small, 8), small), :] = block[step + 8 :, :]
    q_out[...] = held[:cols, :]
    k_out[...] = held[cols : 2 * cols, :]
    v_out[...] = held[2 * cols :, :]


def swap(block, k):
    return lax.ppermute(block, "tensor", swaps[k])


def swap_dp(block, k, n_dp):
    return lax.ppermute(block, "dp", [(i, i ^ k) for i in range(n_dp)])


def together(*items):
    return lax.optimization_barrier(items)


def rest_of_dp(block, n_dp):
    if n_dp == 8:
        return block
    groups = [[i + 8 * j for j in range(n_dp // 8)] for i in range(8)]
    return lax.psum(block, "dp", axis_index_groups=groups)


def core_swap(even, odd, n_dp):
    other = swap_dp(odd, 1, n_dp)
    flat = even.shape[-2] if even.ndim == 3 else even.shape[1] * even.shape[2]
    return even.reshape(4, flat, even.shape[-1]), other.reshape(4, flat, even.shape[-1])


def fold_call(even, other, extra=()):
    _, rows, width = even.shape
    more = sum(item.shape[0] for item in extra)
    blocks = call(
        fold,
        [shape(rows, width)] + [shape(rows + more, width)] * 3,
        [even, other, *extra],
        moved=3 * even.size * 4,
    )
    return list(blocks)


def with_other_core(blocks, n_dp):
    others = [swap_dp(item, 1, n_dp) for item in blocks]
    return [item for pair in zip(blocks, others) for item in pair]


def make_shards(n_dp):
    def shards(
        tokens,
        lengths,
        w_query,
        w_key,
        w_value,
        b_query,
        b_value,
        w_out,
        b_out,
        g_attn,
        b_attn,
        w_up,
        b_up,
        w_down,
        b_down,
        g_ffn,
        b_ffn,
        out_grad,
        pool_grad,
    ):
        me = lax.axis_index("tensor").astype(jnp.int32)
        group = (lax.axis_index("dp") % 8).astype(jnp.int32)
        ids = jnp.stack([me, group])
        slots, width = tokens.shape
        cols = w_query.shape[1]
        units = w_up.shape[1]
        heads = cols // HDIM
        rows = slots // 4
        row = lambda vector: vector.reshape(1, -1)
        wq, wk, wv = w_query.T, w_key.T, w_value.T

        piece = cols // 8
        slice_own = lax.dynamic_slice_in_dim(w_out, group * piece, piece, 0).astype(f32)
        slices = [slice_own] + [swap(slice_own, n) for n in (1, 2, 3)]

        tok_x, q, k, v, probs, mixed = call(
            attend,
            [
                shape(slots, width, kind=bf16),
                shape(slots, cols, kind=bf16),
                shape(slots, cols, kind=bf16),
                shape(slots, cols, kind=bf16),
                shape(heads, slots, slots, kind=bf16),
                shape(packed_rows(slots, cols), 128),
            ],
            [ids]
            + [
                pltpu.with_memory_space_constraint(item, pltpu.HBM)
                for item in (lengths, tokens, wq, wk, wv, row(b_query), row(b_value))
            ],
            flops=2 * slots * width * 3 * cols + 4 * slots * slots * cols,
            moved=slots * width * 4 + 3 * cols * width * 2 + heads * slots * slots * 2,
            scratch=[pltpu.VMEM((slots, cols), bf16)]
            + [pltpu.VMEM((cols, width), bf16)] * 3
            + [pltpu.VMEM((1, cols), f32)] * 2
            + [pltpu.SMEM((1, SENTS), jnp.int32), pltpu.SemaphoreType.DMA((10,))],
            raw=7,
        )
        mixed, *slices = together(mixed, *slices)
        slices = jnp.stack(slices)
        across, near = swap(mixed, 2), swap(mixed, 1)
        w_blocks = [swap_dp(slices, 2 * n, n_dp) for n in (1, 2, 3)]
        across, near, slices, *w_blocks = together(across, near, slices, *w_blocks)
        mixed_all = [mixed, near, across, swap(across, 1)]
        w_all = call(
            join_w_out,
            shape(4, cols, width, kind=bf16),
            [ids] + with_other_core([slices] + w_blocks, n_dp),
            moved=4 * cols * width * 6,
            scratch=[pltpu.VMEM((4, cols, width), f32)],
        )
        feed_ins = [tok_x, *mixed_all, w_all, row(b_out), row(g_attn), row(b_attn)]
        feed_ins += [w_up, row(b_up), w_down]
        part3, low3, upper3, act3 = call(
            feed_first,
            [
                shape(rows, width),
                shape(rows, width, kind=bf16),
                shape(rows, units),
                shape(rows, units, kind=bf16),
            ],
            feed_ins,
            flops=2 * rows * width * (width + 2 * units),
            moved=rows * width * 4 + 3 * width * units * 2,
        )
        far = swap(part3, 1)
        *parts, normed_low, upper, act, normal_own, inverse_own, resid_own = call(
            feed_rest,
            [shape(rows, width)] * 3
            + [
                shape(slots, width, kind=bf16),
                shape(slots, units),
                shape(slots, units, kind=bf16),
                shape(rows, width),
                shape(rows, 128),
                shape(rows, width),
            ],
            feed_ins + [row(b_down), low3, upper3, act3],
            flops=6 * rows * width * (width + 2 * units),
            moved=3 * slots * width * 4 + 3 * width * units * 2,
        )
        slope = call(
            gelu_grad, shape(slots, units), [upper], moved=8 * slots * units, flops=slots * units
        )
        far, slope, part2, part1 = together(far, slope, parts[2], parts[1])
        across, near = swap(part2 + far, 2), swap(part1, 1)
        own = resid_own + parts[0] + near + across
        across, near = swap(own, 2), swap(own, 1)
        across, near = together(across, near)
        resid = [own, near, across, swap(across, 1)]
        part3, layer_out, own_pools, normal, inverse, spread, low3, up3, side3 = call(
            finish_first,
            [
                shape(rows, width),
                shape(slots, width, kind=bf16),
                shape(3 * SENTS, width),
                shape(slots, width),
                shape(slots, 128),
                shape(SENTS, width),
                shape(rows, width, kind=bf16),
                shape(rows, units, kind=bf16),
                shape(8, width),
            ],
            [ids, lengths, *resid, row(g_ffn), row(b_ffn), out_grad, pool_grad, slope]
            + [w_down, w_up],
            flops=4 * rows * width * units,
            moved=6 * slots * width * 4,
            scratch=[pltpu.VMEM((SENTS, width), f32)],
        )
        far = swap(part3, 1)
        step = 2 * width // 8
        *parts, d_resid, side, even, odd = call(
            finish_rest,
            [shape(rows, width)] * 4 + [shape(8, width)] + [shape(4, step, width)] * 2,
            [ids, lengths, row(g_ffn), out_grad, slope, w_down, w_up]
            + [normal, inverse, spread, low3, up3, side3, normed_low, act],
            flops=8 * slots * width * units,
            moved=6 * slots * width * 4 + 8 * width * units,
            scratch=[
                pltpu.VMEM((slots, width), bf16),
                pltpu.VMEM((slots, units), bf16),
                pltpu.VMEM((2 * width, width), f32),
            ],
        )
        even, other = core_swap(even, odd, n_dp)
        part2 = call(add, shape(rows, width), [parts[2], far], flops=100 * order)
        part2, part1, even, other = together(part2, parts[1], even, other)
        across, near = swap(part2, 2), swap(part1, 1)
        half, more = step // 2, 3 * SENTS // 2
        ffn_own, to_x, to_y, keep_y, keep_x = call(
            fold_halves,
            [shape(step, width)] + [shape(step + more, width)] * 2 + [shape(half, width)] * 2,
            [even, other, own_pools],
            moved=3 * even.size * 4,
        )
        from_x, from_y = swap_dp(to_x, 2, n_dp), swap_dp(to_y, 4, n_dp)
        *sent, d_hidden, hidden_low = call(
            back_hidden,
            [shape(packed_rows(rows, cols) + 16 * -(-cols // 128), 128)] * 4
            + [shape(rows, width), shape(rows, width, kind=bf16)],
            [parts[0], near, across, d_resid, normal_own, inverse_own, row(g_attn), w_all],
            flops=30 * order,
            moved=6 * rows * width * 4,
        )
        *sent, d_hidden, hidden_low, from_x, from_y, keep_x, keep_y = together(
            *sent, d_hidden, hidden_low, from_x, from_y, keep_x, keep_y
        )
        d_mixed = [sent[0]] + [swap(sent[n], n) for n in (1, 2, 3)]
        to_y = jnp.concatenate([keep_y + from_x[half:step], own_pools[:more], from_x[step:]])
        to_x = jnp.concatenate([keep_x + from_y[half:step], own_pools[more:], from_y[step:]])
        last_y, last_x = swap_dp(to_y, 4, n_dp), swap_dp(to_x, 2, n_dp)
        even, odd = call(
            out_grads,
            [shape(4, 4, piece, width)] * 2,
            [ids, *mixed_all, hidden_low],
            flops=2 * rows * width * 4 * cols,
            moved=8 * 4 * cols * width,
            scratch=[pltpu.VMEM((4, cols, width), f32)],
        )
        even, other = core_swap(even, odd, n_dp)
        d_mixed = together(*d_mixed)
        *parts, grads, bias, shared = call(
            attend_back,
            [shape(rows, width)] * 4
            + [shape(slots, 3 * cols, kind=bf16), shape(8, cols), shape(16, cols)],
            [*d_mixed, probs, q, k, v, wq, wk, wv],
            flops=10 * order,
            moved=heads * slots * slots * 2 + 2 * slots * width * 4,
            scratch=[
                pltpu.VMEM((slots, cols), bf16),
                pltpu.VMEM((3 * cols, width), bf16),
                pltpu.VMEM((slots, slots), bf16),
            ],
        )
        part3, out_even, out_other, last_x, last_y = together(parts[3], even, other, last_x, last_y)
        ffn_sum = jnp.concatenate([from_x[:half] + last_y[:half], from_y[:half] + last_x[:half]])
        ffn_sum = rest_of_dp(ffn_own + ffn_sum, n_dp)
        all_pools = [own_pools, from_x[step:], last_x[half : half + more]]
        all_pools += [last_y[half : half + more], from_y[step:]]
        all_pools += [last_y[half + more :], last_x[half + more :]]
        far = swap(part3, 1)
        out = fold_call(out_even, out_other)
        out[1:] = [swap_dp(out[n], 2 * n, n_dp) for n in (1, 2, 3)]
        even, odd = call(
            qkv_grads,
            [shape(4, 3 * piece + 8, width)] * 2,
            [ids, grads, tok_x, side, shared, bias],
            flops=6 * slots * width * cols,
            moved=8 * 3 * cols * width,
            scratch=[pltpu.VMEM((3 * cols + 64, width), f32)],
        )
        even, other = core_swap(even, odd, n_dp)
        if n_dp > 8:
            out = [rest_of_dp(sum(out), n_dp)]
        part1, part2, terms = call(
            join_terms,
            [shape(rows + piece, width), shape(rows, width), shape(4, piece, width)],
            [parts[1], parts[2], far, *out],
            flops=20 * order,
        )
        part2, part1, terms, even, other = together(part2, part1, terms, even, other)
        across, near = swap(part2, 2), swap(part1, 1)
        qkv = fold_call(even, other, [ffn_sum])
        from_x, from_y = swap_dp(qkv[1], 2, n_dp), swap_dp(qkv[2], 4, n_dp)
        own_near, own_across = call(
            join_own,
            [shape(rows + piece, width)] * 2,
            [parts[0], near, across, d_hidden, terms],
            flops=30 * order,
            moved=7 * rows * width * 4,
        )
        own_near, own_across, from_x, from_y, qkv_last = together(
            own_near, own_across, from_x, from_y, qkv[3]
        )
        across, near = swap(own_across, 2), swap(own_near, 1)
        from_d = swap_dp(qkv_last, 6, n_dp)
        across, near = together(across, near)
        across_rows = call(cut, shape(rows, width), [across], flops=20 * order)
        across_rows, near, across, from_d = together(across_rows, near, across, from_d)
        far = swap(across_rows, 1)
        low = 3 * piece + 8
        qkv_sum = rest_of_dp(qkv[0] + from_x[:low] + from_y[:low] + from_d[:low], n_dp)
        attn_own = jnp.concatenate([qkv_sum, terms[0] + near[rows:] + across[rows:]])
        attn_blocks = [attn_own] + [swap_dp(attn_own, 2 * n, n_dp) for n in (1, 2, 3)]
        mine = jnp.concatenate([ffn_sum, from_x[low:], from_y[low:], from_d[low:], *all_pools])
        wide = pool_grad.shape[1]
        d_w_up, d_w_down, pools = call(
            unpack_ffn,
            [shape(width, units), shape(units, width), shape(wide, 8 * SENTS)],
            [ids, mine, swap_dp(mine, 1, n_dp)],
            moved=16 * width * units,
            scratch=[pltpu.VMEM((3, 8 * SENTS, width), f32)],
        )
        d_tokens = call(
            place, shape(slots, width), [ids, own_near, near, across, far], moved=8 * slots * width
        )
        d_w_up, d_w_down, pools, d_tokens, *attn_blocks = together(
            d_w_up, d_w_down, pools, d_tokens, *attn_blocks
        )
        attn_blocks = with_other_core(attn_blocks, n_dp)
        pools = pools.T
        if n_dp > 8:
            third = [own_pools[n * SENTS : (n + 1) * SENTS] for n in range(3)]
            third = jnp.concatenate(third, axis=1)[:, :wide]
            pools = lax.all_gather(third, "dp", axis=0, tiled=True)
        d_w_query, d_w_key, d_w_value, d_w_out, vectors = call(
            unpack_attn,
            [shape(cols, width)] * 4 + [shape(64, width)],
            [ids, *attn_blocks],
            moved=8 * 4 * cols * width,
            scratch=[pltpu.VMEM((3 * cols, width), f32)],
        )
        b_q, b_v = vectors[4, :cols], vectors[4, cols : 2 * cols]
        d_b_out, d_g_attn, d_b_attn = vectors[8], vectors[9], vectors[10]
        d_b_up, d_b_down, d_g_ffn, d_b_ffn = vectors[3], vectors[2], vectors[1], vectors[0]
        return (
            layer_out,
            pools,
            d_tokens,
            d_w_query.T,
            d_w_key.T,
            d_w_value.T,
            b_q,
            b_v,
            d_w_out,
            d_b_out,
            d_g_attn,
            d_b_attn,
            d_w_up,
            d_b_up,
            d_w_down,
            d_b_down,
            d_g_ffn,
            d_b_ffn,
        )

    return shards


def solution(mesh):
    return jax.shard_map(
        make_shards(mesh.shape["dp"]),
        mesh=mesh,
        in_specs=(
            P("dp", None),
            P("dp", None),
            P(None, "tensor"),
            P(None, "tensor"),
            P(None, "tensor"),
            P("tensor"),
            P("tensor"),
            P("tensor", None),
            P(),
            P(),
            P(),
            P(None, "tensor"),
            P("tensor"),
            P("tensor", None),
            P(),
            P(),
            P(),
            P("dp", None),
            P("dp", None),
        ),
        out_specs=(
            P("dp", None),
            P(),
            P("dp", None),
            P(None, "tensor"),
            P(None, "tensor"),
            P(None, "tensor"),
            P("tensor"),
            P("tensor"),
            P("tensor", None),
            P(),
            P(),
            P(),
            P(None, "tensor"),
            P("tensor"),
            P("tensor", None),
            P(),
            P(),
            P(),
        ),
        check_vma=False,
    )
```

```python
import functools

import jax
import jax.numpy as jnp
from jax import lax
from jax.experimental import pallas as pl
from jax.experimental.pallas import tpu as pltpu
from jax.sharding import PartitionSpec as P

HDIM = 64
SENTS = 16
norm_eps = 1e-06
pool_eps = 1e-05
highest = lax.Precision.HIGHEST
f32 = jnp.float32
bf16 = jnp.bfloat16
order = 10**9
swaps = {k: [(i, i ^ k) for i in range(4)] for k in (1, 2, 3)}


def truncations(width):
    return [width, width * 2 // 3, width // 3, width // 6, width // 12]


def nn(left, right, precision=None):
    return lax.dot_general(
        left, right, (((1,), (0,)), ((), ())), precision=precision, preferred_element_type=f32
    )


def nt(left, right):
    return lax.dot_general(left, right, (((1,), (1,)), ((), ())), preferred_element_type=f32)


def tn(left, right):
    return lax.dot_general(left, right, (((0,), (0,)), ((), ())), preferred_element_type=f32)


def norm_stats(rows):
    centre = jnp.mean(rows, axis=-1, keepdims=True)
    shifted = rows - centre
    inverse = lax.rsqrt(jnp.mean(shifted * shifted, axis=-1, keepdims=True) + norm_eps)
    return shifted * inverse, inverse


def norm_back(grad_in, normal, inverse):
    centre = jnp.mean(grad_in, axis=-1, keepdims=True)
    along = jnp.mean(grad_in * normal, axis=-1, keepdims=True)
    return inverse * (grad_in - centre - normal * along)


def col_sum(rows):
    return jnp.sum(rows, axis=0, keepdims=True)


def shape(*extent, kind=f32):
    return jax.ShapeDtypeStruct(extent, kind)


def call(body, outs, ins, flops=0, moved=0, scratch=(), limit=32, raw=0):
    specs = [
        pl.BlockSpec(memory_space=pltpu.SMEM if item.dtype == jnp.int32 else pltpu.VMEM)
        for item in ins[: len(ins) - raw]
    ] + [pl.BlockSpec(memory_space=pltpu.HBM)] * raw
    return pl.pallas_call(
        body,
        out_shape=outs,
        in_specs=specs,
        out_specs=jax.tree.map(lambda _: pl.BlockSpec(memory_space=pltpu.VMEM), outs),
        scratch_shapes=list(scratch),
        cost_estimate=pl.CostEstimate(flops=flops, bytes_accessed=moved, transcendentals=0),
        compiler_params=pltpu.CompilerParams(vmem_limit_bytes=limit << 20),
    )(*ins)


def chunk(me, j, rows):
    return pl.ds(pl.multiple_of((me ^ j) * rows, rows), rows)


def segment_of(lengths, places):
    end = jnp.int32(0)
    found = jnp.zeros(places.shape, jnp.int32)
    for s in range(SENTS):
        end = end + lengths[0, s]
        found = found + jnp.where(places >= end, 1, 0)
    return found


def row_places(me, extent, dim, rows):
    at = lax.broadcasted_iota(jnp.int32, extent, dim)
    return ((at // rows) ^ me) * rows + at % rows


def packed_rows(rows, cols):
    return rows * (cols // 128) + (rows // 2 if cols % 128 else 0)


def pack_into(out, block):
    rows, cols = block.shape
    full = cols // 128
    for n in range(full):
        out[n * rows : (n + 1) * rows, :] = block[:, n * 128 : (n + 1) * 128]
    if cols % 128:
        half = rows // 2
        out[full * rows : full * rows + half, :HDIM] = block[:half, full * 128 :]
        out[full * rows : full * rows + half, HDIM:] = block[half:, full * 128 :]


def packed_parts(block, cols, slots, start, rows):
    full = cols // 128
    for n in range(full):
        yield n * 128, block[n * slots + start : n * slots + start + rows, :]
    if cols % 128:
        half = slots // 2
        side = start // half
        at = full * slots + start - side * half
        yield full * 128, block[at : at + rows, side * HDIM : (side + 1) * HDIM]


def attend(ids, lengths, tok, wq_in, wk_in, wv_in, bq_in, bv_in, *refs):
    tok_x, q_out, k_out, v_out, probs_out, packed, low, wq, wk, wv, bq, bv, lens, sems = refs
    me = ids[0]
    slots, cols = q_out.shape
    rows = slots // 4
    moves = [
        (lengths, lens),
        (wk_in, wk),
        *[(tok.at[chunk(me, j, rows), :], tok_x.at[j * rows : (j + 1) * rows, :]) for j in range(4)],
        (wv_in, wv),
        (bv_in, bv),
        (wq_in, wq),
        (bq_in, bq),
    ]
    moves = [pltpu.make_async_copy(a, b, sems.at[n]) for n, (a, b) in enumerate(moves)]
    for move in moves:
        move.start()
    for move in moves[:6]:
        move.wait()
    t = tok_x[...]
    k_out[...] = nt(t, wk[...]).astype(bf16)
    for move in moves[6:]:
        move.wait()
    v_out[...] = (nt(t, wv[...]) + bv[...]).astype(bf16)
    q_out[...] = (nt(t, wq[...]) + bq[...]).astype(bf16)
    seg_row = segment_of(lens, row_places(me, (1, slots), 1, rows))
    seg_col = segment_of(lens, row_places(me, (slots, 1), 0, rows))
    scale = HDIM**-0.5
    for j in range(4):
        at = slice(j * rows, (j + 1) * rows)
        allowed = seg_col[at] == seg_row
        for h in range(cols // HDIM):
            lane = slice(h * HDIM, (h + 1) * HDIM)
            s = jnp.where(allowed, nt(q_out[at, lane], k_out[:, lane]) * scale, -1000000000.0)
            e = jnp.exp(s - jnp.max(s, axis=-1, keepdims=True))
            p = (e * (1.0 / jnp.sum(e, axis=-1, keepdims=True))).astype(bf16)
            probs_out[h, at, :] = p
            low[at, lane] = nn(p, v_out[:, lane]).astype(bf16)
    pack_into(packed, low[...].astype(f32))


def join_w_out(ids, *refs):
    pieces, out, held = refs[:-2], refs[-2], refs[-1]
    step = pieces[0].shape[1]
    for d in range(len(pieces)):
        at = pl.ds(pl.multiple_of((ids[1] ^ d) * step, 8), step)
        for k in range(4):
            held[k, at, :] = pieces[d][k]
    out[...] = held[...].astype(bf16)


def gelu_grad(upper, out):
    rows = 64
    for r in range(0, upper.shape[0], rows):
        u = upper[r : r + rows, :]
        cdf = 0.5 * (1.0 + lax.erf(u * 0.7071067811865476))
        out[r : r + rows, :] = cdf + u * (0.3989422804014327 * jnp.exp(-0.5 * u * u))


def feed_chunk(j, tok_x, mixed, w_all, b_out, g_attn, b_attn, w_up, b_up, w_down, low, upper, act, part):
    rows = part.shape[0]
    at = slice(j * rows, (j + 1) * rows)
    total = tok_x[at, :].astype(f32) + b_out[...]
    for k in range(4):
        for col, block in packed_parts(mixed[k], w_all.shape[1], 4 * rows, (j ^ k) * rows, rows):
            total = total + nn(block.astype(bf16), w_all[k, col : col + block.shape[1], :])
    normal, inverse = norm_stats(total)
    normed = normal * g_attn[...] + b_attn[...]
    low[...] = normed.astype(bf16)
    upper[...] = nn(low[...], w_up[...]) + b_up[...]
    half = rows // 2
    for r in (0, half):
        u = upper[r : r + half, :]
        cdf = 0.5 * (1.0 + lax.erf(u * 0.7071067811865476))
        act[r : r + half, :] = (u * cdf).astype(bf16)
    part[...] = nn(act[...], w_down[...])
    return normed, normal, inverse


def feed_first(tok_x, m0, m1, m2, m3, w_all, b_out, g_attn, b_attn, w_up, b_up, w_down, *outs):
    part, low, upper, act = outs
    mixed = (m0, m1, m2, m3)
    ins = (tok_x, mixed, w_all, b_out, g_attn, b_attn, w_up, b_up, w_down)
    feed_chunk(3, *ins, low, upper, act, part)


def feed_rest(tok_x, m0, m1, m2, m3, w_all, b_out, g_attn, b_attn, w_up, b_up, w_down, b_down, *refs):
    (low3, upper3, act3), outs = refs[:3], refs[3:]
    p0, p1, p2, low, upper, act, normal_own, inverse_own, resid_own = outs
    parts = (p0, p1, p2)
    mixed = (m0, m1, m2, m3)
    ins = (tok_x, mixed, w_all, b_out, g_attn, b_attn, w_up, b_up, w_down)
    rows = p0.shape[0]
    for full, piece in ((low, low3), (upper, upper3), (act, act3)):
        full[3 * rows :, :] = piece[...]
    for j in (2, 1, 0):
        at = slice(j * rows, (j + 1) * rows)
        views = (low.at[at, :], upper.at[at, :], act.at[at, :], parts[j])
        normed, normal, inverse = feed_chunk(j, *ins, *views)
    normal_own[...] = normal
    inverse_own[...] = jnp.broadcast_to(inverse, inverse_own.shape)
    resid_own[...] = normed + b_down[...]


def finish_chunk(seg, normal, inverse, gain, spread, out_grad, grad_of, w_down, w_up, low, up, part):
    slot_row = lax.broadcasted_iota(jnp.int32, (1, SENTS), 1)
    belongs = jnp.where(seg == slot_row, 1.0, 0.0)
    d_final = out_grad.astype(f32) + nn(belongs, spread, highest)
    d_resid = norm_back(d_final * gain, normal, inverse)
    low[...] = d_resid.astype(bf16)
    d_upper = nt(low[...], w_down[...]) * grad_of
    up[...] = d_upper.astype(bf16)
    part[...] = nt(up[...], w_up[...])
    return d_resid, [col_sum(d_final), col_sum(d_final * normal), col_sum(d_resid), col_sum(d_upper)]


def finish_rows(block, seg, gain, shift, normal_out, inverse_out, low_out):
    normal, inverse = norm_stats(block[...])
    normal_out[...] = normal
    inverse_out[...] = jnp.broadcast_to(inverse, inverse_out.shape)
    final = normal * gain + shift
    low_out[...] = final.astype(bf16)
    slot_col = lax.broadcasted_iota(jnp.int32, (SENTS, 1), 0)
    return nn(jnp.where(slot_col == seg, 1.0, 0.0), final, highest)


def finish_early(ids, lens, r0, r1, r2, g_ffn, b_ffn, normal_ref, inverse_ref, final_low, pooled_out):
    rows, width = r0.shape
    seg_row = segment_of(lens, row_places(ids[0], (1, 4 * rows), 1, rows))
    pooled = jnp.zeros((SENTS, width), f32)
    for j, block in enumerate((r0, r1, r2)):
        at = slice(j * rows, (j + 1) * rows)
        views = (normal_ref.at[at, :], inverse_ref.at[at, :], final_low.at[at, :])
        pooled = pooled + finish_rows(block, seg_row[:, at], g_ffn[...], b_ffn[...], *views)
    pooled_out[...] = pooled


def finish_first(
    ids, lens, r3, early, pooled_in, g_ffn, b_ffn, out_grad, pool_grad, grad_of, w_down, w_up, *refs
):
    outs, (normal_ref, inverse_ref, final_low, pooled_grad) = refs[:-4], refs[-4:]
    part, layer_out, pools, spread_out, low, up, side = outs
    me = ids[0]
    rows, width = r3.shape
    gain = g_ffn[...]
    seg_row = segment_of(lens, row_places(me, (1, 4 * rows), 1, rows))
    seg_col = segment_of(lens, row_places(me, (4 * rows, 1), 0, rows))
    slot_col = lax.broadcasted_iota(jnp.int32, (SENTS, 1), 0)
    for j in range(3):
        layer_out[chunk(me, j, rows), :] = early[j * rows : (j + 1) * rows, :]
    pooled = pooled_in[...] + finish_rows(
        r3, seg_row[:, 3 * rows :], gain, b_ffn[...], normal_ref, inverse_ref, final_low
    )
    layer_out[chunk(me, 3, rows), :] = final_low[...]
    denom = jnp.zeros((SENTS, 1), f32)
    for s in range(SENTS):
        size = jnp.maximum(lens[0, s], 1).astype(f32)
        denom = denom + jnp.where(slot_col == s, size, 0.0)
    pooled = pooled / denom
    pooled_grad[...] = jnp.zeros((SENTS, width), f32)
    offset = 0
    for m in truncations(width):
        leading = pooled[:, :m]
        factor = lax.rsqrt(jnp.mean(leading * leading, axis=1, keepdims=True) + pool_eps)
        third, lane = offset // width, offset % width
        pools[third * SENTS : (third + 1) * SENTS, lane : lane + m] = leading * factor
        upstream = pool_grad[:, offset : offset + m]
        inner = jnp.mean(upstream * leading, axis=1, keepdims=True)
        pooled_grad[:, :m] += factor * upstream - leading * (factor * factor * factor * inner)
        offset += m
    rest = offset % width
    pools[2 * SENTS :, rest:] = jnp.zeros((SENTS, width - rest), f32)
    spread = pooled_grad[...] / denom
    spread_out[...] = spread
    _, sums = finish_chunk(
        seg_col[3 * rows :],
        normal_ref[...],
        inverse_ref[:, :1],
        gain,
        spread,
        out_grad[chunk(me, 3, rows), :],
        grad_of[3 * rows :, :],
        w_down,
        w_up,
        low,
        up,
        part,
    )
    for n in range(4):
        side[n : n + 1, :] = sums[n]
    side[4:, :] = jnp.zeros((4, width), f32)


def finish_rest(ids, lens, g_ffn, out_grad, grad_of, w_down, w_up, *refs):
    ins, outs, (resid_low, upper_low, held) = refs[:8], refs[8:-3], refs[-3:]
    normal_ref, inverse_ref, spread, low3, up3, side3, normed_low, act = ins
    p0, p1, p2, d_own, side, even, odd = outs
    parts = (p0, p1, p2)
    me = ids[0]
    rows, width = p0.shape
    seg_col = segment_of(lens, row_places(me, (4 * rows, 1), 0, rows))
    resid_low[3 * rows :, :] = low3[...]
    upper_low[3 * rows :, :] = up3[...]
    total = [side3[n : n + 1, :] for n in range(4)]
    for j in (2, 1, 0):
        at = slice(j * rows, (j + 1) * rows)
        d_resid, sums = finish_chunk(
            seg_col[at],
            normal_ref[at, :],
            inverse_ref[at, :1],
            g_ffn[...],
            spread[...],
            out_grad[chunk(me, j, rows), :],
            grad_of[at, :],
            w_down,
            w_up,
            resid_low.at[at, :],
            upper_low.at[at, :],
            parts[j],
        )
        total = [a + b for a, b in zip(total, sums)]
    d_own[...] = d_resid
    for n in range(4):
        side[n : n + 1, :] = total[n]
    side[4:, :] = jnp.zeros((4, width), f32)
    held[:width, :] = tn(normed_low[...], upper_low[...])
    held[width:, :] = tn(act[...], resid_low[...])
    step = even.shape[1]
    for d in range(8):
        at = pl.ds(pl.multiple_of((ids[1] ^ d) * step, 8), step)
        (odd if d & 1 else even)[d // 2] = held[at, :]


def back_hidden(own, near, across, d_resid, normal, inverse, g_attn, w_all, *outs):
    e0, e1, e2, e3, d_hidden_out, low_out = outs
    d_normed = d_resid[...] + (own[...] + near[...] + across[...])
    rows, width = d_normed.shape
    cols = w_all.shape[1]
    side = [None, col_sum(d_normed * normal[...]), col_sum(d_normed)]
    d_hidden = norm_back(d_normed * g_attn[...], normal[...], inverse[:, :1])
    side[0] = col_sum(d_hidden)
    d_hidden_out[...] = d_hidden
    low_out[...] = d_hidden.astype(bf16)
    base = packed_rows(rows, cols)
    for k, out in enumerate((e0, e1, e2, e3)):
        pack_into(out, nt(low_out[...], w_all[k]).astype(bf16).astype(f32))
        out[base:, :] = jnp.zeros((out.shape[0] - base, 128), f32)
        for v in range(3):
            for s in range(width // cols):
                for n in range(0, cols, 128):
                    r = base + (n // 128) * 16 + 4 * v + s
                    m = min(128, cols - n)
                    out[r : r + 1, :m] = side[v][:, s * cols + n : s * cols + n + m]


def out_grads(ids, m0, m1, m2, m3, hidden_low, even, odd, held):
    rows = hidden_low.shape[0]
    for k, block in enumerate((m0, m1, m2, m3)):
        for col, part in packed_parts(block, held.shape[1], 4 * rows, k * rows, rows):
            held[k, col : col + part.shape[1], :] = tn(part.astype(bf16), hidden_low[...])
    step = even.shape[2]
    for d in range(8):
        at = pl.ds(pl.multiple_of((ids[1] ^ d) * step, 8), step)
        for k in range(4):
            (odd if d & 1 else even)[d // 2, k] = held[k, at, :]


def attend_back(e0, e1, e2, e3, probs, q, k, v, wq, wk, wv, *refs):
    outs, (d_mixed, turned, d_scores) = refs[:-3], refs[-3:]
    p0, p1, p2, p3, grads, bias, shared = outs
    slots, cols = q.shape
    rows = slots // 4
    scale = HDIM**-0.5
    half = rows // 2
    for j, block in enumerate((e0, e1, e2, e3)):
        for r in (0, half):
            for col, part in packed_parts(block, cols, rows, r, half):
                at = slice(j * rows + r, j * rows + r + half)
                d_mixed[at, col : col + part.shape[1]] = part.astype(bf16)
    base = packed_rows(rows, cols)
    side = (e0[base:, :] + e1[base:, :]) + (e2[base:, :] + e3[base:, :])
    for n in range(0, cols, 128):
        m = min(128, cols - n)
        shared[:, n : n + m] = side[(n // 128) * 16 : (n // 128) * 16 + 16, :m]
    for h in range(cols // HDIM):
        lane = slice(h * HDIM, (h + 1) * HDIM)
        for j in range(4):
            at = slice(j * rows, (j + 1) * rows)
            p = probs[h, at, :].astype(f32)
            dp = nt(d_mixed[at, lane], v[:, lane])
            t = p * dp
            ds = (t - p * jnp.sum(t, axis=-1, keepdims=True)) * scale
            d_scores[at, :] = ds.astype(bf16)
        d_query = nn(d_scores[...], k[:, lane])
        bias[0:1, lane] = col_sum(d_query)
        grads[:, lane] = d_query.astype(bf16)
        d_key = tn(d_scores[...], q[:, lane])
        grads[:, cols + h * HDIM : cols + (h + 1) * HDIM] = d_key.astype(bf16)
        d_value = tn(probs[h], d_mixed[:, lane])
        bias[1:2, lane] = col_sum(d_value)
        grads[:, 2 * cols + h * HDIM : 2 * cols + (h + 1) * HDIM] = d_value.astype(bf16)
    bias[2:, :] = jnp.zeros((6, cols), f32)
    turned[:cols, :] = wq[...]
    turned[cols : 2 * cols, :] = wk[...]
    turned[2 * cols :, :] = wv[...]
    for j, out in ((3, p3), (2, p2), (1, p1), (0, p0)):
        out[...] = nn(grads[j * rows : (j + 1) * rows, :], turned[...])


def qkv_grads(ids, grads, tok_x, side, shared, bias, even, odd, held):
    width = tok_x.shape[1]
    cols = bias.shape[1]
    part = width // cols
    total = grads.shape[1]
    step = total // 8
    held[:total, :] = tn(grads[...], tok_x[...])
    held[total:, :] = jnp.zeros((64, width), f32)
    held[total : total + 4, :] = side[:4, :]

    @pl.when(ids[0] >= 0)
    def _():
        for n in range(2):
            held[total + 4 : total + 5, n * cols : (n + 1) * cols] = bias[n : n + 1, :]
        for n in range(3):
            for s in range(part):
                row = shared[4 * n + s : 4 * n + s + 1, :]
                held[total + 8 + n : total + 9 + n, s * cols : (s + 1) * cols] = row

    for d in range(8):
        c = ids[1] ^ d
        out = odd if d & 1 else even
        out[d // 2, :step, :] = held[pl.ds(pl.multiple_of(c * step, 8), step), :]
        out[d // 2, step:, :] = held[pl.ds(pl.multiple_of(total + c * 8, 8), 8), :]


def fold(mine, theirs, *refs):
    extra, outs = refs[: len(refs) - 4], refs[len(refs) - 4 :]
    rows = mine.shape[1]
    for n, out in enumerate(outs):
        out[:rows, :] = mine[n] + theirs[n]
        if n and extra:
            out[rows:, :] = extra[0][...]


def fold_halves(mine, theirs, extra, own, to_x, to_y, keep_y, keep_x):
    half = mine.shape[1] // 2
    more = extra.shape[0] // 2
    own[...] = mine[0] + theirs[0]
    for n, (out, at) in enumerate(((to_x, slice(0, half)), (to_y, slice(half, 2 * half)))):
        for m, block in enumerate((1 + n, 3)):
            out[m * half : (m + 1) * half, :] = mine[block, at, :] + theirs[block, at, :]
        out[2 * half :, :] = extra[n * more : (n + 1) * more, :]
    keep_y[...] = mine[2, :half, :] + theirs[2, :half, :]
    keep_x[...] = mine[1, half:, :] + theirs[1, half:, :]


def add(a, b, out):
    out[...] = a[...] + b[...]


def join_terms(part1, part2, far, o0, o1, o2, o3, near_out, across_out):
    rows = part1.shape[0]
    piece = o3.shape[0]
    near_out[:rows, :] = part1[...]
    near_out[rows:, :] = (o0[3 * piece :, :] + o1[3 * piece :, :]) + (o2[3 * piece :, :] + o3[...])
    across_out[...] = part2[...] + far[...]


def join_own(own, near, across, d_hidden, o0, o1, o2, o3, near_out, across_out, term):
    rows = own.shape[0]
    piece = term.shape[0]
    total = own[...] + near[:rows, :] + across[...] + d_hidden[...]
    near_out[:rows, :] = total
    across_out[:rows, :] = total
    for n, out, at in ((0, term, 0), (1, near_out, rows), (2, across_out, rows)):
        rest = slice(n * piece, (n + 1) * piece)
        sums = (o0[rest, :] + o1[rest, :]) + (o2[rest, :] + o3[rest, :])
        if n == 2:
            sums = sums + near[rows:, :]
        out[at : at + piece, :] = sums


def join_far(across, near, term, out, out_own):
    rows = out.shape[0]
    out[...] = across[:rows, :]
    out_own[...] = term[...] + near[rows:, :] + across[rows:, :]


def spread_halves(out, start, extra, half, from_x, from_y, last_y, last_x):
    more = extra.shape[0] // 2
    out[start : start + 2 * more, :] = extra[...]
    start += 2 * more
    for block, at in (
        (from_x, 2 * half),
        (last_x, half),
        (last_y, half),
        (from_y, 2 * half),
        (last_y, half + more),
        (last_x, half + more),
    ):
        out[start : start + more, :] = block[at : at + more, :]
        start += more
    return start


def collect(own, ffn_sum, from_x, from_y, last_y, last_x, out_own, pools, *refs):
    pool_moves, (qkv_sum, mine) = refs[:4], refs[4:]
    qkv_sum[own.shape[0] :, :] = out_own[...]
    half = own.shape[0] // 2
    qkv_sum[:half, :] = own[:half, :] + from_x[:half, :] + last_y[:half, :]
    qkv_sum[half : 2 * half, :] = own[half:, :] + from_y[:half, :] + last_x[:half, :]
    start = spread_halves(mine, 0, ffn_sum, half, from_x, from_y, last_y, last_x)
    spread_halves(mine, start, pools, ffn_sum.shape[0] // 2, *pool_moves)


def place(me, r0, r1, r2, r3, out):
    rows = out.shape[0] // 4
    for j, block in enumerate((r0, r1, r2, r3)):
        out[chunk(me[0], j, rows), :] = block[:rows, :]


def unpack_ffn(ids, mine, theirs, up_out, down_out, pools_out, held):
    half = up_out.shape[0]
    step = 2 * half // 8
    wide = pools_out.shape[0]
    width = up_out.shape[1]
    for d in range(8):
        block = theirs if d & 1 else mine
        start = (d // 2) * step
        c = ids[1] ^ d
        at = pl.ds(pl.multiple_of((c % 4) * step, 8), step)

        @pl.when(c < 4)
        def _(block=block, at=at, start=start):
            up_out[at, :] = block[start : start + step, :]

        @pl.when(c >= 4)
        def _(block=block, at=at, start=start):
            down_out[at, :] = block[start : start + step, :]

        to = pl.ds(pl.multiple_of(c * SENTS, 8), SENTS)
        start = 4 * step + (d // 2) * 3 * SENTS
        for n in range(3):
            held[n, to, :] = block[start + n * SENTS : start + (n + 1) * SENTS, :]
    for n in range(3):
        m = min(width, wide - n * width)
        pools_out[n * width : n * width + m, :] = held[n].T[:m, :]


def unpack_attn(ids, *refs):
    blocks, outs, (held, side) = refs[:8], refs[8:-2], refs[-2:]
    q_out, k_out, v_out, o_out, *vectors = outs
    cols = o_out.shape[0]
    step = 3 * cols // 8
    small = cols // 8
    for d, block in enumerate(blocks):
        c = ids[1] ^ d
        held[pl.ds(pl.multiple_of(c * step, 8), step), :] = block[:step, :]
        side[pl.ds(pl.multiple_of(c * 8, 8), 8), :] = block[step : step + 8, :]
        o_out[pl.ds(pl.multiple_of(c * small, 8), small), :] = block[step + 8 :, :]
    q_out[...] = held[:cols, :]
    k_out[...] = held[cols : 2 * cols, :]
    v_out[...] = held[2 * cols :, :]
    vectors[0][...] = side[4, :cols]
    vectors[1][...] = side[4, cols : 2 * cols]
    for n, r in enumerate((8, 9, 10, 3, 2, 1, 0)):
        vectors[2 + n][...] = side[r, :]


def swap(block, k):
    return lax.ppermute(block, "tensor", swaps[k])


def swap_dp(block, k, n_dp):
    return lax.ppermute(block, "dp", [(i, i ^ k) for i in range(n_dp)])


def together(*items):
    return lax.optimization_barrier(items)


def rest_of_dp(block, n_dp):
    if n_dp == 8:
        return block
    groups = [[i + 8 * j for j in range(n_dp // 8)] for i in range(8)]
    return lax.psum(block, "dp", axis_index_groups=groups)


def core_swap(even, odd, n_dp):
    other = swap_dp(odd, 1, n_dp)
    flat = even.shape[-2] if even.ndim == 3 else even.shape[1] * even.shape[2]
    return even.reshape(4, flat, even.shape[-1]), other.reshape(4, flat, even.shape[-1])


def halves_start(even, other, extra):
    _, rows, width = even.shape
    half, more = rows // 2, extra.shape[0] // 2
    return call(
        fold_halves,
        [shape(rows, width)] + [shape(rows + more, width)] * 2 + [shape(half, width)] * 2,
        [even, other, extra],
        moved=3 * even.size * 4,
    )


def halves_next(keep_y, keep_x, extra, from_x, from_y):
    half, more = keep_y.shape[0], extra.shape[0] // 2
    to_y = [keep_y + from_x[half : 2 * half], extra[:more], from_x[2 * half :]]
    to_x = [keep_x + from_y[half : 2 * half], extra[more:], from_y[2 * half :]]
    return jnp.concatenate(to_y), jnp.concatenate(to_x)


def halves_end(own, from_x, from_y, last_y, last_x):
    half = own.shape[0] // 2
    terms = [from_x[:half] + last_y[:half], from_y[:half] + last_x[:half]]
    return own + jnp.concatenate(terms)


def with_other_core(blocks, n_dp):
    others = [swap_dp(item, 1, n_dp) for item in blocks]
    return [item for pair in zip(blocks, others) for item in pair]


def make_shards(n_dp):
    def shards(
        tokens,
        lengths,
        w_query,
        w_key,
        w_value,
        b_query,
        b_value,
        w_out,
        b_out,
        g_attn,
        b_attn,
        w_up,
        b_up,
        w_down,
        b_down,
        g_ffn,
        b_ffn,
        out_grad,
        pool_grad,
    ):
        me = lax.axis_index("tensor").astype(jnp.int32)
        group = (lax.axis_index("dp") % 8).astype(jnp.int32)
        ids = jnp.stack([me, group])
        slots, width = tokens.shape
        cols = w_query.shape[1]
        units = w_up.shape[1]
        heads = cols // HDIM
        rows = slots // 4
        row = lambda vector: vector.reshape(1, -1)
        wq, wk, wv = w_query.T, w_key.T, w_value.T

        piece = cols // 8
        slice_own = lax.dynamic_slice_in_dim(w_out, group * piece, piece, 0).astype(f32)
        slices = [slice_own] + [swap(slice_own, n) for n in (1, 2, 3)]

        tok_x, q, k, v, probs, mixed = call(
            attend,
            [
                shape(slots, width, kind=bf16),
                shape(slots, cols, kind=bf16),
                shape(slots, cols, kind=bf16),
                shape(slots, cols, kind=bf16),
                shape(heads, slots, slots, kind=bf16),
                shape(packed_rows(slots, cols), 128),
            ],
            [ids]
            + [
                pltpu.with_memory_space_constraint(item, pltpu.HBM)
                for item in (lengths, tokens, wq, wk, wv, row(b_query), row(b_value))
            ],
            flops=2 * slots * width * 3 * cols + 4 * slots * slots * cols,
            moved=slots * width * 4 + 3 * cols * width * 2 + heads * slots * slots * 2,
            scratch=[pltpu.VMEM((slots, cols), bf16)]
            + [pltpu.VMEM((cols, width), bf16)] * 3
            + [pltpu.VMEM((1, cols), f32)] * 2
            + [pltpu.SMEM((1, SENTS), jnp.int32), pltpu.SemaphoreType.DMA((10,))],
            raw=7,
        )
        mixed, *slices = together(mixed, *slices)
        slices = jnp.stack(slices)
        across, near = swap(mixed, 2), swap(mixed, 1)
        w_blocks = [swap_dp(slices, 2 * n, n_dp) for n in (1, 2, 3)]
        across, near, slices, *w_blocks = together(across, near, slices, *w_blocks)
        mixed_all = [mixed, near, across, swap(across, 1)]
        w_all = call(
            join_w_out,
            shape(4, cols, width, kind=bf16),
            [ids] + with_other_core([slices] + w_blocks, n_dp),
            moved=4 * cols * width * 6,
            scratch=[pltpu.VMEM((4, cols, width), f32)],
        )
        feed_ins = [tok_x, *mixed_all, w_all, row(b_out), row(g_attn), row(b_attn)]
        feed_ins += [w_up, row(b_up), w_down]
        part3, low3, upper3, act3 = call(
            feed_first,
            [
                shape(rows, width),
                shape(rows, width, kind=bf16),
                shape(rows, units),
                shape(rows, units, kind=bf16),
            ],
            feed_ins,
            flops=2 * rows * width * (width + 2 * units),
            moved=rows * width * 4 + 3 * width * units * 2,
        )
        far = swap(part3, 1)
        *parts, normed_low, upper, act, normal_own, inverse_own, resid_own = call(
            feed_rest,
            [shape(rows, width)] * 3
            + [
                shape(slots, width, kind=bf16),
                shape(slots, units),
                shape(slots, units, kind=bf16),
                shape(rows, width),
                shape(rows, 128),
                shape(rows, width),
            ],
            feed_ins + [row(b_down), low3, upper3, act3],
            flops=6 * rows * width * (width + 2 * units),
            moved=3 * slots * width * 4 + 3 * width * units * 2,
        )
        slope = call(
            gelu_grad, shape(slots, units), [upper], moved=8 * slots * units, flops=slots * units
        )
        far, slope, part2, part1 = together(far, slope, parts[2], parts[1])
        across, near = swap(part2 + far, 2), swap(part1, 1)
        own = resid_own + parts[0] + near + across
        across, near = swap(own, 2), swap(own, 1)
        across, near = together(across, near)
        resid = [own, near, across, swap(across, 1)]
        normal, inverse, early, pooled = call(
            finish_early,
            [shape(3 * rows, width), shape(3 * rows, 128)]
            + [shape(3 * rows, width, kind=bf16), shape(SENTS, width)],
            [ids, lengths, *resid[:3], row(g_ffn), row(b_ffn)],
            flops=slots * width * 100,
            moved=3 * slots * width * 4,
        )
        part3, layer_out, own_pools, spread, low3, up3, side3 = call(
            finish_first,
            [
                shape(rows, width),
                shape(slots, width, kind=bf16),
                shape(3 * SENTS, width),
                shape(SENTS, width),
                shape(rows, width, kind=bf16),
                shape(rows, units, kind=bf16),
                shape(8, width),
            ],
            [ids, lengths, resid[3], early, pooled, row(g_ffn), row(b_ffn), out_grad, pool_grad]
            + [slope, w_down, w_up],
            flops=4 * rows * width * units,
            moved=6 * slots * width * 4,
            scratch=[
                pltpu.VMEM((rows, width), f32),
                pltpu.VMEM((rows, 128), f32),
                pltpu.VMEM((rows, width), bf16),
                pltpu.VMEM((SENTS, width), f32),
            ],
        )
        far = swap(part3, 1)
        step = 2 * width // 8
        *parts, d_resid, side, even, odd = call(
            finish_rest,
            [shape(rows, width)] * 4 + [shape(8, width)] + [shape(4, step, width)] * 2,
            [ids, lengths, row(g_ffn), out_grad, slope, w_down, w_up]
            + [normal, inverse, spread, low3, up3, side3, normed_low, act],
            flops=8 * slots * width * units,
            moved=6 * slots * width * 4 + 8 * width * units,
            scratch=[
                pltpu.VMEM((slots, width), bf16),
                pltpu.VMEM((slots, units), bf16),
                pltpu.VMEM((2 * width, width), f32),
            ],
        )
        even, other = core_swap(even, odd, n_dp)
        part2 = call(add, shape(rows, width), [parts[2], far], flops=100 * order)
        part2, part1, even, other = together(part2, parts[1], even, other)
        across, near = swap(part2, 2), swap(part1, 1)
        ffn_own, to_x, to_y, keep_y, keep_x = halves_start(even, other, own_pools)
        from_x, from_y = swap_dp(to_x, 2, n_dp), swap_dp(to_y, 4, n_dp)
        *sent, d_hidden, hidden_low = call(
            back_hidden,
            [shape(packed_rows(rows, cols) + 16 * -(-cols // 128), 128)] * 4
            + [shape(rows, width), shape(rows, width, kind=bf16)],
            [parts[0], near, across, d_resid, normal_own, inverse_own, row(g_attn), w_all],
            flops=30 * order,
            moved=6 * rows * width * 4,
        )
        *sent, d_hidden, hidden_low, from_x, from_y, keep_x, keep_y = together(
            *sent, d_hidden, hidden_low, from_x, from_y, keep_x, keep_y
        )
        d_mixed = [sent[0]] + [swap(sent[n], n) for n in (1, 2, 3)]
        to_y, to_x = halves_next(keep_y, keep_x, own_pools, from_x, from_y)
        last_y, last_x = swap_dp(to_y, 4, n_dp), swap_dp(to_x, 2, n_dp)
        even, odd = call(
            out_grads,
            [shape(4, 4, piece, width)] * 2,
            [ids, *mixed_all, hidden_low],
            flops=2 * rows * width * 4 * cols,
            moved=8 * 4 * cols * width,
            scratch=[pltpu.VMEM((4, cols, width), f32)],
        )
        even, other = core_swap(even, odd, n_dp)
        d_mixed = together(*d_mixed)
        *parts, grads, bias, shared = call(
            attend_back,
            [shape(rows, width)] * 4
            + [shape(slots, 3 * cols, kind=bf16), shape(8, cols), shape(16, cols)],
            [*d_mixed, probs, q, k, v, wq, wk, wv],
            flops=10 * order,
            moved=heads * slots * slots * 2 + 2 * slots * width * 4,
            scratch=[
                pltpu.VMEM((slots, cols), bf16),
                pltpu.VMEM((3 * cols, width), bf16),
                pltpu.VMEM((slots, slots), bf16),
            ],
        )
        part3, out_even, out_other, last_x, last_y = together(parts[3], even, other, last_x, last_y)
        far = swap(part3, 1)
        ffn_sum = rest_of_dp(halves_end(ffn_own, from_x, from_y, last_y, last_x), n_dp)
        pool_moves = [from_x, from_y, last_y, last_x]
        out = call(
            fold,
            [shape(4 * piece, width)] * 4,
            [out_even, out_other],
            moved=3 * out_even.size * 4,
        )
        out_x, out_y = swap_dp(out[1], 2, n_dp), swap_dp(out[2], 4, n_dp)
        even, odd = call(
            qkv_grads,
            [shape(4, 3 * piece + 8, width)] * 2,
            [ids, grads, tok_x, side, shared, bias],
            flops=6 * slots * width * cols,
            moved=8 * 3 * cols * width,
            scratch=[pltpu.VMEM((3 * cols + 64, width), f32)],
        )
        even, other = core_swap(even, odd, n_dp)
        out_d = swap_dp(out[3][3 * piece :], 6, n_dp)
        pieces = [out[0], out_x, out_y, out_d]
        if n_dp > 8:
            pieces[3] = rest_of_dp(sum(item[-piece:] for item in pieces), n_dp)
            pieces[:3] = [jnp.zeros_like(item) for item in pieces[:3]]
        part1, part2 = call(
            join_terms,
            [shape(rows + piece, width), shape(rows, width)],
            [parts[1], parts[2], far, *pieces],
            flops=20 * order,
        )
        part2, part1, even, other, out_x, out_y, out_d = together(
            part2, part1, even, other, out_x, out_y, out[3][: 3 * piece]
        )
        across, near = swap(part2, 2), swap(part1, 1)
        out_d = swap_dp(out_d, 6, n_dp)
        qkv_own, to_x, to_y, keep_y, keep_x = halves_start(even, other, ffn_sum)
        from_x, from_y = swap_dp(to_x, 2, n_dp), swap_dp(to_y, 4, n_dp)
        pieces = [out[0], out_x, out_y, out_d]
        if n_dp > 8:
            pieces[0] = rest_of_dp(sum(item[: 3 * piece] for item in pieces), n_dp)
            pieces[1:] = [jnp.zeros_like(pieces[0])] * 3
        own_near, own_across, term = call(
            join_own,
            [shape(rows + piece, width)] * 2 + [shape(piece, width)],
            [parts[0], near, across, d_hidden, *pieces],
            flops=30 * order,
            moved=7 * rows * width * 4,
        )
        own_near, own_across, from_x, from_y, keep_x, keep_y = together(
            own_near, own_across, from_x, from_y, keep_x, keep_y
        )
        across, near = swap(own_across, 2), swap(own_near, 1)
        to_y, to_x = halves_next(keep_y, keep_x, ffn_sum, from_x, from_y)
        last_y, last_x = swap_dp(to_y, 4, n_dp), swap_dp(to_x, 2, n_dp)
        far, out_own = call(
            join_far,
            [shape(rows, width), shape(piece, width)],
            [across, near, term],
            flops=30 * order,
        )
        far, near, across, out_own, last_y, last_x = together(
            far, near, across, out_own, last_y, last_x
        )
        far = swap(far, 1)
        attn_own, mine = call(
            collect,
            [shape(4 * piece + 8, width), shape(4 * (step + 3 * SENTS), width)],
            [qkv_own, ffn_sum, from_x, from_y, last_y, last_x, out_own]
            + [own_pools, *pool_moves],
            flops=1 * order,
            moved=8 * 4 * step * width,
        )
        if n_dp > 8:
            low = 3 * piece + 8
            attn_own = jnp.concatenate([rest_of_dp(attn_own[:low], n_dp), attn_own[low:]])
        attn_blocks = [attn_own] + [swap_dp(attn_own, 2 * n, n_dp) for n in (1, 2, 3)]
        wide = pool_grad.shape[1]
        d_w_up, d_w_down, pools = call(
            unpack_ffn,
            [shape(width, units), shape(units, width), shape(wide, 8 * SENTS)],
            [ids, mine, swap_dp(mine, 1, n_dp)],
            moved=16 * width * units,
            scratch=[pltpu.VMEM((3, 8 * SENTS, width), f32)],
        )
        d_tokens = call(
            place, shape(slots, width), [ids, own_near, near, across, far], flops=30 * order
        )
        d_w_up, d_w_down, pools, d_tokens, *attn_blocks = together(
            d_w_up, d_w_down, pools, d_tokens, *attn_blocks
        )
        d_w_query, d_w_key, d_w_value, d_w_out, *vectors = call(
            unpack_attn,
            [shape(cols, width)] * 4 + [shape(cols)] * 2 + [shape(width)] * 7,
            [ids, *with_other_core(attn_blocks, n_dp)],
            moved=8 * 4 * cols * width,
            scratch=[pltpu.VMEM((3 * cols, width), f32), pltpu.VMEM((64, width), f32)],
        )
        b_q, b_v, d_b_out, d_g_attn, d_b_attn, d_b_up, d_b_down, d_g_ffn, d_b_ffn = vectors
        pools = pools.T
        if n_dp > 8:
            third = [own_pools[n * SENTS : (n + 1) * SENTS] for n in range(3)]
            third = jnp.concatenate(third, axis=1)[:, :wide]
            pools = lax.all_gather(third, "dp", axis=0, tiled=True)
        return (
            layer_out,
            pools,
            d_tokens,
            d_w_query.T,
            d_w_key.T,
            d_w_value.T,
            b_q,
            b_v,
            d_w_out,
            d_b_out,
            d_g_attn,
            d_b_attn,
            d_w_up,
            d_b_up,
            d_w_down,
            d_b_down,
            d_g_ffn,
            d_b_ffn,
        )

    return shards


def solution(mesh):
    return jax.shard_map(
        make_shards(mesh.shape["dp"]),
        mesh=mesh,
        in_specs=(
            P("dp", None),
            P("dp", None),
            P(None, "tensor"),
            P(None, "tensor"),
            P(None, "tensor"),
            P("tensor"),
            P("tensor"),
            P("tensor", None),
            P(),
            P(),
            P(),
            P(None, "tensor"),
            P("tensor"),
            P("tensor", None),
            P(),
            P(),
            P(),
            P("dp", None),
            P("dp", None),
        ),
        out_specs=(
            P("dp", None),
            P(),
            P("dp", None),
            P(None, "tensor"),
            P(None, "tensor"),
            P(None, "tensor"),
            P("tensor"),
            P("tensor"),
            P("tensor", None),
            P(),
            P(),
            P(),
            P(None, "tensor"),
            P("tensor"),
            P("tensor", None),
            P(),
            P(),
            P(),
        ),
        check_vma=False,
    )
```

```python
import functools

import jax
import jax.numpy as jnp
from jax import lax
from jax.experimental import pallas as pl
from jax.experimental.pallas import tpu as pltpu
from jax.sharding import PartitionSpec as P

HDIM = 64
SENTS = 16
norm_eps = 1e-06
pool_eps = 1e-05
highest = lax.Precision.HIGHEST
f32 = jnp.float32
bf16 = jnp.bfloat16
order = 10**9
swaps = {k: [(i, i ^ k) for i in range(4)] for k in (1, 2, 3)}


def truncations(width):
    return [width, width * 2 // 3, width // 3, width // 6, width // 12]


def nn(left, right, precision=None):
    return lax.dot_general(
        left, right, (((1,), (0,)), ((), ())), precision=precision, preferred_element_type=f32
    )


def nt(left, right):
    return lax.dot_general(left, right, (((1,), (1,)), ((), ())), preferred_element_type=f32)


def tn(left, right):
    return lax.dot_general(left, right, (((0,), (0,)), ((), ())), preferred_element_type=f32)


def norm_stats(rows):
    centre = jnp.mean(rows, axis=-1, keepdims=True)
    shifted = rows - centre
    inverse = lax.rsqrt(jnp.mean(shifted * shifted, axis=-1, keepdims=True) + norm_eps)
    return shifted * inverse, inverse


def norm_back(grad_in, normal, inverse):
    centre = jnp.mean(grad_in, axis=-1, keepdims=True)
    along = jnp.mean(grad_in * normal, axis=-1, keepdims=True)
    return inverse * (grad_in - centre - normal * along)


def col_sum(rows):
    return jnp.sum(rows, axis=0, keepdims=True)


def shape(*extent, kind=f32):
    return jax.ShapeDtypeStruct(extent, kind)


def call(body, outs, ins, flops=0, moved=0, scratch=(), limit=32, raw=0):
    specs = [
        pl.BlockSpec(memory_space=pltpu.SMEM if item.dtype == jnp.int32 else pltpu.VMEM)
        for item in ins[: len(ins) - raw]
    ] + [pl.BlockSpec(memory_space=pltpu.HBM)] * raw
    return pl.pallas_call(
        body,
        out_shape=outs,
        in_specs=specs,
        out_specs=jax.tree.map(lambda _: pl.BlockSpec(memory_space=pltpu.VMEM), outs),
        scratch_shapes=list(scratch),
        cost_estimate=pl.CostEstimate(flops=flops, bytes_accessed=moved, transcendentals=0),
        compiler_params=pltpu.CompilerParams(vmem_limit_bytes=limit << 20),
    )(*ins)


def chunk(me, j, rows):
    return pl.ds(pl.multiple_of((me ^ j) * rows, rows), rows)


def segment_of(lengths, places):
    end = jnp.int32(0)
    found = jnp.zeros(places.shape, jnp.int32)
    for s in range(SENTS):
        end = end + lengths[0, s]
        found = found + jnp.where(places >= end, 1, 0)
    return found


def row_places(me, extent, dim, rows):
    at = lax.broadcasted_iota(jnp.int32, extent, dim)
    return ((at // rows) ^ me) * rows + at % rows


def packed_rows(rows, cols):
    return rows * (cols // 128) + (rows // 2 if cols % 128 else 0)


def pack_into(out, block):
    rows, cols = block.shape
    full = cols // 128
    for n in range(full):
        out[n * rows : (n + 1) * rows, :] = block[:, n * 128 : (n + 1) * 128]
    if cols % 128:
        half = rows // 2
        out[full * rows : full * rows + half, :HDIM] = block[:half, full * 128 :]
        out[full * rows : full * rows + half, HDIM:] = block[half:, full * 128 :]


def packed_parts(block, cols, slots, start, rows):
    full = cols // 128
    for n in range(full):
        yield n * 128, block[n * slots + start : n * slots + start + rows, :]
    if cols % 128:
        half = slots // 2
        side = start // half
        at = full * slots + start - side * half
        yield full * 128, block[at : at + rows, side * HDIM : (side + 1) * HDIM]


def attend(ids, lengths, tok, wq_in, wk_in, wv_in, bq_in, bv_in, *refs):
    tok_x, q_out, k_out, v_out, probs_out, packed, low, wq, wk, wv, bq, bv, lens, sems = refs
    me = ids[0]
    slots, cols = q_out.shape
    rows = slots // 4
    moves = [
        (lengths, lens),
        (wk_in, wk),
        *[(tok.at[chunk(me, j, rows), :], tok_x.at[j * rows : (j + 1) * rows, :]) for j in range(4)],
        (wv_in, wv),
        (bv_in, bv),
        (wq_in, wq),
        (bq_in, bq),
    ]
    moves = [pltpu.make_async_copy(a, b, sems.at[n]) for n, (a, b) in enumerate(moves)]
    for move in moves:
        move.start()
    for move in moves[:6]:
        move.wait()
    t = tok_x[...]
    k_out[...] = nt(t, wk[...]).astype(bf16)
    for move in moves[6:]:
        move.wait()
    v_out[...] = (nt(t, wv[...]) + bv[...]).astype(bf16)
    q_out[...] = (nt(t, wq[...]) + bq[...]).astype(bf16)
    seg_row = segment_of(lens, row_places(me, (1, slots), 1, rows))
    seg_col = segment_of(lens, row_places(me, (slots, 1), 0, rows))
    scale = HDIM**-0.5
    tall = slots
    for r in range(0, slots, tall):
        at = slice(r, r + tall)
        allowed = seg_col[at] == seg_row
        for h in range(cols // HDIM):
            lane = slice(h * HDIM, (h + 1) * HDIM)
            s = jnp.where(allowed, nt(q_out[at, lane], k_out[:, lane]) * scale, -1000000000.0)
            e = jnp.exp(s - jnp.max(s, axis=-1, keepdims=True))
            p = (e * (1.0 / jnp.sum(e, axis=-1, keepdims=True))).astype(bf16)
            probs_out[h, at, :] = p
            low[at, lane] = nn(p, v_out[:, lane]).astype(bf16)
    pack_into(packed, low[...].astype(f32))


def join_w_out(ids, *refs):
    pieces, out, held = refs[:-2], refs[-2], refs[-1]
    step = pieces[0].shape[1]
    for d in range(len(pieces)):
        at = pl.ds(pl.multiple_of((ids[1] ^ d) * step, 8), step)
        for k in range(4):
            held[k, at, :] = pieces[d][k]
    out[...] = held[...].astype(bf16)


def gelu_grad(upper, out):
    rows = 64
    for r in range(0, upper.shape[0], rows):
        u = upper[r : r + rows, :]
        cdf = 0.5 * (1.0 + lax.erf(u * 0.7071067811865476))
        out[r : r + rows, :] = cdf + u * (0.3989422804014327 * jnp.exp(-0.5 * u * u))


def feed_chunk(j, tok_x, mixed, w_all, b_out, g_attn, b_attn, w_up, b_up, w_down, low, upper, act, part):
    rows = part.shape[0]
    at = slice(j * rows, (j + 1) * rows)
    total = tok_x[at, :].astype(f32) + b_out[...]
    for k in range(4):
        for col, block in packed_parts(mixed[k], w_all.shape[1], 4 * rows, (j ^ k) * rows, rows):
            total = total + nn(block.astype(bf16), w_all[k, col : col + block.shape[1], :])
    normal, inverse = norm_stats(total)
    normed = normal * g_attn[...] + b_attn[...]
    low[...] = normed.astype(bf16)
    upper[...] = nn(low[...], w_up[...]) + b_up[...]
    half = rows // 2
    for r in (0, half):
        u = upper[r : r + half, :]
        cdf = 0.5 * (1.0 + lax.erf(u * 0.7071067811865476))
        act[r : r + half, :] = (u * cdf).astype(bf16)
    part[...] = nn(act[...], w_down[...])
    return normed, normal, inverse


def feed_first(tok_x, m0, m1, m2, m3, w_all, b_out, g_attn, b_attn, w_up, b_up, w_down, *outs):
    part, low, upper, act = outs
    mixed = (m0, m1, m2, m3)
    ins = (tok_x, mixed, w_all, b_out, g_attn, b_attn, w_up, b_up, w_down)
    feed_chunk(3, *ins, low, upper, act, part)


def feed_rest(tok_x, m0, m1, m2, m3, w_all, b_out, g_attn, b_attn, w_up, b_up, w_down, b_down, *refs):
    (low3, upper3, act3), outs = refs[:3], refs[3:]
    p0, p1, p2, low, upper, act, normal_own, inverse_own, resid_own = outs
    parts = (p0, p1, p2)
    mixed = (m0, m1, m2, m3)
    ins = (tok_x, mixed, w_all, b_out, g_attn, b_attn, w_up, b_up, w_down)
    rows = p0.shape[0]
    for full, piece in ((low, low3), (upper, upper3), (act, act3)):
        full[3 * rows :, :] = piece[...]
    for j in (2, 1, 0):
        at = slice(j * rows, (j + 1) * rows)
        views = (low.at[at, :], upper.at[at, :], act.at[at, :], parts[j])
        normed, normal, inverse = feed_chunk(j, *ins, *views)
    normal_own[...] = normal
    inverse_own[...] = jnp.broadcast_to(inverse, inverse_own.shape)
    resid_own[...] = normed + b_down[...]


def finish_chunk(seg, normal, inverse, gain, spread, out_grad, grad_of, w_down, w_up, low, up, part):
    slot_row = lax.broadcasted_iota(jnp.int32, (1, SENTS), 1)
    belongs = jnp.where(seg == slot_row, 1.0, 0.0)
    d_final = out_grad.astype(f32) + nn(belongs, spread, highest)
    d_resid = norm_back(d_final * gain, normal, inverse)
    low[...] = d_resid.astype(bf16)
    d_upper = nt(low[...], w_down[...]) * grad_of
    up[...] = d_upper.astype(bf16)
    part[...] = nt(up[...], w_up[...])
    return d_resid, [col_sum(d_final), col_sum(d_final * normal), col_sum(d_resid), col_sum(d_upper)]


def finish_rows(block, seg, gain, shift, normal_out, inverse_out, low_out):
    normal, inverse = norm_stats(block[...])
    normal_out[...] = normal
    inverse_out[...] = jnp.broadcast_to(inverse, inverse_out.shape)
    final = normal * gain + shift
    low_out[...] = final.astype(bf16)
    slot_col = lax.broadcasted_iota(jnp.int32, (SENTS, 1), 0)
    return nn(jnp.where(slot_col == seg, 1.0, 0.0), final, highest)


def finish_early(ids, lens, r0, r1, r2, g_ffn, b_ffn, normal_ref, inverse_ref, final_low, pooled_out):
    rows, width = r0.shape
    seg_row = segment_of(lens, row_places(ids[0], (1, 4 * rows), 1, rows))
    pooled = jnp.zeros((SENTS, width), f32)
    for j, block in enumerate((r0, r1, r2)):
        at = slice(j * rows, (j + 1) * rows)
        views = (normal_ref.at[at, :], inverse_ref.at[at, :], final_low.at[at, :])
        pooled = pooled + finish_rows(block, seg_row[:, at], g_ffn[...], b_ffn[...], *views)
    pooled_out[...] = pooled


def finish_first(
    ids, lens, r3, early, pooled_in, g_ffn, b_ffn, out_grad, pool_grad, grad_of, w_down, w_up, *refs
):
    outs, (normal_ref, inverse_ref, final_low, pooled_grad) = refs[:-4], refs[-4:]
    part, layer_out, pools, spread_out, low, up, side = outs
    me = ids[0]
    rows, width = r3.shape
    gain = g_ffn[...]
    seg_row = segment_of(lens, row_places(me, (1, 4 * rows), 1, rows))
    seg_col = segment_of(lens, row_places(me, (4 * rows, 1), 0, rows))
    slot_col = lax.broadcasted_iota(jnp.int32, (SENTS, 1), 0)
    for j in range(3):
        layer_out[chunk(me, j, rows), :] = early[j * rows : (j + 1) * rows, :]
    pooled = pooled_in[...] + finish_rows(
        r3, seg_row[:, 3 * rows :], gain, b_ffn[...], normal_ref, inverse_ref, final_low
    )
    layer_out[chunk(me, 3, rows), :] = final_low[...]
    denom = jnp.zeros((SENTS, 1), f32)
    for s in range(SENTS):
        size = jnp.maximum(lens[0, s], 1).astype(f32)
        denom = denom + jnp.where(slot_col == s, size, 0.0)
    pooled = pooled / denom
    pooled_grad[...] = jnp.zeros((SENTS, width), f32)
    offset = 0
    for m in truncations(width):
        leading = pooled[:, :m]
        factor = lax.rsqrt(jnp.mean(leading * leading, axis=1, keepdims=True) + pool_eps)
        third, lane = offset // width, offset % width
        pools[third * SENTS : (third + 1) * SENTS, lane : lane + m] = leading * factor
        upstream = pool_grad[:, offset : offset + m]
        inner = jnp.mean(upstream * leading, axis=1, keepdims=True)
        pooled_grad[:, :m] += factor * upstream - leading * (factor * factor * factor * inner)
        offset += m
    rest = offset % width
    pools[2 * SENTS :, rest:] = jnp.zeros((SENTS, width - rest), f32)
    spread = pooled_grad[...] / denom
    spread_out[...] = spread
    _, sums = finish_chunk(
        seg_col[3 * rows :],
        normal_ref[...],
        inverse_ref[:, :1],
        gain,
        spread,
        out_grad[chunk(me, 3, rows), :],
        grad_of[3 * rows :, :],
        w_down,
        w_up,
        low,
        up,
        part,
    )
    for n in range(4):
        side[n : n + 1, :] = sums[n]
    side[4:, :] = jnp.zeros((4, width), f32)


def finish_rest(ids, lens, g_ffn, out_grad, grad_of, w_down, w_up, *refs):
    ins, outs, (resid_low, upper_low, held) = refs[:8], refs[8:-3], refs[-3:]
    normal_ref, inverse_ref, spread, low3, up3, side3, normed_low, act = ins
    p0, p1, p2, d_own, side, even, odd = outs
    parts = (p0, p1, p2)
    me = ids[0]
    rows, width = p0.shape
    seg_col = segment_of(lens, row_places(me, (4 * rows, 1), 0, rows))
    resid_low[3 * rows :, :] = low3[...]
    upper_low[3 * rows :, :] = up3[...]
    total = [side3[n : n + 1, :] for n in range(4)]
    for j in (2, 1, 0):
        at = slice(j * rows, (j + 1) * rows)
        d_resid, sums = finish_chunk(
            seg_col[at],
            normal_ref[at, :],
            inverse_ref[at, :1],
            g_ffn[...],
            spread[...],
            out_grad[chunk(me, j, rows), :],
            grad_of[at, :],
            w_down,
            w_up,
            resid_low.at[at, :],
            upper_low.at[at, :],
            parts[j],
        )
        total = [a + b for a, b in zip(total, sums)]
    d_own[...] = d_resid
    for n in range(4):
        side[n : n + 1, :] = total[n]
    side[4:, :] = jnp.zeros((4, width), f32)
    held[:width, :] = tn(normed_low[...], upper_low[...])
    held[width:, :] = tn(act[...], resid_low[...])
    step = even.shape[1]
    for d in range(8):
        at = pl.ds(pl.multiple_of((ids[1] ^ d) * step, 8), step)
        (odd if d & 1 else even)[d // 2] = held[at, :]


def back_hidden(own, near, across, d_resid, normal, inverse, g_attn, w_all, *outs):
    e0, e1, e2, e3, d_hidden_out, low_out = outs
    d_normed = d_resid[...] + (own[...] + near[...] + across[...])
    rows, width = d_normed.shape
    cols = w_all.shape[1]
    side = [None, col_sum(d_normed * normal[...]), col_sum(d_normed)]
    d_hidden = norm_back(d_normed * g_attn[...], normal[...], inverse[:, :1])
    side[0] = col_sum(d_hidden)
    d_hidden_out[...] = d_hidden
    low_out[...] = d_hidden.astype(bf16)
    base = packed_rows(rows, cols)
    for k, out in enumerate((e0, e1, e2, e3)):
        pack_into(out, nt(low_out[...], w_all[k]).astype(bf16).astype(f32))
        out[base:, :] = jnp.zeros((out.shape[0] - base, 128), f32)
        for v in range(3):
            for s in range(width // cols):
                for n in range(0, cols, 128):
                    r = base + (n // 128) * 16 + 4 * v + s
                    m = min(128, cols - n)
                    out[r : r + 1, :m] = side[v][:, s * cols + n : s * cols + n + m]


def out_grads(ids, m0, m1, m2, m3, hidden_low, even, odd, held):
    rows = hidden_low.shape[0]
    for k, block in enumerate((m0, m1, m2, m3)):
        for col, part in packed_parts(block, held.shape[1], 4 * rows, k * rows, rows):
            held[k, col : col + part.shape[1], :] = tn(part.astype(bf16), hidden_low[...])
    step = even.shape[2]
    for d in range(8):
        at = pl.ds(pl.multiple_of((ids[1] ^ d) * step, 8), step)
        for k in range(4):
            (odd if d & 1 else even)[d // 2, k] = held[k, at, :]


def attend_back(e0, e1, e2, e3, probs, q, k, v, wq, wk, wv, *refs):
    outs, (d_mixed, turned, d_scores) = refs[:-3], refs[-3:]
    p0, p1, p2, p3, grads, bias, shared = outs
    slots, cols = q.shape
    rows = slots // 4
    scale = HDIM**-0.5
    half = rows // 2
    for j, block in enumerate((e0, e1, e2, e3)):
        for r in (0, half):
            for col, part in packed_parts(block, cols, rows, r, half):
                at = slice(j * rows + r, j * rows + r + half)
                d_mixed[at, col : col + part.shape[1]] = part.astype(bf16)
    base = packed_rows(rows, cols)
    side = (e0[base:, :] + e1[base:, :]) + (e2[base:, :] + e3[base:, :])
    for n in range(0, cols, 128):
        m = min(128, cols - n)
        shared[:, n : n + m] = side[(n // 128) * 16 : (n // 128) * 16 + 16, :m]
    for h in range(cols // HDIM):
        lane = slice(h * HDIM, (h + 1) * HDIM)
        for j in range(4):
            at = slice(j * rows, (j + 1) * rows)
            p = probs[h, at, :].astype(f32)
            dp = nt(d_mixed[at, lane], v[:, lane])
            t = p * dp
            ds = (t - p * jnp.sum(t, axis=-1, keepdims=True)) * scale
            d_scores[at, :] = ds.astype(bf16)
        d_query = nn(d_scores[...], k[:, lane])
        bias[0:1, lane] = col_sum(d_query)
        grads[:, lane] = d_query.astype(bf16)
        d_key = tn(d_scores[...], q[:, lane])
        grads[:, cols + h * HDIM : cols + (h + 1) * HDIM] = d_key.astype(bf16)
        d_value = tn(probs[h], d_mixed[:, lane])
        bias[1:2, lane] = col_sum(d_value)
        grads[:, 2 * cols + h * HDIM : 2 * cols + (h + 1) * HDIM] = d_value.astype(bf16)
    bias[2:, :] = jnp.zeros((6, cols), f32)
    turned[:cols, :] = wq[...]
    turned[cols : 2 * cols, :] = wk[...]
    turned[2 * cols :, :] = wv[...]
    for j, out in ((3, p3), (2, p2), (1, p1), (0, p0)):
        out[...] = nn(grads[j * rows : (j + 1) * rows, :], turned[...])


def qkv_grads(ids, grads, tok_x, side, shared, bias, even, odd, held):
    width = tok_x.shape[1]
    cols = bias.shape[1]
    part = width // cols
    total = grads.shape[1]
    step = total // 8
    held[:total, :] = tn(grads[...], tok_x[...])
    held[total:, :] = jnp.zeros((64, width), f32)
    held[total : total + 4, :] = side[:4, :]

    @pl.when(ids[0] >= 0)
    def _():
        for n in range(2):
            held[total + 4 : total + 5, n * cols : (n + 1) * cols] = bias[n : n + 1, :]
        for n in range(3):
            for s in range(part):
                row = shared[4 * n + s : 4 * n + s + 1, :]
                held[total + 8 + n : total + 9 + n, s * cols : (s + 1) * cols] = row

    for d in range(8):
        c = ids[1] ^ d
        out = odd if d & 1 else even
        out[d // 2, :step, :] = held[pl.ds(pl.multiple_of(c * step, 8), step), :]
        out[d // 2, step:, :] = held[pl.ds(pl.multiple_of(total + c * 8, 8), 8), :]


def fold(mine, theirs, *refs):
    extra, outs = refs[: len(refs) - 4], refs[len(refs) - 4 :]
    rows = mine.shape[1]
    for n, out in enumerate(outs):
        out[:rows, :] = mine[n] + theirs[n]
        if n and extra:
            out[rows:, :] = extra[0][...]


def fold_halves(mine, theirs, *refs):
    extra, (own, to_x, to_y, keep_y, keep_x) = refs[:-5], refs[-5:]
    half = mine.shape[1] // 2
    own[...] = mine[0] + theirs[0]
    for n, (out, at) in enumerate(((to_x, slice(0, half)), (to_y, slice(half, 2 * half)))):
        for m, block in enumerate((1 + n, 3)):
            out[m * half : (m + 1) * half, :] = mine[block, at, :] + theirs[block, at, :]
        if extra:
            more = extra[0].shape[0] // 2
            out[2 * half :, :] = extra[0][n * more : (n + 1) * more, :]
    keep_y[...] = mine[2, :half, :] + theirs[2, :half, :]
    keep_x[...] = mine[1, half:, :] + theirs[1, half:, :]


def add(a, b, out):
    out[...] = a[...] + b[...]


def join_terms(part1, part2, far, o0, o1, o2, o3, near_out, across_out):
    rows = part1.shape[0]
    piece = o3.shape[0]
    near_out[:rows, :] = part1[...]
    near_out[rows:, :] = (o0[3 * piece :, :] + o1[3 * piece :, :]) + (o2[3 * piece :, :] + o3[...])
    across_out[...] = part2[...] + far[...]


def join_own(own, near, across, d_hidden, o0, o1, o2, o3, near_out, across_out, term):
    rows = own.shape[0]
    piece = term.shape[0]
    total = own[...] + near[:rows, :] + across[...] + d_hidden[...]
    near_out[:rows, :] = total
    across_out[:rows, :] = total
    for n, out, at in ((0, term, 0), (1, near_out, rows), (2, across_out, rows)):
        rest = slice(n * piece, (n + 1) * piece)
        sums = (o0[rest, :] + o1[rest, :]) + (o2[rest, :] + o3[rest, :])
        if n == 2:
            sums = sums + near[rows:, :]
        out[at : at + piece, :] = sums


def join_far(across, near, term, out, out_own):
    rows = out.shape[0]
    out[...] = across[:rows, :]
    out_own[...] = term[...] + near[rows:, :] + across[rows:, :]


def collect(own, extra, from_x, from_y, last_y, last_x, out_own, sums, mine):
    half = own.shape[0] // 2
    sums[:half, :] = own[:half, :] + from_x[:half, :] + last_y[:half, :]
    sums[half : 2 * half, :] = own[half:, :] + from_y[:half, :] + last_x[:half, :]
    sums[2 * half :, :] = out_own[...]
    travel = extra.shape[0] // 2
    more = 3 * SENTS // 2
    part = travel - more
    for n, (block, at) in enumerate(
        (
            (extra, 0),
            (extra, travel),
            (from_x, 2 * half),
            (last_x, half),
            (last_y, half),
            (from_y, 2 * half),
            (last_y, half + travel),
            (last_x, half + travel),
        )
    ):
        mine[n * part : (n + 1) * part, :] = block[at : at + part, :]
        to = 8 * part + n * more
        mine[to : to + more, :] = block[at + part : at + travel, :]


def place(me, r0, r1, r2, r3, out):
    rows = out.shape[0] // 4
    for j, block in enumerate((r0, r1, r2, r3)):
        out[chunk(me[0], j, rows), :] = block[:rows, :]


def unpack_ffn(ids, mine, theirs, up_out, down_out, pools_out, held):
    half = up_out.shape[0]
    step = 2 * half // 8
    wide = pools_out.shape[0]
    width = up_out.shape[1]
    for d in range(8):
        block = theirs if d & 1 else mine
        start = (d // 2) * step
        c = ids[1] ^ d
        at = pl.ds(pl.multiple_of((c % 4) * step, 8), step)

        @pl.when(c < 4)
        def _(block=block, at=at, start=start):
            up_out[at, :] = block[start : start + step, :]

        @pl.when(c >= 4)
        def _(block=block, at=at, start=start):
            down_out[at, :] = block[start : start + step, :]

        to = pl.ds(pl.multiple_of(c * SENTS, 8), SENTS)
        start = 4 * step + (d // 2) * 3 * SENTS
        for n in range(3):
            held[n, to, :] = block[start + n * SENTS : start + (n + 1) * SENTS, :]
    for n in range(3):
        m = min(width, wide - n * width)
        pools_out[n * width : n * width + m, :] = held[n].T[:m, :]


def unpack_attn(ids, *refs):
    blocks, outs, (held, side) = refs[:8], refs[8:-2], refs[-2:]
    q_out, k_out, v_out, o_out, *vectors = outs
    cols = o_out.shape[0]
    step = 3 * cols // 8
    small = cols // 8
    for d, block in enumerate(blocks):
        c = ids[1] ^ d
        held[pl.ds(pl.multiple_of(c * step, 8), step), :] = block[:step, :]
        side[pl.ds(pl.multiple_of(c * 8, 8), 8), :] = block[step : step + 8, :]
        o_out[pl.ds(pl.multiple_of(c * small, 8), small), :] = block[step + 8 :, :]
    q_out[...] = held[:cols, :]
    k_out[...] = held[cols : 2 * cols, :]
    v_out[...] = held[2 * cols :, :]
    vectors[0][...] = side[4, :cols]
    vectors[1][...] = side[4, cols : 2 * cols]
    for n, r in enumerate((8, 9, 10, 3, 2, 1, 0)):
        vectors[2 + n][...] = side[r, :]


def swap(block, k):
    return lax.ppermute(block, "tensor", swaps[k])


def swap_dp(block, k, n_dp):
    return lax.ppermute(block, "dp", [(i, i ^ k) for i in range(n_dp)])


def together(*items):
    return lax.optimization_barrier(items)


def rest_of_dp(block, n_dp):
    if n_dp == 8:
        return block
    groups = [[i + 8 * j for j in range(n_dp // 8)] for i in range(8)]
    return lax.psum(block, "dp", axis_index_groups=groups)


def core_swap(even, odd, n_dp):
    other = swap_dp(odd, 1, n_dp)
    flat = even.shape[-2] if even.ndim == 3 else even.shape[1] * even.shape[2]
    return even.reshape(4, flat, even.shape[-1]), other.reshape(4, flat, even.shape[-1])


def halves_start(even, other, *extra):
    _, rows, width = even.shape
    half, more = rows // 2, sum(item.shape[0] // 2 for item in extra)
    return call(
        fold_halves,
        [shape(rows, width)] + [shape(rows + more, width)] * 2 + [shape(half, width)] * 2,
        [even, other, *extra],
        moved=3 * even.size * 4,
    )


def with_other_core(blocks, n_dp):
    others = [swap_dp(item, 1, n_dp) for item in blocks]
    return [item for pair in zip(blocks, others) for item in pair]


def make_shards(n_dp):
    def shards(
        tokens,
        lengths,
        w_query,
        w_key,
        w_value,
        b_query,
        b_value,
        w_out,
        b_out,
        g_attn,
        b_attn,
        w_up,
        b_up,
        w_down,
        b_down,
        g_ffn,
        b_ffn,
        out_grad,
        pool_grad,
    ):
        me = lax.axis_index("tensor").astype(jnp.int32)
        group = (lax.axis_index("dp") % 8).astype(jnp.int32)
        ids = jnp.stack([me, group])
        slots, width = tokens.shape
        cols = w_query.shape[1]
        units = w_up.shape[1]
        heads = cols // HDIM
        rows = slots // 4
        row = lambda vector: vector.reshape(1, -1)
        wq, wk, wv = w_query.T, w_key.T, w_value.T

        piece = cols // 8
        slice_own = lax.dynamic_slice_in_dim(w_out, group * piece, piece, 0).astype(f32)
        slices = [slice_own] + [swap(slice_own, n) for n in (1, 2, 3)]

        tok_x, q, k, v, probs, mixed = call(
            attend,
            [
                shape(slots, width, kind=bf16),
                shape(slots, cols, kind=bf16),
                shape(slots, cols, kind=bf16),
                shape(slots, cols, kind=bf16),
                shape(heads, slots, slots, kind=bf16),
                shape(packed_rows(slots, cols), 128),
            ],
            [ids]
            + [
                pltpu.with_memory_space_constraint(item, pltpu.HBM)
                for item in (lengths, tokens, wq, wk, wv, row(b_query), row(b_value))
            ],
            flops=2 * slots * width * 3 * cols + 4 * slots * slots * cols,
            moved=slots * width * 4 + 3 * cols * width * 2 + heads * slots * slots * 2,
            scratch=[pltpu.VMEM((slots, cols), bf16)]
            + [pltpu.VMEM((cols, width), bf16)] * 3
            + [pltpu.VMEM((1, cols), f32)] * 2
            + [pltpu.SMEM((1, SENTS), jnp.int32), pltpu.SemaphoreType.DMA((10,))],
            raw=7,
        )
        mixed, *slices = together(mixed, *slices)
        slices = jnp.stack(slices)
        across, near = swap(mixed, 2), swap(mixed, 1)
        w_blocks = [swap_dp(slices, 2 * n, n_dp) for n in (1, 2, 3)]
        across, near, slices, *w_blocks = together(across, near, slices, *w_blocks)
        mixed_all = [mixed, near, across, swap(across, 1)]
        w_all = call(
            join_w_out,
            shape(4, cols, width, kind=bf16),
            [ids] + with_other_core([slices] + w_blocks, n_dp),
            moved=4 * cols * width * 6,
            scratch=[pltpu.VMEM((4, cols, width), f32)],
        )
        feed_ins = [tok_x, *mixed_all, w_all, row(b_out), row(g_attn), row(b_attn)]
        feed_ins += [w_up, row(b_up), w_down]
        part3, low3, upper3, act3 = call(
            feed_first,
            [
                shape(rows, width),
                shape(rows, width, kind=bf16),
                shape(rows, units),
                shape(rows, units, kind=bf16),
            ],
            feed_ins,
            flops=2 * rows * width * (width + 2 * units),
            moved=rows * width * 4 + 3 * width * units * 2,
        )
        far = swap(part3, 1)
        *parts, normed_low, upper, act, normal_own, inverse_own, resid_own = call(
            feed_rest,
            [shape(rows, width)] * 3
            + [
                shape(slots, width, kind=bf16),
                shape(slots, units),
                shape(slots, units, kind=bf16),
                shape(rows, width),
                shape(rows, 128),
                shape(rows, width),
            ],
            feed_ins + [row(b_down), low3, upper3, act3],
            flops=6 * rows * width * (width + 2 * units),
            moved=3 * slots * width * 4 + 3 * width * units * 2,
        )
        slope = call(
            gelu_grad, shape(slots, units), [upper], moved=8 * slots * units, flops=slots * units
        )
        far, slope, part2, part1 = together(far, slope, parts[2], parts[1])
        across, near = swap(part2 + far, 2), swap(part1, 1)
        own = resid_own + parts[0] + near + across
        across, near = swap(own, 2), swap(own, 1)
        across, near = together(across, near)
        resid = [own, near, across, swap(across, 1)]
        normal, inverse, early, pooled = call(
            finish_early,
            [shape(3 * rows, width), shape(3 * rows, 128)]
            + [shape(3 * rows, width, kind=bf16), shape(SENTS, width)],
            [ids, lengths, *resid[:3], row(g_ffn), row(b_ffn)],
            flops=slots * width * 100,
            moved=3 * slots * width * 4,
        )
        part3, layer_out, own_pools, spread, low3, up3, side3 = call(
            finish_first,
            [
                shape(rows, width),
                shape(slots, width, kind=bf16),
                shape(3 * SENTS, width),
                shape(SENTS, width),
                shape(rows, width, kind=bf16),
                shape(rows, units, kind=bf16),
                shape(8, width),
            ],
            [ids, lengths, resid[3], early, pooled, row(g_ffn), row(b_ffn), out_grad, pool_grad]
            + [slope, w_down, w_up],
            flops=4 * rows * width * units,
            moved=6 * slots * width * 4,
            scratch=[
                pltpu.VMEM((rows, width), f32),
                pltpu.VMEM((rows, 128), f32),
                pltpu.VMEM((rows, width), bf16),
                pltpu.VMEM((SENTS, width), f32),
            ],
        )
        far = swap(part3, 1)
        step = 2 * width // 8
        *parts, d_resid, side, even, odd = call(
            finish_rest,
            [shape(rows, width)] * 4 + [shape(8, width)] + [shape(4, step, width)] * 2,
            [ids, lengths, row(g_ffn), out_grad, slope, w_down, w_up]
            + [normal, inverse, spread, low3, up3, side3, normed_low, act],
            flops=8 * slots * width * units,
            moved=6 * slots * width * 4 + 8 * width * units,
            scratch=[
                pltpu.VMEM((slots, width), bf16),
                pltpu.VMEM((slots, units), bf16),
                pltpu.VMEM((2 * width, width), f32),
            ],
        )
        even, other = core_swap(even, odd, n_dp)
        part2 = call(add, shape(rows, width), [parts[2], far], flops=100 * order)
        part2, part1, even, other = together(part2, parts[1], even, other)
        across, near = swap(part2, 2), swap(part1, 1)
        ffn_own, to_x, to_y, keep_y, keep_x = halves_start(even, other)
        from_x, from_y = swap_dp(to_x, 2, n_dp), swap_dp(to_y, 4, n_dp)
        *sent, d_hidden, hidden_low = call(
            back_hidden,
            [shape(packed_rows(rows, cols) + 16 * -(-cols // 128), 128)] * 4
            + [shape(rows, width), shape(rows, width, kind=bf16)],
            [parts[0], near, across, d_resid, normal_own, inverse_own, row(g_attn), w_all],
            flops=30 * order,
            moved=6 * rows * width * 4,
        )
        *sent, d_hidden, hidden_low, from_x, from_y, keep_x, keep_y = together(
            *sent, d_hidden, hidden_low, from_x, from_y, keep_x, keep_y
        )
        d_mixed = [sent[0]] + [swap(sent[n], n) for n in (1, 2, 3)]
        half = step // 2
        to_y, to_x = keep_y + from_x[half:], keep_x + from_y[half:]
        last_y, last_x = swap_dp(to_y, 4, n_dp), swap_dp(to_x, 2, n_dp)
        even, odd = call(
            out_grads,
            [shape(4, 4, piece, width)] * 2,
            [ids, *mixed_all, hidden_low],
            flops=2 * rows * width * 4 * cols,
            moved=8 * 4 * cols * width,
            scratch=[pltpu.VMEM((4, cols, width), f32)],
        )
        even, other = core_swap(even, odd, n_dp)
        d_mixed = together(*d_mixed)
        *parts, grads, bias, shared = call(
            attend_back,
            [shape(rows, width)] * 4
            + [shape(slots, 3 * cols, kind=bf16), shape(8, cols), shape(16, cols)],
            [*d_mixed, probs, q, k, v, wq, wk, wv],
            flops=10 * order,
            moved=heads * slots * slots * 2 + 2 * slots * width * 4,
            scratch=[
                pltpu.VMEM((slots, cols), bf16),
                pltpu.VMEM((3 * cols, width), bf16),
                pltpu.VMEM((slots, slots), bf16),
            ],
        )
        part3, out_even, out_other, last_x, last_y = together(parts[3], even, other, last_x, last_y)
        far = swap(part3, 1)
        ffn_sum = [ffn_own[:half] + from_x[:half] + last_y, ffn_own[half:] + from_y[:half] + last_x]
        if n_dp > 8:
            ffn_sum = [rest_of_dp(item, n_dp) for item in ffn_sum]
        more = 3 * SENTS // 2
        extra = [ffn_sum[0], own_pools[:more], ffn_sum[1], own_pools[more:]]
        extra = jnp.concatenate(extra)
        out = call(
            fold,
            [shape(4 * piece, width)] * 4,
            [out_even, out_other],
            moved=3 * out_even.size * 4,
        )
        out_x, out_y = swap_dp(out[1], 2, n_dp), swap_dp(out[2], 4, n_dp)
        even, odd = call(
            qkv_grads,
            [shape(4, 3 * piece + 8, width)] * 2,
            [ids, grads, tok_x, side, shared, bias],
            flops=6 * slots * width * cols,
            moved=8 * 3 * cols * width,
            scratch=[pltpu.VMEM((3 * cols + 64, width), f32)],
        )
        even, other = core_swap(even, odd, n_dp)
        out_d = swap_dp(out[3][3 * piece :], 6, n_dp)
        pieces = [out[0], out_x, out_y, out_d]
        if n_dp > 8:
            pieces[3] = rest_of_dp(sum(item[-piece:] for item in pieces), n_dp)
            pieces[:3] = [jnp.zeros_like(item) for item in pieces[:3]]
        part1, part2 = call(
            join_terms,
            [shape(rows + piece, width), shape(rows, width)],
            [parts[1], parts[2], far, *pieces],
            flops=20 * order,
        )
        part2, part1, even, other, out_x, out_y, out_d = together(
            part2, part1, even, other, out_x, out_y, out[3][: 3 * piece]
        )
        across, near = swap(part2, 2), swap(part1, 1)
        out_d = swap_dp(out_d, 6, n_dp)
        qkv_own, to_x, to_y, keep_y, keep_x = halves_start(even, other, extra)
        from_x, from_y = swap_dp(to_x, 2, n_dp), swap_dp(to_y, 4, n_dp)
        pieces = [out[0], out_x, out_y, out_d]
        if n_dp > 8:
            pieces[0] = rest_of_dp(sum(item[: 3 * piece] for item in pieces), n_dp)
            pieces[1:] = [jnp.zeros_like(pieces[0])] * 3
        own_near, own_across, term = call(
            join_own,
            [shape(rows + piece, width)] * 2 + [shape(piece, width)],
            [parts[0], near, across, d_hidden, *pieces],
            flops=30 * order,
            moved=7 * rows * width * 4,
        )
        own_near, own_across, from_x, from_y, keep_x, keep_y = together(
            own_near, own_across, from_x, from_y, keep_x, keep_y
        )
        across, near = swap(own_across, 2), swap(own_near, 1)
        low, travel = keep_y.shape[0], half + more
        to_y = [keep_y + from_x[low : 2 * low], extra[:travel], from_x[2 * low :]]
        to_x = [keep_x + from_y[low : 2 * low], extra[travel:], from_y[2 * low :]]
        to_y, to_x = jnp.concatenate(to_y), jnp.concatenate(to_x)
        last_y, last_x = swap_dp(to_y, 4, n_dp), swap_dp(to_x, 2, n_dp)
        far, out_own = call(
            join_far,
            [shape(rows, width), shape(piece, width)],
            [across, near, term],
            flops=30 * order,
        )
        far, near, across, out_own, last_y, last_x = together(
            far, near, across, out_own, last_y, last_x
        )
        far = swap(far, 1)
        attn_own, mine = call(
            collect,
            [shape(4 * piece + 8, width), shape(4 * (step + 3 * SENTS), width)],
            [qkv_own, extra, from_x, from_y, last_y, last_x, out_own],
            flops=1 * order,
            moved=8 * 4 * step * width,
        )
        if n_dp > 8:
            low = 3 * piece + 8
            attn_own = jnp.concatenate([rest_of_dp(attn_own[:low], n_dp), attn_own[low:]])
        attn_blocks = [attn_own] + [swap_dp(attn_own, 2 * n, n_dp) for n in (1, 2, 3)]
        wide = pool_grad.shape[1]
        d_w_up, d_w_down, pools = call(
            unpack_ffn,
            [shape(width, units), shape(units, width), shape(wide, 8 * SENTS)],
            [ids, mine, swap_dp(mine, 1, n_dp)],
            moved=16 * width * units,
            scratch=[pltpu.VMEM((3, 8 * SENTS, width), f32)],
        )
        d_tokens = call(
            place, shape(slots, width), [ids, own_near, near, across, far], flops=30 * order
        )
        d_w_up, d_w_down, pools, d_tokens, *attn_blocks = together(
            d_w_up, d_w_down, pools, d_tokens, *attn_blocks
        )
        d_w_query, d_w_key, d_w_value, d_w_out, *vectors = call(
            unpack_attn,
            [shape(cols, width)] * 4 + [shape(cols)] * 2 + [shape(width)] * 7,
            [ids, *with_other_core(attn_blocks, n_dp)],
            moved=8 * 4 * cols * width,
            scratch=[pltpu.VMEM((3 * cols, width), f32), pltpu.VMEM((64, width), f32)],
        )
        b_q, b_v, d_b_out, d_g_attn, d_b_attn, d_b_up, d_b_down, d_g_ffn, d_b_ffn = vectors
        pools = pools.T
        if n_dp > 8:
            third = [own_pools[n * SENTS : (n + 1) * SENTS] for n in range(3)]
            third = jnp.concatenate(third, axis=1)[:, :wide]
            pools = lax.all_gather(third, "dp", axis=0, tiled=True)
        return (
            layer_out,
            pools,
            d_tokens,
            d_w_query.T,
            d_w_key.T,
            d_w_value.T,
            b_q,
            b_v,
            d_w_out,
            d_b_out,
            d_g_attn,
            d_b_attn,
            d_w_up,
            d_b_up,
            d_w_down,
            d_b_down,
            d_g_ffn,
            d_b_ffn,
        )

    return shards


def solution(mesh):
    return jax.shard_map(
        make_shards(mesh.shape["dp"]),
        mesh=mesh,
        in_specs=(
            P("dp", None),
            P("dp", None),
            P(None, "tensor"),
            P(None, "tensor"),
            P(None, "tensor"),
            P("tensor"),
            P("tensor"),
            P("tensor", None),
            P(),
            P(),
            P(),
            P(None, "tensor"),
            P("tensor"),
            P("tensor", None),
            P(),
            P(),
            P(),
            P("dp", None),
            P("dp", None),
        ),
        out_specs=(
            P("dp", None),
            P(),
            P("dp", None),
            P(None, "tensor"),
            P(None, "tensor"),
            P(None, "tensor"),
            P("tensor"),
            P("tensor"),
            P("tensor", None),
            P(),
            P(),
            P(),
            P(None, "tensor"),
            P("tensor"),
            P("tensor", None),
            P(),
            P(),
            P(),
        ),
        check_vma=False,
    )
```

```python
import functools

import jax
import jax.numpy as jnp
from jax import lax
from jax.experimental import pallas as pl
from jax.experimental.pallas import tpu as pltpu
from jax.sharding import PartitionSpec as P

HDIM = 64
SENTS = 16
norm_eps = 1e-06
pool_eps = 1e-05
highest = lax.Precision.HIGHEST
f32 = jnp.float32
bf16 = jnp.bfloat16
order = 10**9
swaps = {k: [(i, i ^ k) for i in range(4)] for k in (1, 2, 3)}


def truncations(width):
    return [width, width * 2 // 3, width // 3, width // 6, width // 12]


def nn(left, right, precision=None):
    return lax.dot_general(
        left, right, (((1,), (0,)), ((), ())), precision=precision, preferred_element_type=f32
    )


def nt(left, right):
    return lax.dot_general(left, right, (((1,), (1,)), ((), ())), preferred_element_type=f32)


def tn(left, right):
    return lax.dot_general(left, right, (((0,), (0,)), ((), ())), preferred_element_type=f32)


def norm_stats(rows):
    centre = jnp.mean(rows, axis=-1, keepdims=True)
    shifted = rows - centre
    inverse = lax.rsqrt(jnp.mean(shifted * shifted, axis=-1, keepdims=True) + norm_eps)
    return shifted * inverse, inverse


def norm_back(grad_in, normal, inverse):
    centre = jnp.mean(grad_in, axis=-1, keepdims=True)
    along = jnp.mean(grad_in * normal, axis=-1, keepdims=True)
    return inverse * (grad_in - centre - normal * along)


def col_sum(rows):
    return jnp.sum(rows, axis=0, keepdims=True)


def shape(*extent, kind=f32):
    return jax.ShapeDtypeStruct(extent, kind)


def call(body, outs, ins, flops=0, moved=0, scratch=(), limit=32, raw=0):
    specs = [
        pl.BlockSpec(memory_space=pltpu.SMEM if item.dtype == jnp.int32 else pltpu.VMEM)
        for item in ins[: len(ins) - raw]
    ] + [pl.BlockSpec(memory_space=pltpu.HBM)] * raw
    return pl.pallas_call(
        body,
        out_shape=outs,
        in_specs=specs,
        out_specs=jax.tree.map(lambda _: pl.BlockSpec(memory_space=pltpu.VMEM), outs),
        scratch_shapes=list(scratch),
        cost_estimate=pl.CostEstimate(flops=flops, bytes_accessed=moved, transcendentals=0),
        compiler_params=pltpu.CompilerParams(vmem_limit_bytes=limit << 20),
    )(*ins)


def chunk(me, j, rows):
    return pl.ds(pl.multiple_of((me ^ j) * rows, rows), rows)


def segment_of(lengths, places):
    end = jnp.int32(0)
    found = jnp.zeros(places.shape, jnp.int32)
    for s in range(SENTS):
        end = end + lengths[0, s]
        found = found + jnp.where(places >= end, 1, 0)
    return found


def row_places(me, extent, dim, rows):
    at = lax.broadcasted_iota(jnp.int32, extent, dim)
    return ((at // rows) ^ me) * rows + at % rows


def packed_rows(rows, cols):
    return rows * (cols // 128) + (rows // 2 if cols % 128 else 0)


def pack_into(out, block):
    rows, cols = block.shape
    full = cols // 128
    for n in range(full):
        out[n * rows : (n + 1) * rows, :] = block[:, n * 128 : (n + 1) * 128]
    if cols % 128:
        half = rows // 2
        out[full * rows : full * rows + half, :HDIM] = block[:half, full * 128 :]
        out[full * rows : full * rows + half, HDIM:] = block[half:, full * 128 :]


def packed_parts(block, cols, slots, start, rows):
    full = cols // 128
    for n in range(full):
        yield n * 128, block[n * slots + start : n * slots + start + rows, :]
    if cols % 128:
        half = slots // 2
        side = start // half
        at = full * slots + start - side * half
        yield full * 128, block[at : at + rows, side * HDIM : (side + 1) * HDIM]


def attend(ids, lengths, tok, wq_in, wk_in, wv_in, bq_in, bv_in, *refs):
    tok_x, q_out, k_out, v_out, probs_out, packed, low, wq, wk, wv, bq, bv, lens, sems = refs
    me = ids[0]
    slots, cols = q_out.shape
    rows = slots // 4
    moves = [
        (lengths, lens),
        (wk_in, wk),
        *[(tok.at[chunk(me, j, rows), :], tok_x.at[j * rows : (j + 1) * rows, :]) for j in range(4)],
        (wv_in, wv),
        (bv_in, bv),
        (wq_in, wq),
        (bq_in, bq),
    ]
    moves = [pltpu.make_async_copy(a, b, sems.at[n]) for n, (a, b) in enumerate(moves)]
    for move in moves:
        move.start()
    for move in moves[:6]:
        move.wait()
    t = tok_x[...]
    k_out[...] = nt(t, wk[...]).astype(bf16)
    for move in moves[6:]:
        move.wait()
    v_out[...] = (nt(t, wv[...]) + bv[...]).astype(bf16)
    q_out[...] = (nt(t, wq[...]) + bq[...]).astype(bf16)
    seg_row = segment_of(lens, row_places(me, (1, slots), 1, rows))
    seg_col = segment_of(lens, row_places(me, (slots, 1), 0, rows))
    scale = HDIM**-0.5
    tall = slots
    for r in range(0, slots, tall):
        at = slice(r, r + tall)
        allowed = seg_col[at] == seg_row
        for h in range(cols // HDIM):
            lane = slice(h * HDIM, (h + 1) * HDIM)
            s = jnp.where(allowed, nt(q_out[at, lane], k_out[:, lane]) * scale, -1000000000.0)
            e = jnp.exp(s - jnp.max(s, axis=-1, keepdims=True))
            p = (e * (1.0 / jnp.sum(e, axis=-1, keepdims=True))).astype(bf16)
            probs_out[h, at, :] = p
            low[at, lane] = nn(p, v_out[:, lane]).astype(bf16)
    pack_into(packed, low[...].astype(f32))


def join_w_out(ids, *refs):
    pieces, out, held = refs[:-2], refs[-2], refs[-1]
    step = pieces[0].shape[1]
    for d in range(len(pieces)):
        at = pl.ds(pl.multiple_of((ids[1] ^ d) * step, 8), step)
        for k in range(4):
            held[k, at, :] = pieces[d][k]
    out[...] = held[...].astype(bf16)


def gelu_grad(upper, out):
    rows = 64
    for r in range(0, upper.shape[0], rows):
        u = upper[r : r + rows, :]
        cdf = 0.5 * (1.0 + lax.erf(u * 0.7071067811865476))
        out[r : r + rows, :] = cdf + u * (0.3989422804014327 * jnp.exp(-0.5 * u * u))


def feed_chunk(j, tok_x, mixed, w_all, b_out, g_attn, b_attn, w_up, b_up, w_down, low, upper, act, part):
    rows = part.shape[0]
    at = slice(j * rows, (j + 1) * rows)
    total = tok_x[at, :].astype(f32) + b_out[...]
    for k in range(4):
        for col, block in packed_parts(mixed[k], w_all.shape[1], 4 * rows, (j ^ k) * rows, rows):
            total = total + nn(block.astype(bf16), w_all[k, col : col + block.shape[1], :])
    normal, inverse = norm_stats(total)
    normed = normal * g_attn[...] + b_attn[...]
    low[...] = normed.astype(bf16)
    upper[...] = nn(low[...], w_up[...]) + b_up[...]
    half = rows // 2
    for r in (0, half):
        u = upper[r : r + half, :]
        cdf = 0.5 * (1.0 + lax.erf(u * 0.7071067811865476))
        act[r : r + half, :] = (u * cdf).astype(bf16)
    part[...] = nn(act[...], w_down[...])
    return normed, normal, inverse


def feed_first(tok_x, m0, m1, m2, m3, w_all, b_out, g_attn, b_attn, w_up, b_up, w_down, *outs):
    part, low, upper, act = outs
    mixed = (m0, m1, m2, m3)
    ins = (tok_x, mixed, w_all, b_out, g_attn, b_attn, w_up, b_up, w_down)
    feed_chunk(3, *ins, low, upper, act, part)


def feed_rest(tok_x, m0, m1, m2, m3, w_all, b_out, g_attn, b_attn, w_up, b_up, w_down, b_down, *refs):
    (low3, upper3, act3), outs = refs[:3], refs[3:]
    p0, p1, p2, low, upper, act, normal_own, inverse_own, resid_own = outs
    parts = (p0, p1, p2)
    mixed = (m0, m1, m2, m3)
    ins = (tok_x, mixed, w_all, b_out, g_attn, b_attn, w_up, b_up, w_down)
    rows = p0.shape[0]
    for full, piece in ((low, low3), (upper, upper3), (act, act3)):
        full[3 * rows :, :] = piece[...]
    for j in (2, 1, 0):
        at = slice(j * rows, (j + 1) * rows)
        views = (low.at[at, :], upper.at[at, :], act.at[at, :], parts[j])
        normed, normal, inverse = feed_chunk(j, *ins, *views)
    normal_own[...] = normal
    inverse_own[...] = jnp.broadcast_to(inverse, inverse_own.shape)
    resid_own[...] = normed + b_down[...]


def finish_chunk(seg, normal, inverse, gain, spread, out_grad, grad_of, w_down, w_up, low, up):
    slot_row = lax.broadcasted_iota(jnp.int32, (1, SENTS), 1)
    belongs = jnp.where(seg == slot_row, 1.0, 0.0)
    d_final = out_grad.astype(f32) + nn(belongs, spread, highest)
    d_resid = norm_back(d_final * gain, normal, inverse)
    low[...] = d_resid.astype(bf16)
    d_upper = nt(low[...], w_down[...]) * grad_of
    up[...] = d_upper.astype(bf16)
    part = nt(up[...], w_up[...])
    return part, d_resid, [col_sum(d_final), col_sum(d_final * normal), col_sum(d_resid), col_sum(d_upper)]


def finish_rows(block, seg, gain, shift, normal_out, inverse_out, low_out):
    normal, inverse = norm_stats(block[...])
    normal_out[...] = normal
    inverse_out[...] = jnp.broadcast_to(inverse, inverse_out.shape)
    final = normal * gain + shift
    low_out[...] = final.astype(bf16)
    slot_col = lax.broadcasted_iota(jnp.int32, (SENTS, 1), 0)
    return nn(jnp.where(slot_col == seg, 1.0, 0.0), final, highest)


def finish_early(ids, lens, r0, r1, r2, g_ffn, b_ffn, normal_ref, inverse_ref, final_low, pooled_out):
    rows, width = r0.shape
    seg_row = segment_of(lens, row_places(ids[0], (1, 4 * rows), 1, rows))
    pooled = jnp.zeros((SENTS, width), f32)
    for j, block in enumerate((r0, r1, r2)):
        at = slice(j * rows, (j + 1) * rows)
        views = (normal_ref.at[at, :], inverse_ref.at[at, :], final_low.at[at, :])
        pooled = pooled + finish_rows(block, seg_row[:, at], g_ffn[...], b_ffn[...], *views)
    pooled_out[...] = pooled


def finish_first(
    ids, lens, r3, early, pooled_in, g_ffn, b_ffn, out_grad, pool_grad, grad_of, w_down, w_up, *refs
):
    outs, (normal_ref, inverse_ref, final_low, pooled_grad) = refs[:-4], refs[-4:]
    part, layer_out, pools, spread_out, low, up, side = outs
    me = ids[0]
    rows, width = r3.shape
    gain = g_ffn[...]
    seg_row = segment_of(lens, row_places(me, (1, 4 * rows), 1, rows))
    seg_col = segment_of(lens, row_places(me, (4 * rows, 1), 0, rows))
    slot_col = lax.broadcasted_iota(jnp.int32, (SENTS, 1), 0)
    for j in range(3):
        layer_out[chunk(me, j, rows), :] = early[j * rows : (j + 1) * rows, :]
    pooled = pooled_in[...] + finish_rows(
        r3, seg_row[:, 3 * rows :], gain, b_ffn[...], normal_ref, inverse_ref, final_low
    )
    layer_out[chunk(me, 3, rows), :] = final_low[...]
    denom = jnp.zeros((SENTS, 1), f32)
    for s in range(SENTS):
        size = jnp.maximum(lens[0, s], 1).astype(f32)
        denom = denom + jnp.where(slot_col == s, size, 0.0)
    pooled = pooled / denom
    pooled_grad[...] = jnp.zeros((SENTS, width), f32)
    offset = 0
    for m in truncations(width):
        leading = pooled[:, :m]
        factor = lax.rsqrt(jnp.mean(leading * leading, axis=1, keepdims=True) + pool_eps)
        third, lane = offset // width, offset % width
        pools[third * SENTS : (third + 1) * SENTS, lane : lane + m] = leading * factor
        upstream = pool_grad[:, offset : offset + m]
        inner = jnp.mean(upstream * leading, axis=1, keepdims=True)
        pooled_grad[:, :m] += factor * upstream - leading * (factor * factor * factor * inner)
        offset += m
    rest = offset % width
    pools[2 * SENTS :, rest:] = jnp.zeros((SENTS, width - rest), f32)
    spread = pooled_grad[...] / denom
    spread_out[...] = spread
    part[...], _, sums = finish_chunk(
        seg_col[3 * rows :],
        normal_ref[...],
        inverse_ref[:, :1],
        gain,
        spread,
        out_grad[chunk(me, 3, rows), :],
        grad_of[3 * rows :, :],
        w_down,
        w_up,
        low,
        up,
    )
    for n in range(4):
        side[n : n + 1, :] = sums[n]
    side[4:, :] = jnp.zeros((4, width), f32)


def finish_rest(ids, lens, g_ffn, out_grad, grad_of, w_down, w_up, *refs):
    ins, outs, (resid_low, upper_low, held) = refs[:8], refs[8:-3], refs[-3:]
    normal_ref, inverse_ref, spread, low3, up3, side3, normed_low, act = ins
    p0, p1, p2, d_own, side, even, odd = outs
    me = ids[0]
    rows, width = p0.shape
    seg_col = segment_of(lens, row_places(me, (4 * rows, 1), 0, rows))
    resid_low[3 * rows :, :] = low3[...]
    upper_low[3 * rows :, :] = up3[...]
    at = slice(0, 3 * rows)
    part, d_resid, sums = finish_chunk(
        seg_col[at],
        normal_ref[...],
        inverse_ref[:, :1],
        g_ffn[...],
        spread[...],
        jnp.concatenate([out_grad[chunk(me, j, rows), :] for j in range(3)]),
        grad_of[at, :],
        w_down,
        w_up,
        resid_low.at[at, :],
        upper_low.at[at, :],
    )
    for j, out in enumerate((p0, p1, p2)):
        out[...] = part[j * rows : (j + 1) * rows, :]
    d_own[...] = d_resid[:rows, :]
    for n in range(4):
        side[n : n + 1, :] = side3[n : n + 1, :] + sums[n]
    side[4:, :] = jnp.zeros((4, width), f32)
    held[:width, :] = tn(normed_low[...], upper_low[...])
    held[width:, :] = tn(act[...], resid_low[...])
    step = even.shape[1]
    for d in range(8):
        at = pl.ds(pl.multiple_of((ids[1] ^ d) * step, 8), step)
        (odd if d & 1 else even)[d // 2] = held[at, :]


def back_hidden(own, near, across, d_resid, normal, inverse, g_attn, w_all, *outs):
    e0, e1, e2, e3, d_hidden_out, low_out = outs
    d_normed = d_resid[...] + (own[...] + near[...] + across[...])
    rows, width = d_normed.shape
    cols = w_all.shape[1]
    side = [None, col_sum(d_normed * normal[...]), col_sum(d_normed)]
    d_hidden = norm_back(d_normed * g_attn[...], normal[...], inverse[:, :1])
    side[0] = col_sum(d_hidden)
    d_hidden_out[...] = d_hidden
    low_out[...] = d_hidden.astype(bf16)
    base = packed_rows(rows, cols)
    for k, out in enumerate((e0, e1, e2, e3)):
        pack_into(out, nt(low_out[...], w_all[k]).astype(bf16).astype(f32))
        out[base:, :] = jnp.zeros((out.shape[0] - base, 128), f32)
        for v in range(3):
            for s in range(width // cols):
                for n in range(0, cols, 128):
                    r = base + (n // 128) * 16 + 4 * v + s
                    m = min(128, cols - n)
                    out[r : r + 1, :m] = side[v][:, s * cols + n : s * cols + n + m]


def out_grads(ids, m0, m1, m2, m3, hidden_low, even, odd, held):
    rows = hidden_low.shape[0]
    for k, block in enumerate((m0, m1, m2, m3)):
        for col, part in packed_parts(block, held.shape[1], 4 * rows, k * rows, rows):
            held[k, col : col + part.shape[1], :] = tn(part.astype(bf16), hidden_low[...])
    step = even.shape[2]
    for d in range(8):
        at = pl.ds(pl.multiple_of((ids[1] ^ d) * step, 8), step)
        for k in range(4):
            (odd if d & 1 else even)[d // 2, k] = held[k, at, :]


def attend_back(e0, e1, e2, e3, probs, q, k, v, wq, wk, wv, *refs):
    outs, (d_mixed, turned, d_scores) = refs[:-3], refs[-3:]
    p0, p1, p2, p3, grads, bias, shared = outs
    slots, cols = q.shape
    rows = slots // 4
    scale = HDIM**-0.5
    half = rows // 2
    for j, block in enumerate((e0, e1, e2, e3)):
        for r in (0, half):
            for col, part in packed_parts(block, cols, rows, r, half):
                at = slice(j * rows + r, j * rows + r + half)
                d_mixed[at, col : col + part.shape[1]] = part.astype(bf16)
    base = packed_rows(rows, cols)
    side = (e0[base:, :] + e1[base:, :]) + (e2[base:, :] + e3[base:, :])
    for n in range(0, cols, 128):
        m = min(128, cols - n)
        shared[:, n : n + m] = side[(n // 128) * 16 : (n // 128) * 16 + 16, :m]
    for h in range(cols // HDIM):
        lane = slice(h * HDIM, (h + 1) * HDIM)
        for j in range(4):
            at = slice(j * rows, (j + 1) * rows)
            p = probs[h, at, :].astype(f32)
            dp = nt(d_mixed[at, lane], v[:, lane])
            t = p * dp
            ds = (t - p * jnp.sum(t, axis=-1, keepdims=True)) * scale
            d_scores[at, :] = ds.astype(bf16)
        d_query = nn(d_scores[...], k[:, lane])
        bias[0:1, lane] = col_sum(d_query)
        grads[:, lane] = d_query.astype(bf16)
        d_key = tn(q[:, lane], d_scores[...]).T
        grads[:, cols + h * HDIM : cols + (h + 1) * HDIM] = d_key.astype(bf16)
        d_value = tn(d_mixed[:, lane], probs[h]).T
        bias[1:2, lane] = col_sum(d_value)
        grads[:, 2 * cols + h * HDIM : 2 * cols + (h + 1) * HDIM] = d_value.astype(bf16)
    bias[2:, :] = jnp.zeros((6, cols), f32)
    turned[:cols, :] = wq[...]
    turned[cols : 2 * cols, :] = wk[...]
    turned[2 * cols :, :] = wv[...]
    for j, out in ((3, p3), (2, p2), (1, p1), (0, p0)):
        out[...] = nn(grads[j * rows : (j + 1) * rows, :], turned[...])


def qkv_grads(ids, grads, tok_x, side, shared, bias, even, odd, held):
    width = tok_x.shape[1]
    cols = bias.shape[1]
    part = width // cols
    total = grads.shape[1]
    step = total // 8
    held[:total, :] = tn(grads[...], tok_x[...])
    held[total:, :] = jnp.zeros((64, width), f32)
    held[total : total + 4, :] = side[:4, :]

    @pl.when(ids[0] >= 0)
    def _():
        for n in range(2):
            held[total + 4 : total + 5, n * cols : (n + 1) * cols] = bias[n : n + 1, :]
        for n in range(3):
            for s in range(part):
                row = shared[4 * n + s : 4 * n + s + 1, :]
                held[total + 8 + n : total + 9 + n, s * cols : (s + 1) * cols] = row

    for d in range(8):
        c = ids[1] ^ d
        out = odd if d & 1 else even
        out[d // 2, :step, :] = held[pl.ds(pl.multiple_of(c * step, 8), step), :]
        out[d // 2, step:, :] = held[pl.ds(pl.multiple_of(total + c * 8, 8), 8), :]


def fold(mine, theirs, *refs):
    extra, outs = refs[: len(refs) - 4], refs[len(refs) - 4 :]
    rows = mine.shape[1]
    for n, out in enumerate(outs):
        out[:rows, :] = mine[n] + theirs[n]
        if n and extra:
            out[rows:, :] = extra[0][...]


def fold_halves(mine, theirs, *refs):
    extra, (own, to_x, to_y, keep_y, keep_x) = refs[:-5], refs[-5:]
    half = mine.shape[1] // 2
    own[...] = mine[0] + theirs[0]
    for n, (out, at) in enumerate(((to_x, slice(0, half)), (to_y, slice(half, 2 * half)))):
        for m, block in enumerate((1 + n, 3)):
            out[m * half : (m + 1) * half, :] = mine[block, at, :] + theirs[block, at, :]
        if extra:
            more = extra[0].shape[0] // 2
            out[2 * half :, :] = extra[0][n * more : (n + 1) * more, :]
    keep_y[...] = mine[2, :half, :] + theirs[2, :half, :]
    keep_x[...] = mine[1, half:, :] + theirs[1, half:, :]


def add(a, b, out):
    out[...] = a[...] + b[...]


def join_terms(part1, part2, far, o0, o1, o2, o3, near_out, across_out):
    rows = part1.shape[0]
    piece = o3.shape[0]
    near_out[:rows, :] = part1[...]
    near_out[rows:, :] = (o0[3 * piece :, :] + o1[3 * piece :, :]) + (o2[3 * piece :, :] + o3[...])
    across_out[...] = part2[...] + far[...]


def join_own(own, near, across, d_hidden, o0, o1, o2, o3, near_out, across_out, term):
    rows = own.shape[0]
    piece = term.shape[0]
    total = own[...] + near[:rows, :] + across[...] + d_hidden[...]
    near_out[:rows, :] = total
    across_out[:rows, :] = total
    for n, out, at in ((0, term, 0), (1, near_out, rows), (2, across_out, rows)):
        rest = slice(n * piece, (n + 1) * piece)
        sums = (o0[rest, :] + o1[rest, :]) + (o2[rest, :] + o3[rest, :])
        if n == 2:
            sums = sums + near[rows:, :]
        out[at : at + piece, :] = sums


def join_far(across, near, term, out, out_own):
    rows = out.shape[0]
    out[...] = across[:rows, :]
    out_own[...] = term[...] + near[rows:, :] + across[rows:, :]


def collect(own, extra, from_x, from_y, last_y, last_x, out_own, sums, mine):
    half = own.shape[0] // 2
    sums[:half, :] = own[:half, :] + from_x[:half, :] + last_y[:half, :]
    sums[half : 2 * half, :] = own[half:, :] + from_y[:half, :] + last_x[:half, :]
    sums[2 * half :, :] = out_own[...]
    travel = extra.shape[0] // 2
    more = 3 * SENTS // 2
    part = travel - more
    for n, (block, at) in enumerate(
        (
            (extra, 0),
            (extra, travel),
            (from_x, 2 * half),
            (last_x, half),
            (last_y, half),
            (from_y, 2 * half),
            (last_y, half + travel),
            (last_x, half + travel),
        )
    ):
        mine[n * part : (n + 1) * part, :] = block[at : at + part, :]
        to = 8 * part + n * more
        mine[to : to + more, :] = block[at + part : at + travel, :]


def place(me, r0, r1, r2, r3, out):
    rows = out.shape[0] // 4
    for j, block in enumerate((r0, r1, r2, r3)):
        out[chunk(me[0], j, rows), :] = block[:rows, :]


def unpack_ffn(ids, mine, theirs, up_out, down_out, pools_out, held):
    half = up_out.shape[0]
    step = 2 * half // 8
    wide = pools_out.shape[0]
    width = up_out.shape[1]
    for d in range(8):
        block = theirs if d & 1 else mine
        start = (d // 2) * step
        c = ids[1] ^ d
        at = pl.ds(pl.multiple_of((c % 4) * step, 8), step)

        @pl.when(c < 4)
        def _(block=block, at=at, start=start):
            up_out[at, :] = block[start : start + step, :]

        @pl.when(c >= 4)
        def _(block=block, at=at, start=start):
            down_out[at, :] = block[start : start + step, :]

        to = pl.ds(pl.multiple_of(c * SENTS, 8), SENTS)
        start = 4 * step + (d // 2) * 3 * SENTS
        for n in range(3):
            held[n, to, :] = block[start + n * SENTS : start + (n + 1) * SENTS, :]
    for n in range(3):
        m = min(width, wide - n * width)
        pools_out[n * width : n * width + m, :] = held[n].T[:m, :]


def unpack_attn(ids, *refs):
    blocks, outs, (held, side) = refs[:8], refs[8:-2], refs[-2:]
    q_out, k_out, v_out, o_out, *vectors = outs
    cols = o_out.shape[0]
    step = 3 * cols // 8
    small = cols // 8
    for d, block in enumerate(blocks):
        c = ids[1] ^ d
        held[pl.ds(pl.multiple_of(c * step, 8), step), :] = block[:step, :]
        side[pl.ds(pl.multiple_of(c * 8, 8), 8), :] = block[step : step + 8, :]
        o_out[pl.ds(pl.multiple_of(c * small, 8), small), :] = block[step + 8 :, :]
    q_out[...] = held[:cols, :]
    k_out[...] = held[cols : 2 * cols, :]
    v_out[...] = held[2 * cols :, :]
    vectors[0][...] = side[4, :cols]
    vectors[1][...] = side[4, cols : 2 * cols]
    for n, r in enumerate((8, 9, 10, 3, 2, 1, 0)):
        vectors[2 + n][...] = side[r, :]


def swap(block, k):
    return lax.ppermute(block, "tensor", swaps[k])


def swap_dp(block, k, n_dp):
    return lax.ppermute(block, "dp", [(i, i ^ k) for i in range(n_dp)])


def together(*items):
    return lax.optimization_barrier(items)


def rest_of_dp(block, n_dp):
    if n_dp == 8:
        return block
    groups = [[i + 8 * j for j in range(n_dp // 8)] for i in range(8)]
    return lax.psum(block, "dp", axis_index_groups=groups)


def core_swap(even, odd, n_dp):
    other = swap_dp(odd, 1, n_dp)
    flat = even.shape[-2] if even.ndim == 3 else even.shape[1] * even.shape[2]
    return even.reshape(4, flat, even.shape[-1]), other.reshape(4, flat, even.shape[-1])


def halves_start(even, other, *extra):
    _, rows, width = even.shape
    half, more = rows // 2, sum(item.shape[0] // 2 for item in extra)
    return call(
        fold_halves,
        [shape(rows, width)] + [shape(rows + more, width)] * 2 + [shape(half, width)] * 2,
        [even, other, *extra],
        moved=3 * even.size * 4,
    )


def with_other_core(blocks, n_dp):
    others = [swap_dp(item, 1, n_dp) for item in blocks]
    return [item for pair in zip(blocks, others) for item in pair]


def make_shards(n_dp):
    def shards(
        tokens,
        lengths,
        w_query,
        w_key,
        w_value,
        b_query,
        b_value,
        w_out,
        b_out,
        g_attn,
        b_attn,
        w_up,
        b_up,
        w_down,
        b_down,
        g_ffn,
        b_ffn,
        out_grad,
        pool_grad,
    ):
        me = lax.axis_index("tensor").astype(jnp.int32)
        group = (lax.axis_index("dp") % 8).astype(jnp.int32)
        ids = jnp.stack([me, group])
        slots, width = tokens.shape
        cols = w_query.shape[1]
        units = w_up.shape[1]
        heads = cols // HDIM
        rows = slots // 4
        row = lambda vector: vector.reshape(1, -1)
        wq, wk, wv = w_query.T, w_key.T, w_value.T

        piece = cols // 8
        slice_own = lax.dynamic_slice_in_dim(w_out, group * piece, piece, 0).astype(f32)
        slices = [slice_own] + [swap(slice_own, n) for n in (1, 2, 3)]

        tok_x, q, k, v, probs, mixed = call(
            attend,
            [
                shape(slots, width, kind=bf16),
                shape(slots, cols, kind=bf16),
                shape(slots, cols, kind=bf16),
                shape(slots, cols, kind=bf16),
                shape(heads, slots, slots, kind=bf16),
                shape(packed_rows(slots, cols), 128),
            ],
            [ids]
            + [
                pltpu.with_memory_space_constraint(item, pltpu.HBM)
                for item in (lengths, tokens, wq, wk, wv, row(b_query), row(b_value))
            ],
            flops=2 * slots * width * 3 * cols + 4 * slots * slots * cols,
            moved=slots * width * 4 + 3 * cols * width * 2 + heads * slots * slots * 2,
            scratch=[pltpu.VMEM((slots, cols), bf16)]
            + [pltpu.VMEM((cols, width), bf16)] * 3
            + [pltpu.VMEM((1, cols), f32)] * 2
            + [pltpu.SMEM((1, SENTS), jnp.int32), pltpu.SemaphoreType.DMA((10,))],
            raw=7,
        )
        mixed, *slices = together(mixed, *slices)
        slices = jnp.stack(slices)
        across, near = swap(mixed, 2), swap(mixed, 1)
        w_blocks = [swap_dp(slices, 2 * n, n_dp) for n in (1, 2, 3)]
        across, near, slices, *w_blocks = together(across, near, slices, *w_blocks)
        mixed_all = [mixed, near, across, swap(across, 1)]
        w_all = call(
            join_w_out,
            shape(4, cols, width, kind=bf16),
            [ids] + with_other_core([slices] + w_blocks, n_dp),
            moved=4 * cols * width * 6,
            scratch=[pltpu.VMEM((4, cols, width), f32)],
        )
        feed_ins = [tok_x, *mixed_all, w_all, row(b_out), row(g_attn), row(b_attn)]
        feed_ins += [w_up, row(b_up), w_down]
        part3, low3, upper3, act3 = call(
            feed_first,
            [
                shape(rows, width),
                shape(rows, width, kind=bf16),
                shape(rows, units),
                shape(rows, units, kind=bf16),
            ],
            feed_ins,
            flops=2 * rows * width * (width + 2 * units),
            moved=rows * width * 4 + 3 * width * units * 2,
        )
        far = swap(part3, 1)
        *parts, normed_low, upper, act, normal_own, inverse_own, resid_own = call(
            feed_rest,
            [shape(rows, width)] * 3
            + [
                shape(slots, width, kind=bf16),
                shape(slots, units),
                shape(slots, units, kind=bf16),
                shape(rows, width),
                shape(rows, 128),
                shape(rows, width),
            ],
            feed_ins + [row(b_down), low3, upper3, act3],
            flops=6 * rows * width * (width + 2 * units),
            moved=3 * slots * width * 4 + 3 * width * units * 2,
        )
        slope = call(
            gelu_grad, shape(slots, units), [upper], moved=8 * slots * units, flops=slots * units
        )
        far, slope, part2, part1 = together(far, slope, parts[2], parts[1])
        across, near = swap(part2 + far, 2), swap(part1, 1)
        own = resid_own + parts[0] + near + across
        across, near = swap(own, 2), swap(own, 1)
        across, near = together(across, near)
        resid = [own, near, across, swap(across, 1)]
        normal, inverse, early, pooled = call(
            finish_early,
            [shape(3 * rows, width), shape(3 * rows, 128)]
            + [shape(3 * rows, width, kind=bf16), shape(SENTS, width)],
            [ids, lengths, *resid[:3], row(g_ffn), row(b_ffn)],
            flops=slots * width * 100,
            moved=3 * slots * width * 4,
        )
        part3, layer_out, own_pools, spread, low3, up3, side3 = call(
            finish_first,
            [
                shape(rows, width),
                shape(slots, width, kind=bf16),
                shape(3 * SENTS, width),
                shape(SENTS, width),
                shape(rows, width, kind=bf16),
                shape(rows, units, kind=bf16),
                shape(8, width),
            ],
            [ids, lengths, resid[3], early, pooled, row(g_ffn), row(b_ffn), out_grad, pool_grad]
            + [slope, w_down, w_up],
            flops=4 * rows * width * units,
            moved=6 * slots * width * 4,
            scratch=[
                pltpu.VMEM((rows, width), f32),
                pltpu.VMEM((rows, 128), f32),
                pltpu.VMEM((rows, width), bf16),
                pltpu.VMEM((SENTS, width), f32),
            ],
        )
        far = swap(part3, 1)
        step = 2 * width // 8
        *parts, d_resid, side, even, odd = call(
            finish_rest,
            [shape(rows, width)] * 4 + [shape(8, width)] + [shape(4, step, width)] * 2,
            [ids, lengths, row(g_ffn), out_grad, slope, w_down, w_up]
            + [normal, inverse, spread, low3, up3, side3, normed_low, act],
            flops=8 * slots * width * units,
            moved=6 * slots * width * 4 + 8 * width * units,
            scratch=[
                pltpu.VMEM((slots, width), bf16),
                pltpu.VMEM((slots, units), bf16),
                pltpu.VMEM((2 * width, width), f32),
            ],
        )
        even, other = core_swap(even, odd, n_dp)
        part2 = call(add, shape(rows, width), [parts[2], far], flops=100 * order)
        part2, part1, even, other = together(part2, parts[1], even, other)
        across, near = swap(part2, 2), swap(part1, 1)
        ffn_own, to_x, to_y, keep_y, keep_x = halves_start(even, other)
        from_x, from_y = swap_dp(to_x, 2, n_dp), swap_dp(to_y, 4, n_dp)
        *sent, d_hidden, hidden_low = call(
            back_hidden,
            [shape(packed_rows(rows, cols) + 16 * -(-cols // 128), 128)] * 4
            + [shape(rows, width), shape(rows, width, kind=bf16)],
            [parts[0], near, across, d_resid, normal_own, inverse_own, row(g_attn), w_all],
            flops=30 * order,
            moved=6 * rows * width * 4,
        )
        *sent, d_hidden, hidden_low, from_x, from_y, keep_x, keep_y = together(
            *sent, d_hidden, hidden_low, from_x, from_y, keep_x, keep_y
        )
        d_mixed = [sent[0]] + [swap(sent[n], n) for n in (1, 2, 3)]
        half = step // 2
        to_y, to_x = keep_y + from_x[half:], keep_x + from_y[half:]
        last_y, last_x = swap_dp(to_y, 4, n_dp), swap_dp(to_x, 2, n_dp)
        even, odd = call(
            out_grads,
            [shape(4, 4, piece, width)] * 2,
            [ids, *mixed_all, hidden_low],
            flops=2 * rows * width * 4 * cols,
            moved=8 * 4 * cols * width,
            scratch=[pltpu.VMEM((4, cols, width), f32)],
        )
        even, other = core_swap(even, odd, n_dp)
        d_mixed = together(*d_mixed)
        *parts, grads, bias, shared = call(
            attend_back,
            [shape(rows, width)] * 4
            + [shape(slots, 3 * cols, kind=bf16), shape(8, cols), shape(16, cols)],
            [*d_mixed, probs, q, k, v, wq, wk, wv],
            flops=10 * order,
            moved=heads * slots * slots * 2 + 2 * slots * width * 4,
            scratch=[
                pltpu.VMEM((slots, cols), bf16),
                pltpu.VMEM((3 * cols, width), bf16),
                pltpu.VMEM((slots, slots), bf16),
            ],
        )
        part3, out_even, out_other, last_x, last_y = together(parts[3], even, other, last_x, last_y)
        far = swap(part3, 1)
        ffn_sum = [ffn_own[:half] + from_x[:half] + last_y, ffn_own[half:] + from_y[:half] + last_x]
        if n_dp > 8:
            ffn_sum = [rest_of_dp(item, n_dp) for item in ffn_sum]
        more = 3 * SENTS // 2
        extra = [ffn_sum[0], own_pools[:more], ffn_sum[1], own_pools[more:]]
        extra = jnp.concatenate(extra)
        out = call(
            fold,
            [shape(4 * piece, width)] * 4,
            [out_even, out_other],
            moved=3 * out_even.size * 4,
        )
        out_x, out_y = swap_dp(out[1], 2, n_dp), swap_dp(out[2], 4, n_dp)
        even, odd = call(
            qkv_grads,
            [shape(4, 3 * piece + 8, width)] * 2,
            [ids, grads, tok_x, side, shared, bias],
            flops=6 * slots * width * cols,
            moved=8 * 3 * cols * width,
            scratch=[pltpu.VMEM((3 * cols + 64, width), f32)],
        )
        even, other = core_swap(even, odd, n_dp)
        out_d = swap_dp(out[3][3 * piece :], 6, n_dp)
        pieces = [out[0], out_x, out_y, out_d]
        if n_dp > 8:
            pieces[3] = rest_of_dp(sum(item[-piece:] for item in pieces), n_dp)
            pieces[:3] = [jnp.zeros_like(item) for item in pieces[:3]]
        part1, part2 = call(
            join_terms,
            [shape(rows + piece, width), shape(rows, width)],
            [parts[1], parts[2], far, *pieces],
            flops=20 * order,
        )
        part2, part1, even, other, out_x, out_y, out_d = together(
            part2, part1, even, other, out_x, out_y, out[3][: 3 * piece]
        )
        across, near = swap(part2, 2), swap(part1, 1)
        out_d = swap_dp(out_d, 6, n_dp)
        qkv_own, to_x, to_y, keep_y, keep_x = halves_start(even, other, extra)
        from_x, from_y = swap_dp(to_x, 2, n_dp), swap_dp(to_y, 4, n_dp)
        pieces = [out[0], out_x, out_y, out_d]
        if n_dp > 8:
            pieces[0] = rest_of_dp(sum(item[: 3 * piece] for item in pieces), n_dp)
            pieces[1:] = [jnp.zeros_like(pieces[0])] * 3
        own_near, own_across, term = call(
            join_own,
            [shape(rows + piece, width)] * 2 + [shape(piece, width)],
            [parts[0], near, across, d_hidden, *pieces],
            flops=30 * order,
            moved=7 * rows * width * 4,
        )
        own_near, own_across, from_x, from_y, keep_x, keep_y = together(
            own_near, own_across, from_x, from_y, keep_x, keep_y
        )
        across, near = swap(own_across, 2), swap(own_near, 1)
        low, travel = keep_y.shape[0], half + more
        to_y = [keep_y + from_x[low : 2 * low], extra[:travel], from_x[2 * low :]]
        to_x = [keep_x + from_y[low : 2 * low], extra[travel:], from_y[2 * low :]]
        to_y, to_x = jnp.concatenate(to_y), jnp.concatenate(to_x)
        last_y, last_x = swap_dp(to_y, 4, n_dp), swap_dp(to_x, 2, n_dp)
        far, out_own = call(
            join_far,
            [shape(rows, width), shape(piece, width)],
            [across, near, term],
            flops=30 * order,
        )
        far, near, across, out_own, last_y, last_x = together(
            far, near, across, out_own, last_y, last_x
        )
        far = swap(far, 1)
        attn_own, mine = call(
            collect,
            [shape(4 * piece + 8, width), shape(4 * (step + 3 * SENTS), width)],
            [qkv_own, extra, from_x, from_y, last_y, last_x, out_own],
            flops=1 * order,
            moved=8 * 4 * step * width,
        )
        if n_dp > 8:
            low = 3 * piece + 8
            attn_own = jnp.concatenate([rest_of_dp(attn_own[:low], n_dp), attn_own[low:]])
        attn_blocks = [attn_own] + [swap_dp(attn_own, 2 * n, n_dp) for n in (1, 2, 3)]
        wide = pool_grad.shape[1]
        d_w_up, d_w_down, pools = call(
            unpack_ffn,
            [shape(width, units), shape(units, width), shape(wide, 8 * SENTS)],
            [ids, mine, swap_dp(mine, 1, n_dp)],
            moved=16 * width * units,
            scratch=[pltpu.VMEM((3, 8 * SENTS, width), f32)],
        )
        d_tokens = call(
            place, shape(slots, width), [ids, own_near, near, across, far], flops=30 * order
        )
        d_w_up, d_w_down, pools, d_tokens, *attn_blocks = together(
            d_w_up, d_w_down, pools, d_tokens, *attn_blocks
        )
        d_w_query, d_w_key, d_w_value, d_w_out, *vectors = call(
            unpack_attn,
            [shape(cols, width)] * 4 + [shape(cols)] * 2 + [shape(width)] * 7,
            [ids, *with_other_core(attn_blocks, n_dp)],
            moved=8 * 4 * cols * width,
            scratch=[pltpu.VMEM((3 * cols, width), f32), pltpu.VMEM((64, width), f32)],
        )
        b_q, b_v, d_b_out, d_g_attn, d_b_attn, d_b_up, d_b_down, d_g_ffn, d_b_ffn = vectors
        pools = pools.T
        if n_dp > 8:
            third = [own_pools[n * SENTS : (n + 1) * SENTS] for n in range(3)]
            third = jnp.concatenate(third, axis=1)[:, :wide]
            pools = lax.all_gather(third, "dp", axis=0, tiled=True)
        return (
            layer_out,
            pools,
            d_tokens,
            d_w_query.T,
            d_w_key.T,
            d_w_value.T,
            b_q,
            b_v,
            d_w_out,
            d_b_out,
            d_g_attn,
            d_b_attn,
            d_w_up,
            d_b_up,
            d_w_down,
            d_b_down,
            d_g_ffn,
            d_b_ffn,
        )

    return shards


def solution(mesh):
    return jax.shard_map(
        make_shards(mesh.shape["dp"]),
        mesh=mesh,
        in_specs=(
            P("dp", None),
            P("dp", None),
            P(None, "tensor"),
            P(None, "tensor"),
            P(None, "tensor"),
            P("tensor"),
            P("tensor"),
            P("tensor", None),
            P(),
            P(),
            P(),
            P(None, "tensor"),
            P("tensor"),
            P("tensor", None),
            P(),
            P(),
            P(),
            P("dp", None),
            P("dp", None),
        ),
        out_specs=(
            P("dp", None),
            P(),
            P("dp", None),
            P(None, "tensor"),
            P(None, "tensor"),
            P(None, "tensor"),
            P("tensor"),
            P("tensor"),
            P("tensor", None),
            P(),
            P(),
            P(),
            P(None, "tensor"),
            P("tensor"),
            P("tensor", None),
            P(),
            P(),
            P(),
        ),
        check_vma=False,
    )
```

```python
import functools

import jax
import jax.numpy as jnp
from jax import lax
from jax.experimental import pallas as pl
from jax.experimental.pallas import tpu as pltpu
from jax.sharding import PartitionSpec as P

HDIM = 64
SENTS = 16
norm_eps = 1e-06
pool_eps = 1e-05
highest = lax.Precision.HIGHEST
f32 = jnp.float32
bf16 = jnp.bfloat16
order = 10**9
swaps = {k: [(i, i ^ k) for i in range(4)] for k in (1, 2, 3)}


def truncations(width):
    return [width, width * 2 // 3, width // 3, width // 6, width // 12]


def nn(left, right, precision=None):
    return lax.dot_general(
        left, right, (((1,), (0,)), ((), ())), precision=precision, preferred_element_type=f32
    )


def nt(left, right):
    return lax.dot_general(left, right, (((1,), (1,)), ((), ())), preferred_element_type=f32)


def tn(left, right):
    return lax.dot_general(left, right, (((0,), (0,)), ((), ())), preferred_element_type=f32)


def norm_stats(rows):
    centre = jnp.mean(rows, axis=-1, keepdims=True)
    shifted = rows - centre
    inverse = lax.rsqrt(jnp.mean(shifted * shifted, axis=-1, keepdims=True) + norm_eps)
    return shifted * inverse, inverse


def norm_back(grad_in, normal, inverse):
    centre = jnp.mean(grad_in, axis=-1, keepdims=True)
    along = jnp.mean(grad_in * normal, axis=-1, keepdims=True)
    return inverse * (grad_in - centre - normal * along)


def col_sum(rows):
    return jnp.sum(rows, axis=0, keepdims=True)


def shape(*extent, kind=f32):
    return jax.ShapeDtypeStruct(extent, kind)


def call(body, outs, ins, flops=0, moved=0, scratch=(), limit=32, raw=0):
    specs = [
        pl.BlockSpec(memory_space=pltpu.SMEM if item.dtype == jnp.int32 else pltpu.VMEM)
        for item in ins[: len(ins) - raw]
    ] + [pl.BlockSpec(memory_space=pltpu.HBM)] * raw
    return pl.pallas_call(
        body,
        out_shape=outs,
        in_specs=specs,
        out_specs=jax.tree.map(lambda _: pl.BlockSpec(memory_space=pltpu.VMEM), outs),
        scratch_shapes=list(scratch),
        cost_estimate=pl.CostEstimate(flops=flops, bytes_accessed=moved, transcendentals=0),
        compiler_params=pltpu.CompilerParams(vmem_limit_bytes=limit << 20),
    )(*ins)


def chunk(me, j, rows):
    return pl.ds(pl.multiple_of((me ^ j) * rows, rows), rows)


def segment_of(lengths, places):
    end = jnp.int32(0)
    found = jnp.zeros(places.shape, jnp.int32)
    for s in range(SENTS):
        end = end + lengths[0, s]
        found = found + jnp.where(places >= end, 1, 0)
    return found


def row_places(me, extent, dim, rows):
    at = lax.broadcasted_iota(jnp.int32, extent, dim)
    return ((at // rows) ^ me) * rows + at % rows


def packed_rows(rows, cols):
    return rows * (cols // 128) + (rows // 2 if cols % 128 else 0)


def pack_into(out, block):
    rows, cols = block.shape
    full = cols // 128
    for n in range(full):
        out[n * rows : (n + 1) * rows, :] = block[:, n * 128 : (n + 1) * 128]
    if cols % 128:
        half = rows // 2
        out[full * rows : full * rows + half, :HDIM] = block[:half, full * 128 :]
        out[full * rows : full * rows + half, HDIM:] = block[half:, full * 128 :]


def packed_parts(block, cols, slots, start, rows):
    full = cols // 128
    for n in range(full):
        yield n * 128, block[n * slots + start : n * slots + start + rows, :]
    if cols % 128:
        half = slots // 2
        side = start // half
        at = full * slots + start - side * half
        yield full * 128, block[at : at + rows, side * HDIM : (side + 1) * HDIM]


def attend(ids, lengths, tok, wq_in, wk_in, wv_in, bq_in, bv_in, *refs):
    tok_x, q_out, k_out, v_out, probs_out, packed, low, wq, wk, wv, bq, bv, lens, sems = refs
    me = ids[0]
    slots, cols = q_out.shape
    rows = slots // 4
    moves = [
        (lengths, lens),
        (wk_in, wk),
        *[(tok.at[chunk(me, j, rows), :], tok_x.at[j * rows : (j + 1) * rows, :]) for j in range(4)],
        (wv_in, wv),
        (bv_in, bv),
        (wq_in, wq),
        (bq_in, bq),
    ]
    moves = [pltpu.make_async_copy(a, b, sems.at[n]) for n, (a, b) in enumerate(moves)]
    for move in moves:
        move.start()
    for move in moves[:6]:
        move.wait()
    t = tok_x[...]
    k_out[...] = nt(t, wk[...]).astype(bf16)
    for move in moves[6:]:
        move.wait()
    v_out[...] = (nt(t, wv[...]) + bv[...]).astype(bf16)
    q_out[...] = (nt(t, wq[...]) + bq[...]).astype(bf16)
    seg_row = segment_of(lens, row_places(me, (1, slots), 1, rows))
    seg_col = segment_of(lens, row_places(me, (slots, 1), 0, rows))
    scale = HDIM**-0.5
    tall = slots
    for r in range(0, slots, tall):
        at = slice(r, r + tall)
        allowed = seg_col[at] == seg_row
        for h in range(cols // HDIM):
            lane = slice(h * HDIM, (h + 1) * HDIM)
            s = jnp.where(allowed, nt(q_out[at, lane], k_out[:, lane]) * scale, -1000000000.0)
            e = jnp.exp(s - jnp.max(s, axis=-1, keepdims=True))
            p = (e * (1.0 / jnp.sum(e, axis=-1, keepdims=True))).astype(bf16)
            probs_out[h, at, :] = p
            low[at, lane] = nn(p, v_out[:, lane]).astype(bf16)
    pack_into(packed, low[...].astype(f32))


def join_w_out(ids, *refs):
    pieces, out, held = refs[:-2], refs[-2], refs[-1]
    step = pieces[0].shape[1]
    for d in range(len(pieces)):
        at = pl.ds(pl.multiple_of((ids[1] ^ d) * step, 8), step)
        for k in range(4):
            held[k, at, :] = pieces[d][k]
    out[...] = held[...].astype(bf16)


def gelu_grad(upper, out):
    rows = 64
    for r in range(0, upper.shape[0], rows):
        u = upper[r : r + rows, :]
        cdf = 0.5 * (1.0 + lax.erf(u * 0.7071067811865476))
        out[r : r + rows, :] = cdf + u * (0.3989422804014327 * jnp.exp(-0.5 * u * u))


def feed_chunk(j, tok_x, mixed, w_all, b_out, g_attn, b_attn, w_up, b_up, w_down, low, upper, act, part):
    rows = part.shape[0]
    at = slice(j * rows, (j + 1) * rows)
    total = tok_x[at, :].astype(f32) + b_out[...]
    for k in range(4):
        for col, block in packed_parts(mixed[k], w_all.shape[1], 4 * rows, (j ^ k) * rows, rows):
            total = total + nn(block.astype(bf16), w_all[k, col : col + block.shape[1], :])
    normal, inverse = norm_stats(total)
    normed = normal * g_attn[...] + b_attn[...]
    low[...] = normed.astype(bf16)
    upper[...] = nn(low[...], w_up[...]) + b_up[...]
    half = rows // 2
    for r in (0, half):
        u = upper[r : r + half, :]
        cdf = 0.5 * (1.0 + lax.erf(u * 0.7071067811865476))
        act[r : r + half, :] = (u * cdf).astype(bf16)
    part[...] = nn(act[...], w_down[...])
    return normed, normal, inverse


def feed_first(tok_x, m0, m1, m2, m3, w_all, b_out, g_attn, b_attn, w_up, b_up, w_down, *outs):
    part, low, upper, act = outs
    mixed = (m0, m1, m2, m3)
    ins = (tok_x, mixed, w_all, b_out, g_attn, b_attn, w_up, b_up, w_down)
    feed_chunk(3, *ins, low, upper, act, part)


def feed_rest(tok_x, m0, m1, m2, m3, w_all, b_out, g_attn, b_attn, w_up, b_up, w_down, b_down, *refs):
    (low3, upper3, act3), outs = refs[:3], refs[3:]
    p0, p1, p2, low, upper, act, normal_own, inverse_own, resid_own = outs
    parts = (p0, p1, p2)
    mixed = (m0, m1, m2, m3)
    ins = (tok_x, mixed, w_all, b_out, g_attn, b_attn, w_up, b_up, w_down)
    rows = p0.shape[0]
    for full, piece in ((low, low3), (upper, upper3), (act, act3)):
        full[3 * rows :, :] = piece[...]
    for j in (2, 1, 0):
        at = slice(j * rows, (j + 1) * rows)
        views = (low.at[at, :], upper.at[at, :], act.at[at, :], parts[j])
        normed, normal, inverse = feed_chunk(j, *ins, *views)
    normal_own[...] = normal
    inverse_own[...] = jnp.broadcast_to(inverse, inverse_own.shape)
    resid_own[...] = normed + b_down[...]


def finish_chunk(seg, normal, inverse, gain, spread, out_grad, grad_of, w_down, w_up, low, up):
    slot_row = lax.broadcasted_iota(jnp.int32, (1, SENTS), 1)
    belongs = jnp.where(seg == slot_row, 1.0, 0.0)
    d_final = out_grad.astype(f32) + nn(belongs, spread, highest)
    d_resid = norm_back(d_final * gain, normal, inverse)
    low[...] = d_resid.astype(bf16)
    d_upper = nt(low[...], w_down[...]) * grad_of
    up[...] = d_upper.astype(bf16)
    part = nt(up[...], w_up[...])
    return part, d_resid, [col_sum(d_final), col_sum(d_final * normal), col_sum(d_resid), col_sum(d_upper)]


def finish_rows(block, seg, gain, shift, normal_out, inverse_out, low_out):
    normal, inverse = norm_stats(block[...])
    normal_out[...] = normal
    inverse_out[...] = jnp.broadcast_to(inverse, inverse_out.shape)
    final = normal * gain + shift
    low_out[...] = final.astype(bf16)
    slot_col = lax.broadcasted_iota(jnp.int32, (SENTS, 1), 0)
    return nn(jnp.where(slot_col == seg, 1.0, 0.0), final, highest)


def finish_early(ids, lens, r0, r1, r2, g_ffn, b_ffn, normal_ref, inverse_ref, final_low, pooled_out):
    rows, width = r0.shape
    seg_row = segment_of(lens, row_places(ids[0], (1, 4 * rows), 1, rows))
    pooled = jnp.zeros((SENTS, width), f32)
    for j, block in enumerate((r0, r1, r2)):
        at = slice(j * rows, (j + 1) * rows)
        views = (normal_ref.at[at, :], inverse_ref.at[at, :], final_low.at[at, :])
        pooled = pooled + finish_rows(block, seg_row[:, at], g_ffn[...], b_ffn[...], *views)
    pooled_out[...] = pooled


def finish_first(
    ids, lens, r3, early, pooled_in, g_ffn, b_ffn, out_grad, pool_grad, grad_of, w_down, w_up, *refs
):
    outs, (normal_ref, inverse_ref, final_low, pooled_grad) = refs[:-4], refs[-4:]
    part, layer_out, pools, spread_out, low, up, side = outs
    me = ids[0]
    rows, width = r3.shape
    gain = g_ffn[...]
    seg_row = segment_of(lens, row_places(me, (1, 4 * rows), 1, rows))
    seg_col = segment_of(lens, row_places(me, (4 * rows, 1), 0, rows))
    slot_col = lax.broadcasted_iota(jnp.int32, (SENTS, 1), 0)
    for j in range(3):
        layer_out[chunk(me, j, rows), :] = early[j * rows : (j + 1) * rows, :]
    pooled = pooled_in[...] + finish_rows(
        r3, seg_row[:, 3 * rows :], gain, b_ffn[...], normal_ref, inverse_ref, final_low
    )
    layer_out[chunk(me, 3, rows), :] = final_low[...]
    denom = jnp.zeros((SENTS, 1), f32)
    for s in range(SENTS):
        size = jnp.maximum(lens[0, s], 1).astype(f32)
        denom = denom + jnp.where(slot_col == s, size, 0.0)
    pooled = pooled / denom
    pooled_grad[...] = jnp.zeros((SENTS, width), f32)
    offset = 0
    for m in truncations(width):
        leading = pooled[:, :m]
        factor = lax.rsqrt(jnp.mean(leading * leading, axis=1, keepdims=True) + pool_eps)
        third, lane = offset // width, offset % width
        pools[third * SENTS : (third + 1) * SENTS, lane : lane + m] = leading * factor
        upstream = pool_grad[:, offset : offset + m]
        inner = jnp.mean(upstream * leading, axis=1, keepdims=True)
        pooled_grad[:, :m] += factor * upstream - leading * (factor * factor * factor * inner)
        offset += m
    rest = offset % width
    pools[2 * SENTS :, rest:] = jnp.zeros((SENTS, width - rest), f32)
    spread = pooled_grad[...] / denom
    spread_out[...] = spread
    part[...], _, sums = finish_chunk(
        seg_col[3 * rows :],
        normal_ref[...],
        inverse_ref[:, :1],
        gain,
        spread,
        out_grad[chunk(me, 3, rows), :],
        grad_of[3 * rows :, :],
        w_down,
        w_up,
        low,
        up,
    )
    for n in range(4):
        side[n : n + 1, :] = sums[n]
    side[4:, :] = jnp.zeros((4, width), f32)


def finish_rest(ids, lens, g_ffn, out_grad, grad_of, w_down, w_up, *refs):
    ins, outs, (resid_low, upper_low, held) = refs[:8], refs[8:-3], refs[-3:]
    normal_ref, inverse_ref, spread, low3, up3, side3, normed_low, act = ins
    p0, p1, p2, d_own, side, even, odd = outs
    me = ids[0]
    rows, width = p0.shape
    seg_col = segment_of(lens, row_places(me, (4 * rows, 1), 0, rows))
    resid_low[3 * rows :, :] = low3[...]
    upper_low[3 * rows :, :] = up3[...]
    at = slice(0, 3 * rows)
    part, d_resid, sums = finish_chunk(
        seg_col[at],
        normal_ref[...],
        inverse_ref[:, :1],
        g_ffn[...],
        spread[...],
        jnp.concatenate([out_grad[chunk(me, j, rows), :] for j in range(3)]),
        grad_of[at, :],
        w_down,
        w_up,
        resid_low.at[at, :],
        upper_low.at[at, :],
    )
    for j, out in enumerate((p0, p1, p2)):
        out[...] = part[j * rows : (j + 1) * rows, :]
    d_own[...] = d_resid[:rows, :]
    for n in range(4):
        side[n : n + 1, :] = side3[n : n + 1, :] + sums[n]
    side[4:, :] = jnp.zeros((4, width), f32)
    held[:width, :] = tn(normed_low[...], upper_low[...])
    held[width:, :] = tn(act[...], resid_low[...])
    step = even.shape[1]
    for d in range(8):
        at = pl.ds(pl.multiple_of((ids[1] ^ d) * step, 8), step)
        (odd if d & 1 else even)[d // 2] = held[at, :]


def back_hidden(own, near, across, d_resid, normal, inverse, g_attn, w_all, *outs):
    e0, e1, e2, e3, d_hidden_out, low_out = outs
    d_normed = d_resid[...] + (own[...] + near[...] + across[...])
    rows, width = d_normed.shape
    cols = w_all.shape[1]
    side = [None, col_sum(d_normed * normal[...]), col_sum(d_normed)]
    d_hidden = norm_back(d_normed * g_attn[...], normal[...], inverse[:, :1])
    side[0] = col_sum(d_hidden)
    d_hidden_out[...] = d_hidden
    low_out[...] = d_hidden.astype(bf16)
    base = packed_rows(rows, cols)
    for k, out in enumerate((e0, e1, e2, e3)):
        pack_into(out, nt(low_out[...], w_all[k]).astype(bf16).astype(f32))
        out[base:, :] = jnp.zeros((out.shape[0] - base, 128), f32)
        for v in range(3):
            for s in range(width // cols):
                for n in range(0, cols, 128):
                    r = base + (n // 128) * 16 + 4 * v + s
                    m = min(128, cols - n)
                    out[r : r + 1, :m] = side[v][:, s * cols + n : s * cols + n + m]


def out_grads(ids, m0, m1, m2, m3, hidden_low, even, odd, held):
    rows = hidden_low.shape[0]
    for k, block in enumerate((m0, m1, m2, m3)):
        for col, part in packed_parts(block, held.shape[1], 4 * rows, k * rows, rows):
            held[k, col : col + part.shape[1], :] = tn(part.astype(bf16), hidden_low[...])
    step = even.shape[2]
    for d in range(8):
        at = pl.ds(pl.multiple_of((ids[1] ^ d) * step, 8), step)
        for k in range(4):
            (odd if d & 1 else even)[d // 2, k] = held[k, at, :]


def attend_back(e0, e1, e2, e3, probs, q, k, v, wq, wk, wv, *refs):
    outs, (d_mixed, turned, d_scores) = refs[:-3], refs[-3:]
    p0, p1, p2, p3, grads, bias, shared = outs
    slots, cols = q.shape
    rows = slots // 4
    scale = HDIM**-0.5
    half = rows // 2
    for j, block in enumerate((e0, e1, e2, e3)):
        for r in (0, half):
            for col, part in packed_parts(block, cols, rows, r, half):
                at = slice(j * rows + r, j * rows + r + half)
                d_mixed[at, col : col + part.shape[1]] = part.astype(bf16)
    base = packed_rows(rows, cols)
    side = (e0[base:, :] + e1[base:, :]) + (e2[base:, :] + e3[base:, :])
    for n in range(0, cols, 128):
        m = min(128, cols - n)
        shared[:, n : n + m] = side[(n // 128) * 16 : (n // 128) * 16 + 16, :m]
    for h in range(cols // HDIM):
        lane = slice(h * HDIM, (h + 1) * HDIM)
        for j in range(4):
            at = slice(j * rows, (j + 1) * rows)
            p = probs[h, at, :].astype(f32)
            dp = nt(d_mixed[at, lane], v[:, lane])
            t = p * dp
            ds = (t - p * jnp.sum(t, axis=-1, keepdims=True)) * scale
            d_scores[at, :] = ds.astype(bf16)
        d_query = nn(d_scores[...], k[:, lane])
        bias[0:1, lane] = col_sum(d_query)
        grads[:, lane] = d_query.astype(bf16)
        d_key = tn(q[:, lane], d_scores[...]).T
        grads[:, cols + h * HDIM : cols + (h + 1) * HDIM] = d_key.astype(bf16)
        d_value = tn(d_mixed[:, lane], probs[h]).T
        bias[1:2, lane] = col_sum(d_value)
        grads[:, 2 * cols + h * HDIM : 2 * cols + (h + 1) * HDIM] = d_value.astype(bf16)
    bias[2:, :] = jnp.zeros((6, cols), f32)
    turned[:cols, :] = wq[...]
    turned[cols : 2 * cols, :] = wk[...]
    turned[2 * cols :, :] = wv[...]
    for j, out in ((3, p3), (2, p2), (1, p1), (0, p0)):
        out[...] = nn(grads[j * rows : (j + 1) * rows, :], turned[...])


def qkv_grads(ids, grads, tok_x, side, shared, bias, even, odd, held):
    width = tok_x.shape[1]
    cols = bias.shape[1]
    part = width // cols
    total = grads.shape[1]
    step = total // 8
    held[:total, :] = tn(grads[...], tok_x[...])
    held[total:, :] = jnp.zeros((64, width), f32)
    held[total : total + 4, :] = side[:4, :]

    @pl.when(ids[0] >= 0)
    def _():
        for n in range(2):
            held[total + 4 : total + 5, n * cols : (n + 1) * cols] = bias[n : n + 1, :]
        for n in range(3):
            for s in range(part):
                row = shared[4 * n + s : 4 * n + s + 1, :]
                held[total + 8 + n : total + 9 + n, s * cols : (s + 1) * cols] = row

    for d in range(8):
        c = ids[1] ^ d
        out = odd if d & 1 else even
        out[d // 2, :step, :] = held[pl.ds(pl.multiple_of(c * step, 8), step), :]
        out[d // 2, step:, :] = held[pl.ds(pl.multiple_of(total + c * 8, 8), 8), :]


def fold(mine, theirs, *refs):
    extra, outs = refs[: len(refs) - 4], refs[len(refs) - 4 :]
    rows = mine.shape[1]
    for n, out in enumerate(outs):
        out[:rows, :] = mine[n] + theirs[n]
        if n and extra:
            out[rows:, :] = extra[0][...]


def fold_halves(mine, theirs, *refs):
    extra, (own, to_x, to_y, keep_y, keep_x) = refs[:-5], refs[-5:]
    half = mine.shape[1] // 2
    own[...] = mine[0] + theirs[0]
    for n, (out, at) in enumerate(((to_x, slice(0, half)), (to_y, slice(half, 2 * half)))):
        for m, block in enumerate((1 + n, 3)):
            out[m * half : (m + 1) * half, :] = mine[block, at, :] + theirs[block, at, :]
        if extra:
            more = extra[0].shape[0] // 2
            out[2 * half :, :] = extra[0][n * more : (n + 1) * more, :]
    keep_y[...] = mine[2, :half, :] + theirs[2, :half, :]
    keep_x[...] = mine[1, half:, :] + theirs[1, half:, :]


def add(a, b, out):
    out[...] = a[...] + b[...]


def join_terms(part1, part2, far, o0, o1, o2, o3, near_out, across_out):
    rows = part1.shape[0]
    piece = o3.shape[0]
    near_out[:rows, :] = part1[...]
    near_out[rows:, :] = (o0[3 * piece :, :] + o1[3 * piece :, :]) + (o2[3 * piece :, :] + o3[...])
    across_out[...] = part2[...] + far[...]


def join_own(own, near, across, d_hidden, o0, o1, o2, o3, near_out, across_out, term):
    rows = own.shape[0]
    piece = term.shape[0]
    total = own[...] + near[:rows, :] + across[...] + d_hidden[...]
    near_out[:rows, :] = total
    across_out[:rows, :] = total
    for n, out, at in ((0, term, 0), (1, near_out, rows), (2, across_out, rows)):
        rest = slice(n * piece, (n + 1) * piece)
        sums = (o0[rest, :] + o1[rest, :]) + (o2[rest, :] + o3[rest, :])
        if n == 2:
            sums = sums + near[rows:, :]
        out[at : at + piece, :] = sums


def join_far(across, near, term, out, out_own):
    rows = out.shape[0]
    out[...] = across[:rows, :]
    out_own[...] = term[...] + near[rows:, :] + across[rows:, :]


def collect(own, extra, from_x, from_y, last_y, last_x, out_own, sums, mine):
    half = own.shape[0] // 2
    sums[:half, :] = own[:half, :] + from_x[:half, :] + last_y[:half, :]
    sums[half : 2 * half, :] = own[half:, :] + from_y[:half, :] + last_x[:half, :]
    sums[2 * half :, :] = out_own[...]
    travel = extra.shape[0] // 2
    more = 3 * SENTS // 2
    part = travel - more
    for n, (block, at) in enumerate(
        (
            (extra, 0),
            (extra, travel),
            (from_x, 2 * half),
            (last_x, half),
            (last_y, half),
            (from_y, 2 * half),
            (last_y, half + travel),
            (last_x, half + travel),
        )
    ):
        mine[n * part : (n + 1) * part, :] = block[at : at + part, :]
        to = 8 * part + n * more
        mine[to : to + more, :] = block[at + part : at + travel, :]


def place(me, r0, r1, r2, r3, out):
    rows = out.shape[0] // 4
    for j, block in enumerate((r0, r1, r2, r3)):
        out[chunk(me[0], j, rows), :] = block[:rows, :]


def unpack_ffn(ids, mine, theirs, up_out, down_out, pools_out, held):
    half = up_out.shape[0]
    step = 2 * half // 8
    wide = pools_out.shape[0]
    width = up_out.shape[1]
    for d in range(8):
        block = theirs if d & 1 else mine
        start = (d // 2) * step
        c = ids[1] ^ d
        at = pl.ds(pl.multiple_of((c % 4) * step, 8), step)

        @pl.when(c < 4)
        def _(block=block, at=at, start=start):
            up_out[at, :] = block[start : start + step, :]

        @pl.when(c >= 4)
        def _(block=block, at=at, start=start):
            down_out[at, :] = block[start : start + step, :]

        to = pl.ds(pl.multiple_of(c * SENTS, 8), SENTS)
        start = 4 * step + (d // 2) * 3 * SENTS
        for n in range(3):
            held[n, to, :] = block[start + n * SENTS : start + (n + 1) * SENTS, :]
    for n in range(3):
        m = min(width, wide - n * width)
        pools_out[n * width : n * width + m, :] = held[n].T[:m, :]


def unpack_attn(ids, *refs):
    blocks, outs, (held, side) = refs[:8], refs[8:-2], refs[-2:]
    q_out, k_out, v_out, o_out, *vectors = outs
    cols = o_out.shape[0]
    step = 3 * cols // 8
    small = cols // 8
    for d, block in enumerate(blocks):
        c = ids[1] ^ d
        held[pl.ds(pl.multiple_of(c * step, 8), step), :] = block[:step, :]
        side[pl.ds(pl.multiple_of(c * 8, 8), 8), :] = block[step : step + 8, :]
        o_out[pl.ds(pl.multiple_of(c * small, 8), small), :] = block[step + 8 :, :]
    q_out[...] = held[:cols, :]
    k_out[...] = held[cols : 2 * cols, :]
    v_out[...] = held[2 * cols :, :]
    vectors[0][...] = side[4, :cols]
    vectors[1][...] = side[4, cols : 2 * cols]
    for n, r in enumerate((8, 9, 10, 3, 2, 1, 0)):
        vectors[2 + n][...] = side[r, :]


def swap(block, k):
    return lax.ppermute(block, "tensor", swaps[k])


def swap_dp(block, k, n_dp):
    return lax.ppermute(block, "dp", [(i, i ^ k) for i in range(n_dp)])


def together(*items):
    return lax.optimization_barrier(items)


def rest_of_dp(block, n_dp):
    if n_dp == 8:
        return block
    groups = [[i + 8 * j for j in range(n_dp // 8)] for i in range(8)]
    return lax.psum(block, "dp", axis_index_groups=groups)


def core_swap(even, odd, n_dp):
    other = swap_dp(odd, 1, n_dp)
    flat = even.shape[-2] if even.ndim == 3 else even.shape[1] * even.shape[2]
    return even.reshape(4, flat, even.shape[-1]), other.reshape(4, flat, even.shape[-1])


def halves_start(even, other, *extra):
    _, rows, width = even.shape
    half, more = rows // 2, sum(item.shape[0] // 2 for item in extra)
    return call(
        fold_halves,
        [shape(rows, width)] + [shape(rows + more, width)] * 2 + [shape(half, width)] * 2,
        [even, other, *extra],
        moved=3 * even.size * 4,
    )


def with_other_core(blocks, n_dp):
    others = [swap_dp(item, 1, n_dp) for item in blocks]
    return [item for pair in zip(blocks, others) for item in pair]


def make_shards(n_dp):
    def shards(
        tokens,
        lengths,
        w_query,
        w_key,
        w_value,
        b_query,
        b_value,
        w_out,
        b_out,
        g_attn,
        b_attn,
        w_up,
        b_up,
        w_down,
        b_down,
        g_ffn,
        b_ffn,
        out_grad,
        pool_grad,
    ):
        me = lax.axis_index("tensor").astype(jnp.int32)
        group = (lax.axis_index("dp") % 8).astype(jnp.int32)
        ids = jnp.stack([me, group])
        slots, width = tokens.shape
        cols = w_query.shape[1]
        units = w_up.shape[1]
        heads = cols // HDIM
        rows = slots // 4
        row = lambda vector: vector.reshape(1, -1)
        wq, wk, wv = w_query.T, w_key.T, w_value.T

        piece = cols // 8
        slice_own = lax.dynamic_slice_in_dim(w_out, group * piece, piece, 0).astype(f32)
        slices = [slice_own] + [swap(slice_own, n) for n in (1, 2, 3)]

        tok_x, q, k, v, probs, mixed = call(
            attend,
            [
                shape(slots, width, kind=bf16),
                shape(slots, cols, kind=bf16),
                shape(slots, cols, kind=bf16),
                shape(slots, cols, kind=bf16),
                shape(heads, slots, slots, kind=bf16),
                shape(packed_rows(slots, cols), 128),
            ],
            [ids]
            + [
                pltpu.with_memory_space_constraint(item, pltpu.HBM)
                for item in (lengths, tokens, wq, wk, wv, row(b_query), row(b_value))
            ],
            flops=2 * slots * width * 3 * cols + 4 * slots * slots * cols,
            moved=slots * width * 4 + 3 * cols * width * 2 + heads * slots * slots * 2,
            scratch=[pltpu.VMEM((slots, cols), bf16)]
            + [pltpu.VMEM((cols, width), bf16)] * 3
            + [pltpu.VMEM((1, cols), f32)] * 2
            + [pltpu.SMEM((1, SENTS), jnp.int32), pltpu.SemaphoreType.DMA((10,))],
            raw=7,
        )
        mixed, *slices = together(mixed, *slices)
        slices = jnp.stack(slices)
        across, near = swap(mixed, 2), swap(mixed, 1)
        w_blocks = [swap_dp(slices, 2 * n, n_dp) for n in (1, 2, 3)]
        across, near, slices, *w_blocks = together(across, near, slices, *w_blocks)
        mixed_all = [mixed, near, across, swap(across, 1)]
        w_all = call(
            join_w_out,
            shape(4, cols, width, kind=bf16),
            [ids] + with_other_core([slices] + w_blocks, n_dp),
            moved=4 * cols * width * 6,
            scratch=[pltpu.VMEM((4, cols, width), f32)],
        )
        feed_ins = [tok_x, *mixed_all, w_all, row(b_out), row(g_attn), row(b_attn)]
        feed_ins += [w_up, row(b_up), w_down]
        part3, low3, upper3, act3 = call(
            feed_first,
            [
                shape(rows, width),
                shape(rows, width, kind=bf16),
                shape(rows, units),
                shape(rows, units, kind=bf16),
            ],
            feed_ins,
            flops=2 * rows * width * (width + 2 * units),
            moved=rows * width * 4 + 3 * width * units * 2,
        )
        far = swap(part3, 1)
        *parts, normed_low, upper, act, normal_own, inverse_own, resid_own = call(
            feed_rest,
            [shape(rows, width)] * 3
            + [
                shape(slots, width, kind=bf16),
                shape(slots, units),
                shape(slots, units, kind=bf16),
                shape(rows, width),
                shape(rows, 128),
                shape(rows, width),
            ],
            feed_ins + [row(b_down), low3, upper3, act3],
            flops=6 * rows * width * (width + 2 * units),
            moved=3 * slots * width * 4 + 3 * width * units * 2,
        )
        slope = call(
            gelu_grad, shape(slots, units), [upper], moved=8 * slots * units, flops=slots * units
        )
        far, slope, part2, part1 = together(far, slope, parts[2], parts[1])
        across, near = swap(part2 + far, 2), swap(part1, 1)
        own = resid_own + parts[0] + near + across
        across, near = swap(own, 2), swap(own, 1)
        across, near = together(across, near)
        resid = [own, near, across, swap(across, 1)]
        normal, inverse, early, pooled = call(
            finish_early,
            [shape(3 * rows, width), shape(3 * rows, 128)]
            + [shape(3 * rows, width, kind=bf16), shape(SENTS, width)],
            [ids, lengths, *resid[:3], row(g_ffn), row(b_ffn)],
            flops=slots * width * 100,
            moved=3 * slots * width * 4,
        )
        part3, layer_out, own_pools, spread, low3, up3, side3 = call(
            finish_first,
            [
                shape(rows, width),
                shape(slots, width, kind=bf16),
                shape(3 * SENTS, width),
                shape(SENTS, width),
                shape(rows, width, kind=bf16),
                shape(rows, units, kind=bf16),
                shape(8, width),
            ],
            [ids, lengths, resid[3], early, pooled, row(g_ffn), row(b_ffn), out_grad, pool_grad]
            + [slope, w_down, w_up],
            flops=4 * rows * width * units,
            moved=6 * slots * width * 4,
            scratch=[
                pltpu.VMEM((rows, width), f32),
                pltpu.VMEM((rows, 128), f32),
                pltpu.VMEM((rows, width), bf16),
                pltpu.VMEM((SENTS, width), f32),
            ],
        )
        far = swap(part3, 1)
        step = 2 * width // 8
        *parts, d_resid, side, even, odd = call(
            finish_rest,
            [shape(rows, width)] * 4 + [shape(8, width)] + [shape(4, step, width)] * 2,
            [ids, lengths, row(g_ffn), out_grad, slope, w_down, w_up]
            + [normal, inverse, spread, low3, up3, side3, normed_low, act],
            flops=8 * slots * width * units,
            moved=6 * slots * width * 4 + 8 * width * units,
            scratch=[
                pltpu.VMEM((slots, width), bf16),
                pltpu.VMEM((slots, units), bf16),
                pltpu.VMEM((2 * width, width), f32),
            ],
        )
        even, other = core_swap(even, odd, n_dp)
        part2 = call(add, shape(rows, width), [parts[2], far], flops=100 * order)
        part2, part1, even, other = together(part2, parts[1], even, other)
        across, near = swap(part2, 2), swap(part1, 1)
        ffn_own, to_x, to_y, keep_y, keep_x = halves_start(even, other)
        from_x, from_y = swap_dp(to_x, 2, n_dp), swap_dp(to_y, 4, n_dp)
        *sent, d_hidden, hidden_low = call(
            back_hidden,
            [shape(packed_rows(rows, cols) + 16 * -(-cols // 128), 128)] * 4
            + [shape(rows, width), shape(rows, width, kind=bf16)],
            [parts[0], near, across, d_resid, normal_own, inverse_own, row(g_attn), w_all],
            flops=30 * order,
            moved=6 * rows * width * 4,
        )
        *sent, d_hidden, hidden_low, from_x, from_y, keep_x, keep_y = together(
            *sent, d_hidden, hidden_low, from_x, from_y, keep_x, keep_y
        )
        d_mixed = [sent[0]] + [swap(sent[n], n) for n in (1, 2, 3)]
        half = step // 2
        to_y, to_x = keep_y + from_x[half:], keep_x + from_y[half:]
        last_y, last_x = swap_dp(to_y, 4, n_dp), swap_dp(to_x, 2, n_dp)
        even, odd = call(
            out_grads,
            [shape(4, 4, piece, width)] * 2,
            [ids, *mixed_all, hidden_low],
            flops=2 * rows * width * 4 * cols,
            moved=8 * 4 * cols * width,
            scratch=[pltpu.VMEM((4, cols, width), f32)],
        )
        even, other = core_swap(even, odd, n_dp)
        d_mixed = together(*d_mixed)
        *parts, grads, bias, shared = call(
            attend_back,
            [shape(rows, width)] * 4
            + [shape(slots, 3 * cols, kind=bf16), shape(8, cols), shape(16, cols)],
            [*d_mixed, probs, q, k, v, wq, wk, wv],
            flops=20 * order,
            moved=heads * slots * slots * 2 + 2 * slots * width * 4,
            scratch=[
                pltpu.VMEM((slots, cols), bf16),
                pltpu.VMEM((3 * cols, width), bf16),
                pltpu.VMEM((slots, slots), bf16),
            ],
        )
        part3, out_even, out_other, last_x, last_y = together(parts[3], even, other, last_x, last_y)
        far = swap(part3, 1)
        ffn_sum = [ffn_own[:half] + from_x[:half] + last_y, ffn_own[half:] + from_y[:half] + last_x]
        if n_dp > 8:
            ffn_sum = [rest_of_dp(item, n_dp) for item in ffn_sum]
        more = 3 * SENTS // 2
        extra = [ffn_sum[0], own_pools[:more], ffn_sum[1], own_pools[more:]]
        extra = jnp.concatenate(extra)
        out = call(
            fold,
            [shape(4 * piece, width)] * 4,
            [out_even, out_other],
            moved=3 * out_even.size * 4,
        )
        out_x, out_y = swap_dp(out[1], 2, n_dp), swap_dp(out[2], 4, n_dp)
        even, odd = call(
            qkv_grads,
            [shape(4, 3 * piece + 8, width)] * 2,
            [ids, grads, tok_x, side, shared, bias],
            flops=6 * slots * width * cols,
            moved=8 * 3 * cols * width,
            scratch=[pltpu.VMEM((3 * cols + 64, width), f32)],
        )
        even, other = core_swap(even, odd, n_dp)
        out_d = swap_dp(out[3][3 * piece :], 6, n_dp)
        pieces = [out[0], out_x, out_y, out_d]
        if n_dp > 8:
            pieces[3] = rest_of_dp(sum(item[-piece:] for item in pieces), n_dp)
            pieces[:3] = [jnp.zeros_like(item) for item in pieces[:3]]
        part1, part2 = call(
            join_terms,
            [shape(rows + piece, width), shape(rows, width)],
            [parts[1], parts[2], far, *pieces],
            flops=20 * order,
        )
        part2, part1, even, other, out_x, out_y, out_d = together(
            part2, part1, even, other, out_x, out_y, out[3][: 3 * piece]
        )
        across, near = swap(part2, 2), swap(part1, 1)
        out_d = swap_dp(out_d, 6, n_dp)
        qkv_own, to_x, to_y, keep_y, keep_x = halves_start(even, other, extra)
        from_x, from_y = swap_dp(to_x, 2, n_dp), swap_dp(to_y, 4, n_dp)
        pieces = [out[0], out_x, out_y, out_d]
        if n_dp > 8:
            pieces[0] = rest_of_dp(sum(item[: 3 * piece] for item in pieces), n_dp)
            pieces[1:] = [jnp.zeros_like(pieces[0])] * 3
        own_near, own_across, term = call(
            join_own,
            [shape(rows + piece, width)] * 2 + [shape(piece, width)],
            [parts[0], near, across, d_hidden, *pieces],
            flops=30 * order,
            moved=7 * rows * width * 4,
        )
        own_near, own_across, from_x, from_y, keep_x, keep_y = together(
            own_near, own_across, from_x, from_y, keep_x, keep_y
        )
        across, near = swap(own_across, 2), swap(own_near, 1)
        low, travel = keep_y.shape[0], half + more
        to_y = [keep_y + from_x[low : 2 * low], extra[:travel], from_x[2 * low :]]
        to_x = [keep_x + from_y[low : 2 * low], extra[travel:], from_y[2 * low :]]
        to_y, to_x = jnp.concatenate(to_y), jnp.concatenate(to_x)
        last_y, last_x = swap_dp(to_y, 4, n_dp), swap_dp(to_x, 2, n_dp)
        far, out_own = call(
            join_far,
            [shape(rows, width), shape(piece, width)],
            [across, near, term],
            flops=30 * order,
        )
        far, near, across, out_own, last_y, last_x = together(
            far, near, across, out_own, last_y, last_x
        )
        far = swap(far, 1)
        attn_own, mine = call(
            collect,
            [shape(4 * piece + 8, width), shape(4 * (step + 3 * SENTS), width)],
            [qkv_own, extra, from_x, from_y, last_y, last_x, out_own],
            flops=1 * order,
            moved=8 * 4 * step * width,
        )
        if n_dp > 8:
            low = 3 * piece + 8
            attn_own = jnp.concatenate([rest_of_dp(attn_own[:low], n_dp), attn_own[low:]])
        attn_blocks = [attn_own] + [swap_dp(attn_own, 2 * n, n_dp) for n in (1, 2, 3)]
        wide = pool_grad.shape[1]
        d_w_up, d_w_down, pools = call(
            unpack_ffn,
            [shape(width, units), shape(units, width), shape(wide, 8 * SENTS)],
            [ids, mine, swap_dp(mine, 1, n_dp)],
            moved=16 * width * units,
            scratch=[pltpu.VMEM((3, 8 * SENTS, width), f32)],
        )
        d_tokens = call(
            place, shape(slots, width), [ids, own_near, near, across, far], flops=30 * order
        )
        d_w_up, d_w_down, pools, d_tokens, *attn_blocks = together(
            d_w_up, d_w_down, pools, d_tokens, *attn_blocks
        )
        d_w_query, d_w_key, d_w_value, d_w_out, *vectors = call(
            unpack_attn,
            [shape(cols, width)] * 4 + [shape(cols)] * 2 + [shape(width)] * 7,
            [ids, *with_other_core(attn_blocks, n_dp)],
            moved=8 * 4 * cols * width,
            scratch=[pltpu.VMEM((3 * cols, width), f32), pltpu.VMEM((64, width), f32)],
        )
        b_q, b_v, d_b_out, d_g_attn, d_b_attn, d_b_up, d_b_down, d_g_ffn, d_b_ffn = vectors
        pools = pools.T
        if n_dp > 8:
            third = [own_pools[n * SENTS : (n + 1) * SENTS] for n in range(3)]
            third = jnp.concatenate(third, axis=1)[:, :wide]
            pools = lax.all_gather(third, "dp", axis=0, tiled=True)
        return (
            layer_out,
            pools,
            d_tokens,
            d_w_query.T,
            d_w_key.T,
            d_w_value.T,
            b_q,
            b_v,
            d_w_out,
            d_b_out,
            d_g_attn,
            d_b_attn,
            d_w_up,
            d_b_up,
            d_w_down,
            d_b_down,
            d_g_ffn,
            d_b_ffn,
        )

    return shards


def solution(mesh):
    return jax.shard_map(
        make_shards(mesh.shape["dp"]),
        mesh=mesh,
        in_specs=(
            P("dp", None),
            P("dp", None),
            P(None, "tensor"),
            P(None, "tensor"),
            P(None, "tensor"),
            P("tensor"),
            P("tensor"),
            P("tensor", None),
            P(),
            P(),
            P(),
            P(None, "tensor"),
            P("tensor"),
            P("tensor", None),
            P(),
            P(),
            P(),
            P("dp", None),
            P("dp", None),
        ),
        out_specs=(
            P("dp", None),
            P(),
            P("dp", None),
            P(None, "tensor"),
            P(None, "tensor"),
            P(None, "tensor"),
            P("tensor"),
            P("tensor"),
            P("tensor", None),
            P(),
            P(),
            P(),
            P(None, "tensor"),
            P("tensor"),
            P("tensor", None),
            P(),
            P(),
            P(),
        ),
        check_vma=False,
    )
```
